512 devices in a mesh: seq: 64 (over y, x, core), head: 8 (over z).
Axes of the slice: x: 4, y: 8, z: 8, core: 2. Of those that a mesh axis runs over, the one named last changes fastest.
Arguments:
- token_values: bfloat16 [24576, 4096], P('seq', 'head'), may hold values from -6 to 6
- b_inputs: bfloat16 [24576, 128], P('seq'), may hold values from -6 to 6
- c_inputs: bfloat16 [24576, 128], P('seq'), may hold values from -6 to 6
- log_decay: float32 [64, 24576], P('head', 'seq'), may hold values from -1 to 0
- grad_out: bfloat16 [24576, 4096], P('seq', 'head'), may hold values from -0.005859375 to 0.005859375
Outputs:
- grad_values: bfloat16 [24576, 4096], P('seq', 'head')
- grad_b: bfloat16 [24576, 128], P('seq')
- grad_c: bfloat16 [24576, 128], P('seq')
The draws below stay inside these ranges and needn't reach their ends.
All inputs are finite; a program needn't handle non-finite values.
Results may differ from the reference program's by a relative error of at most 0.014.
Values may be sent and summed in bfloat16 or wider, within the bound.
A program may use at most 128 MiB of HBM per device.

```python
import math
import jax
import jax.numpy as jnp
from jax import lax

HEADS = 64
HEAD_DIM = 64
STATE = 128
TOK_DEV = 384
HEADS_DEV = 8
WIDTH = 4096
WIDTH_DEV = 512
STEP_TOTAL = 24576
N_HEAD = 8


def draw_log_decay(key, part):
    derived_prng_seeds = jax.random.split(key, 7)
    fast_share = 0.5
    halving = math.log(2.0)
    quick_heads = jax.random.uniform(derived_prng_seeds[0], (HEADS, 1)) < fast_share
    fast_rate = jnp.exp(jax.random.uniform(derived_prng_seeds[1], (HEADS, 1), minval=math.log(1.0 / 50.0), maxval=math.log(1.0 / 30.0)))
    slow_rate = jnp.exp(jax.random.uniform(derived_prng_seeds[2], (HEADS, 1), minval=math.log(0.02), maxval=math.log(0.17))) / STEP_TOTAL
    floor_intensity = jnp.where(quick_heads, fast_rate, slow_rate)
    jaggedness_level = jnp.exp(jax.random.uniform(derived_prng_seeds[3], (HEADS, STEP_TOTAL), minval=-halving, maxval=halving))
    number_within_segment = jnp.exp(jax.random.uniform(derived_prng_seeds[4], (HEADS, STEP_TOTAL // TOK_DEV), minval=-halving, maxval=halving))
    number_within_segment = jnp.repeat(number_within_segment, TOK_DEV, axis=1)
    spike_places = jax.random.randint(derived_prng_seeds[5], (3,), 0, STEP_TOTAL)
    kept_indicator = jax.random.uniform(derived_prng_seeds[6], (HEADS, 3), minval=0.6, maxval=0.8)
    entry_indices = jnp.arange(STEP_TOTAL, dtype=jnp.int32)
    hit_entries = entry_indices[:, None] == spike_places[None, :]
    spike_happenings = jnp.sum(jnp.where(hit_entries[None, :, :], jnp.log(kept_indicator)[:, None, :], 0.0), axis=2)
    return -(floor_intensity * jaggedness_level * number_within_segment) + spike_happenings


def block_scale(rng, extent, pieces, smallest, top_value):
    factor_of = 1.0
    for position, blocks in pieces:
        steps = jax.random.uniform(jax.random.fold_in(jax.random.fold_in(rng, 6), position), (blocks,), jnp.float32, smallest / len(pieces), top_value / len(pieces))
        factor_of = factor_of * jnp.repeat(jnp.exp(steps), extent[position] // blocks).reshape((-1,) + (1,) * (len(extent) - 1 - position))
    return factor_of


def centred(rng, shape, deviation, reach, cuts=(), kind=jnp.bfloat16):
    entries = jax.random.normal(rng, shape, jnp.float32) * deviation
    if len(cuts) > 0:
        entries = block_scale(rng, shape, cuts, -0.22, 0.18) * entries
    return jnp.clip(entries, min=-reach, max=reach).astype(kind)


def setup_inputs(seed: int = 0) -> dict:
    arg_keys = jax.random.split(jax.random.key(seed), 6)
    return {
        "token_values": centred(arg_keys[0], (STEP_TOTAL, WIDTH), 1.0, 6.0, ((0, 64), (1, 8))),
        "b_inputs": centred(arg_keys[1], (STEP_TOTAL, STATE), 1.0, 6.0, ((0, 64),)),
        "c_inputs": centred(arg_keys[2], (STEP_TOTAL, STATE), 1.0, 6.0, ((0, 64),)),
        "log_decay": draw_log_decay(jax.random.fold_in(arg_keys[5], 71), 0),
        "grad_out": centred(arg_keys[4], (STEP_TOTAL, WIDTH), 0.001, 0.005859375, ((0, 64), (1, 8))),
    }


PRECISE = lax.Precision.HIGHEST


def rounded(value):
    return lax.optimization_barrier(value.astype(jnp.bfloat16)).astype(jnp.float32)


def block_decays(decay_block):
    cumulative = jnp.cumsum(decay_block, axis=1)
    block_log = cumulative[:, -1]
    into_end = jnp.exp(block_log[:, None] - cumulative)
    from_start = jnp.exp(cumulative)
    return cumulative, into_end, from_start, jnp.exp(block_log)


def block_states(block_data):
    x_block, b_block, c_block, decay_block, dy_block = block_data
    cumulative, into_end, from_start, block_decay = block_decays(decay_block)
    b_float = b_block.astype(jnp.float32)
    c_float = c_block.astype(jnp.float32)
    decayed_b = rounded(into_end[:, :, None] * b_float[None])
    decayed_c = rounded(from_start[:, :, None] * c_float[None])
    x_heads = x_block.astype(jnp.float32).reshape(TOK_DEV, HEADS, HEAD_DIM)
    dy_heads = dy_block.astype(jnp.float32).reshape(TOK_DEV, HEADS, HEAD_DIM)
    state_local = jnp.einsum("htn,thp->nhp", decayed_b, x_heads, precision=PRECISE).reshape(STATE, WIDTH)
    adjoint_local = jnp.einsum("hsn,shp->nhp", decayed_c, dy_heads, precision=PRECISE).reshape(STATE, WIDTH)
    return state_local, adjoint_local, block_decay


def block_grads(block_data):
    x_block, b_block, c_block, decay_block, dy_block, state_in, adjoint_out = block_data
    cumulative, into_end, from_start, block_decay = block_decays(decay_block)
    b_float = b_block.astype(jnp.float32)
    c_float = c_block.astype(jnp.float32)
    x_float = x_block.astype(jnp.float32)
    dy_float = dy_block.astype(jnp.float32)
    scores = jnp.dot(c_float, b_float.T, precision=PRECISE)
    entry_indices = jnp.arange(TOK_DEV, dtype=jnp.int32)
    causal = entry_indices[:, None] >= entry_indices[None, :]
    to_end_cols = jnp.repeat(into_end.T, HEAD_DIM, axis=1)
    from_start_cols = jnp.repeat(from_start.T, HEAD_DIM, axis=1)
    x_scaled = x_float * to_end_cols
    dy_scaled = dy_float * from_start_cols

    def group_terms(group_idx):
        def head_step(running, offset):
            head_idx = group_idx * HEADS_DEV + offset
            cum_head = lax.dynamic_index_in_dim(cumulative, head_idx, 0, keepdims=False)
            log_gaps = cum_head[:, None] - cum_head[None, :]
            decays = jnp.where(causal, jnp.exp(jnp.where(causal, log_gaps, 0.0)), 0.0)
            mixing = rounded(scores * decays)
            x_head = lax.dynamic_slice_in_dim(x_float, head_idx * HEAD_DIM, HEAD_DIM, 1)
            dy_head = lax.dynamic_slice_in_dim(dy_float, head_idx * HEAD_DIM, HEAD_DIM, 1)
            dx_head = jnp.dot(mixing.T, dy_head, precision=PRECISE)
            dot_pairs = jnp.dot(dy_head, x_head.T, precision=PRECISE)
            return running + decays * dot_pairs, dx_head

        running, dx_heads = lax.scan(head_step, jnp.zeros((TOK_DEV, TOK_DEV), jnp.float32), jnp.arange(HEADS_DEV, dtype=jnp.int32))
        weighted = rounded(running)
        first_col = group_idx * WIDTH_DEV
        x_group = lax.dynamic_slice_in_dim(x_scaled, first_col, WIDTH_DEV, 1)
        dy_group = lax.dynamic_slice_in_dim(dy_scaled, first_col, WIDTH_DEV, 1)
        adj_group = lax.dynamic_slice_in_dim(adjoint_out, first_col, WIDTH_DEV, 1)
        state_group = lax.dynamic_slice_in_dim(state_in, first_col, WIDTH_DEV, 1)
        part_b = jnp.dot(weighted.T, c_float, precision=PRECISE) + jnp.dot(x_group, adj_group.T, precision=PRECISE)
        part_c = jnp.dot(weighted, b_float, precision=PRECISE) + jnp.dot(dy_group, state_group.T, precision=PRECISE)
        return dx_heads, rounded(part_b), rounded(part_c)

    dx_heads, db_groups, dc_groups = lax.map(group_terms, jnp.arange(N_HEAD, dtype=jnp.int32))
    dx_local = jnp.transpose(dx_heads.reshape(HEADS, TOK_DEV, HEAD_DIM), (1, 0, 2)).reshape(TOK_DEV, WIDTH)
    grad_values = dx_local + to_end_cols * jnp.dot(b_float, adjoint_out, precision=PRECISE)
    grad_b = jnp.sum(db_groups, axis=0)
    grad_c = jnp.sum(dc_groups, axis=0)
    return grad_values.astype(jnp.bfloat16), grad_b.astype(jnp.bfloat16), grad_c.astype(jnp.bfloat16)


def reference(token_values, b_inputs, c_inputs, log_decay, grad_out):
    blocks = STEP_TOTAL // TOK_DEV
    x_blocks = token_values.reshape(blocks, TOK_DEV, WIDTH)
    b_blocks = b_inputs.reshape(blocks, TOK_DEV, STATE)
    c_blocks = c_inputs.reshape(blocks, TOK_DEV, STATE)
    decay_blocks = jnp.transpose(log_decay.reshape(HEADS, blocks, TOK_DEV), (1, 0, 2))
    dy_blocks = grad_out.reshape(blocks, TOK_DEV, WIDTH)
    state_local, adjoint_local, block_decay = lax.map(block_states, (x_blocks, b_blocks, c_blocks, decay_blocks, dy_blocks))
    spread = jnp.repeat(block_decay, HEAD_DIM, axis=1)[:, None, :]

    def forward(carried, inputs):
        local_part, factor = inputs
        return factor * carried + local_part, carried

    def backward(carried, inputs):
        local_part, factor = inputs
        return local_part + factor * carried, carried

    start = jnp.zeros((STATE, WIDTH), jnp.float32)
    final_state, state_in = lax.scan(forward, start, (state_local, spread))
    final_adjoint, adjoint_out = lax.scan(backward, start, (adjoint_local, spread), reverse=True)
    grad_values, grad_b, grad_c = lax.map(block_grads, (x_blocks, b_blocks, c_blocks, decay_blocks, dy_blocks, state_in, adjoint_out))
    return grad_values.reshape(STEP_TOTAL, WIDTH), grad_b.reshape(STEP_TOTAL, STATE), grad_c.reshape(STEP_TOTAL, STATE)
```

```python
import functools

import jax
import jax.numpy as jnp
from jax import lax
from jax.sharding import PartitionSpec as P

PRECISE = lax.Precision.HIGHEST


def shift(value, count, distance, reverse):
    if reverse:
        pairs = [(p, p - distance) for p in range(distance, count)]
    else:
        pairs = [(p, p + distance) for p in range(count - distance)]
    return lax.ppermute(value, "seq", pairs)


def exclusive_scans(count, decay_cols, parts):
    packed = [jnp.concatenate([decay_cols, s], axis=0) for s, _ in parts]
    windows = [shift(pk, count, 1, rev) for pk, (_, rev) in zip(packed, parts)]
    distance = 1
    while distance < count:
        received = [shift(w, count, distance, rev) for w, (_, rev) in zip(windows, parts)]
        windows = [
            jnp.concatenate([w[:1] * r[:1], w[1:] + w[:1] * r[1:]], axis=0)
            for w, r in zip(windows, received)
        ]
        distance *= 2
    return [w[1:] for w in windows]


def shards(count, token_values, b_inputs, c_inputs, log_decay, grad_out):
    length = token_values.shape[0]
    heads_here = log_decay.shape[0]
    head_dim = token_values.shape[1] // heads_here
    state_size = b_inputs.shape[1]
    cumulative = jnp.cumsum(log_decay, axis=1)
    block_log = cumulative[:, -1]
    into_end = jnp.exp(block_log[:, None] - cumulative)
    from_start = jnp.exp(cumulative)
    block_decay = jnp.exp(block_log)
    b_float = b_inputs.astype(jnp.float32)
    c_float = c_inputs.astype(jnp.float32)
    decayed_b = (into_end[:, :, None] * b_float[None]).astype(jnp.bfloat16)
    decayed_c = (from_start[:, :, None] * c_float[None]).astype(jnp.bfloat16)
    x_heads = token_values.reshape(length, heads_here, head_dim)
    dy_heads = grad_out.reshape(length, heads_here, head_dim)
    state_local = jnp.einsum(
        "htn,thp->nhp", decayed_b, x_heads, preferred_element_type=jnp.float32
    ).reshape(state_size, heads_here * head_dim)
    adjoint_local = jnp.einsum(
        "hsn,shp->nhp", decayed_c, dy_heads, preferred_element_type=jnp.float32
    ).reshape(state_size, heads_here * head_dim)
    decay_cols = jnp.repeat(block_decay, head_dim)[None, :]
    state_in, adjoint_out = exclusive_scans(
        count, decay_cols, [(state_local, False), (adjoint_local, True)]
    )
    scores = lax.dot_general(
        c_inputs, b_inputs, (((1,), (1,)), ((), ())), preferred_element_type=jnp.float32
    )
    entry_indices = lax.iota(jnp.int32, length)
    causal = entry_indices[:, None] >= entry_indices[None, :]

    def head_step(head_idx, carried):
        running, dx_local = carried
        cum_head = lax.dynamic_index_in_dim(cumulative, head_idx, 0, keepdims=False)
        log_gaps = cum_head[:, None] - cum_head[None, :]
        decays = jnp.where(causal, jnp.exp(jnp.where(causal, log_gaps, 0.0)), 0.0)
        mixing = (scores * decays).astype(jnp.bfloat16)
        x_head = lax.dynamic_slice_in_dim(token_values, head_idx * head_dim, head_dim, 1)
        dy_head = lax.dynamic_slice_in_dim(grad_out, head_idx * head_dim, head_dim, 1)
        dx_head = lax.dot_general(
            mixing, dy_head, (((0,), (0,)), ((), ())), preferred_element_type=jnp.float32
        )
        dot_pairs = lax.dot_general(
            dy_head, x_head, (((1,), (1,)), ((), ())), preferred_element_type=jnp.float32
        )
        dx_local = lax.dynamic_update_slice_in_dim(dx_local, dx_head, head_idx * head_dim, 1)
        return (running + decays * dot_pairs, dx_local)

    start_pair = (
        jnp.zeros((length, length), jnp.float32),
        jnp.zeros((length, heads_here * head_dim), jnp.float32),
    )
    running, dx_local = lax.fori_loop(0, heads_here, head_step, start_pair)
    weighted = running.astype(jnp.bfloat16)
    db_part = lax.dot_general(
        weighted, c_inputs, (((0,), (0,)), ((), ())), preferred_element_type=jnp.float32
    )
    dc_part = jnp.dot(weighted, b_inputs, preferred_element_type=jnp.float32)
    to_end_cols = jnp.repeat(into_end.T, head_dim, axis=1)
    from_start_cols = jnp.repeat(from_start.T, head_dim, axis=1)
    grad_values = dx_local + to_end_cols * jnp.dot(b_float, adjoint_out, precision=PRECISE)
    db_part = db_part + jnp.dot(
        token_values.astype(jnp.float32) * to_end_cols, adjoint_out.T, precision=PRECISE
    )
    dc_part = dc_part + jnp.dot(
        grad_out.astype(jnp.float32) * from_start_cols, state_in.T, precision=PRECISE
    )
    grad_b, grad_c = (
        lax.psum(db_part.astype(jnp.bfloat16), "head").astype(jnp.float32),
        lax.psum(dc_part.astype(jnp.bfloat16), "head").astype(jnp.float32),
    )
    return (
        grad_values.astype(jnp.bfloat16),
        grad_b.astype(jnp.bfloat16),
        grad_c.astype(jnp.bfloat16),
    )


def solution(mesh):
    in_specs = (
        P("seq", "head"),
        P("seq", None),
        P("seq", None),
        P("head", "seq"),
        P("seq", "head"),
    )
    out_specs = (P("seq", "head"), P("seq", None), P("seq", None))
    body = functools.partial(shards, mesh.shape["seq"])
    return jax.shard_map(body, mesh=mesh, in_specs=in_specs, out_specs=out_specs, check_vma=False)
```

```python
import functools

import jax
import jax.numpy as jnp
from jax import lax
from jax.experimental import pallas as pl
from jax.experimental.pallas import tpu as pltpu
from jax.sharding import PartitionSpec as P

PRECISE = lax.Precision.HIGHEST
MESH = pl.DeviceIdType.MESH


def head_sum_kernel(n, x_ref, o_ref, gather1, gather2, send1, recv1, send2, recv2):
    me = lax.axis_index("head")
    row = lax.axis_index("seq")
    rows = gather1.shape[1]
    barrier = pltpu.get_barrier_semaphore()
    for k in range(1, n):
        peer = lax.rem(me + k, n)
        pl.semaphore_signal(barrier, inc=1, device_id=(row, peer), device_id_type=MESH)
    pl.semaphore_wait(barrier, n - 1)

    def chunk(i):
        return x_ref.at[pl.ds(pl.multiple_of(i * rows, rows), rows)]

    sends = []
    for k in range(1, n):
        peer = lax.rem(me + k, n)
        c = pltpu.make_async_remote_copy(
            src_ref=chunk(peer), dst_ref=gather1.at[me], send_sem=send1.at[k],
            recv_sem=recv1.at[k], device_id=(row, peer), device_id_type=MESH)
        c.start()
        sends.append(c)
    total = x_ref[pl.ds(pl.multiple_of(me * rows, rows), rows), :].astype(jnp.float32)
    for k in range(1, n):
        source = lax.rem(me + n - k, n)
        pltpu.make_async_remote_copy(
            src_ref=chunk(source), dst_ref=gather1.at[source], send_sem=send1.at[k],
            recv_sem=recv1.at[k], device_id=(row, source), device_id_type=MESH).wait_recv()
        total = total + gather1[source].astype(jnp.float32)
    for c in sends:
        c.wait_send()
    gather2[me] = total.astype(gather2.dtype)
    sends = []
    for k in range(1, n):
        peer = lax.rem(me + k, n)
        c = pltpu.make_async_remote_copy(
            src_ref=gather2.at[me], dst_ref=gather2.at[me], send_sem=send2.at[k],
            recv_sem=recv2.at[k], device_id=(row, peer), device_id_type=MESH)
        c.start()
        sends.append(c)
    for k in range(1, n):
        source = lax.rem(me + n - k, n)
        pltpu.make_async_remote_copy(
            src_ref=gather2.at[source], dst_ref=gather2.at[source], send_sem=send2.at[k],
            recv_sem=recv2.at[k], device_id=(row, source), device_id_type=MESH).wait_recv()
    for c in sends:
        c.wait_send()
    o_ref[...] = gather2[...]


def head_sum(n, parts):
    rows = parts.shape[0] // n
    width = parts.shape[1]
    out = pl.pallas_call(
        functools.partial(head_sum_kernel, n),
        out_shape=jax.ShapeDtypeStruct((n, rows, width), parts.dtype),
        in_specs=[pl.BlockSpec(memory_space=pltpu.VMEM)],
        out_specs=pl.BlockSpec(memory_space=pltpu.VMEM),
        scratch_shapes=[
            pltpu.VMEM((n, rows, width), parts.dtype),
            pltpu.VMEM((n, rows, width), parts.dtype),
            pltpu.SemaphoreType.DMA((n,)),
            pltpu.SemaphoreType.DMA((n,)),
            pltpu.SemaphoreType.DMA((n,)),
            pltpu.SemaphoreType.DMA((n,)),
        ],
        compiler_params=pltpu.CompilerParams(collective_id=0, has_side_effects=True),
    )(parts)
    return out.reshape(n * rows, width)


def shift(value, count, distance, reverse):
    if reverse:
        pairs = [(p, p - distance) for p in range(distance, count)]
    else:
        pairs = [(p, p + distance) for p in range(count - distance)]
    return lax.ppermute(value, "seq", pairs)


def exclusive_scans(count, decay_cols, parts):
    packed = [jnp.concatenate([decay_cols, s], axis=0) for s, _ in parts]
    windows = [shift(pk, count, 1, rev) for pk, (_, rev) in zip(packed, parts)]
    distance = 1
    while distance < count:
        received = [shift(w, count, distance, rev) for w, (_, rev) in zip(windows, parts)]
        windows = [
            jnp.concatenate([w[:1] * r[:1], w[1:] + w[:1] * r[1:]], axis=0)
            for w, r in zip(windows, received)
        ]
        distance *= 2
    return [w[1:] for w in windows]


def shards(count, groups, token_values, b_inputs, c_inputs, log_decay, grad_out):
    length = token_values.shape[0]
    heads_here = log_decay.shape[0]
    head_dim = token_values.shape[1] // heads_here
    state_size = b_inputs.shape[1]
    cumulative = jnp.cumsum(log_decay, axis=1)
    block_log = cumulative[:, -1]
    into_end = jnp.exp(block_log[:, None] - cumulative)
    from_start = jnp.exp(cumulative)
    block_decay = jnp.exp(block_log)
    b_float = b_inputs.astype(jnp.float32)
    c_float = c_inputs.astype(jnp.float32)
    decayed_b = (into_end[:, :, None] * b_float[None]).astype(jnp.bfloat16)
    decayed_c = (from_start[:, :, None] * c_float[None]).astype(jnp.bfloat16)
    x_heads = token_values.reshape(length, heads_here, head_dim)
    dy_heads = grad_out.reshape(length, heads_here, head_dim)
    state_local = jnp.einsum(
        "htn,thp->nhp", decayed_b, x_heads, preferred_element_type=jnp.float32
    ).reshape(state_size, heads_here * head_dim)
    adjoint_local = jnp.einsum(
        "hsn,shp->nhp", decayed_c, dy_heads, preferred_element_type=jnp.float32
    ).reshape(state_size, heads_here * head_dim)
    decay_cols = jnp.repeat(block_decay, head_dim)[None, :]
    state_in, adjoint_out = exclusive_scans(
        count, decay_cols, [(state_local, False), (adjoint_local, True)]
    )
    scores = lax.dot_general(
        c_inputs, b_inputs, (((1,), (1,)), ((), ())), preferred_element_type=jnp.float32
    )
    entry_indices = lax.iota(jnp.int32, length)
    causal = entry_indices[:, None] >= entry_indices[None, :]

    def head_step(head_idx, carried):
        running, dx_local = carried
        cum_head = lax.dynamic_index_in_dim(cumulative, head_idx, 0, keepdims=False)
        log_gaps = cum_head[:, None] - cum_head[None, :]
        decays = jnp.where(causal, jnp.exp(jnp.where(causal, log_gaps, 0.0)), 0.0)
        mixing = (scores * decays).astype(jnp.bfloat16)
        x_head = lax.dynamic_slice_in_dim(token_values, head_idx * head_dim, head_dim, 1)
        dy_head = lax.dynamic_slice_in_dim(grad_out, head_idx * head_dim, head_dim, 1)
        dx_head = lax.dot_general(
            mixing, dy_head, (((0,), (0,)), ((), ())), preferred_element_type=jnp.float32
        )
        dot_pairs = lax.dot_general(
            dy_head, x_head, (((1,), (1,)), ((), ())), preferred_element_type=jnp.float32
        )
        dx_local = lax.dynamic_update_slice_in_dim(dx_local, dx_head, head_idx * head_dim, 1)
        return (running + decays * dot_pairs, dx_local)

    start_pair = (
        jnp.zeros((length, length), jnp.float32),
        jnp.zeros((length, heads_here * head_dim), jnp.float32),
    )
    running, dx_local = lax.fori_loop(0, heads_here, head_step, start_pair)
    weighted = running.astype(jnp.bfloat16)
    db_part = lax.dot_general(
        weighted, c_inputs, (((0,), (0,)), ((), ())), preferred_element_type=jnp.float32
    )
    dc_part = jnp.dot(weighted, b_inputs, preferred_element_type=jnp.float32)
    to_end_cols = jnp.repeat(into_end.T, head_dim, axis=1)
    from_start_cols = jnp.repeat(from_start.T, head_dim, axis=1)
    grad_values = dx_local + to_end_cols * jnp.dot(b_float, adjoint_out, precision=PRECISE)
    db_part = db_part + jnp.dot(
        token_values.astype(jnp.float32) * to_end_cols, adjoint_out.T, precision=PRECISE
    )
    dc_part = dc_part + jnp.dot(
        grad_out.astype(jnp.float32) * from_start_cols, state_in.T, precision=PRECISE
    )
    both = head_sum(
        groups, jnp.concatenate([db_part, dc_part], axis=0).astype(jnp.bfloat16)
    )
    return grad_values.astype(jnp.bfloat16), both[:length], both[length:]


def solution(mesh):
    in_specs = (
        P("seq", "head"),
        P("seq", None),
        P("seq", None),
        P("head", "seq"),
        P("seq", "head"),
    )
    out_specs = (P("seq", "head"), P("seq", None), P("seq", None))
    body = functools.partial(shards, mesh.shape["seq"], mesh.shape["head"])
    return jax.shard_map(body, mesh=mesh, in_specs=in_specs, out_specs=out_specs, check_vma=False)
```

```python
import functools

import jax
import jax.numpy as jnp
from jax import lax
from jax.experimental import pallas as pl
from jax.experimental.pallas import tpu as pltpu
from jax.sharding import PartitionSpec as P

PRECISE = lax.Precision.HIGHEST
MESH = pl.DeviceIdType.MESH


def head_sum_kernel(n, x_ref, o_ref, gather1, gather2, send1, recv1, send2, recv2):
    me = lax.axis_index("head")
    row = lax.axis_index("seq")
    rows = gather1.shape[1]
    barrier = pltpu.get_barrier_semaphore()
    for k in range(1, n):
        peer = lax.rem(me + k, n)
        pl.semaphore_signal(barrier, inc=1, device_id=(row, peer), device_id_type=MESH)
    pl.semaphore_wait(barrier, n - 1)

    def chunk(i):
        return x_ref.at[pl.ds(pl.multiple_of(i * rows, rows), rows)]

    sends = []
    for k in range(1, n):
        peer = lax.rem(me + k, n)
        c = pltpu.make_async_remote_copy(
            src_ref=chunk(peer), dst_ref=gather1.at[me], send_sem=send1.at[k],
            recv_sem=recv1.at[k], device_id=(row, peer), device_id_type=MESH)
        c.start()
        sends.append(c)
    total = x_ref[pl.ds(pl.multiple_of(me * rows, rows), rows), :].astype(jnp.float32)
    for k in range(1, n):
        source = lax.rem(me + n - k, n)
        pltpu.make_async_remote_copy(
            src_ref=chunk(source), dst_ref=gather1.at[source], send_sem=send1.at[k],
            recv_sem=recv1.at[k], device_id=(row, source), device_id_type=MESH).wait_recv()
        total = total + gather1[source].astype(jnp.float32)
    for c in sends:
        c.wait_send()
    gather2[me] = total.astype(gather2.dtype)
    sends = []
    for k in range(1, n):
        peer = lax.rem(me + k, n)
        c = pltpu.make_async_remote_copy(
            src_ref=gather2.at[me], dst_ref=gather2.at[me], send_sem=send2.at[k],
            recv_sem=recv2.at[k], device_id=(row, peer), device_id_type=MESH)
        c.start()
        sends.append(c)
    for k in range(1, n):
        source = lax.rem(me + n - k, n)
        pltpu.make_async_remote_copy(
            src_ref=gather2.at[source], dst_ref=gather2.at[source], send_sem=send2.at[k],
            recv_sem=recv2.at[k], device_id=(row, source), device_id_type=MESH).wait_recv()
    for c in sends:
        c.wait_send()
    o_ref[...] = gather2[...]


def head_sum(n, parts):
    rows = parts.shape[0] // n
    width = parts.shape[1]
    out = pl.pallas_call(
        functools.partial(head_sum_kernel, n),
        out_shape=jax.ShapeDtypeStruct((n, rows, width), parts.dtype),
        in_specs=[pl.BlockSpec(memory_space=pltpu.VMEM)],
        out_specs=pl.BlockSpec(memory_space=pltpu.VMEM),
        scratch_shapes=[
            pltpu.VMEM((n, rows, width), parts.dtype),
            pltpu.VMEM((n, rows, width), parts.dtype),
            pltpu.SemaphoreType.DMA((n,)),
            pltpu.SemaphoreType.DMA((n,)),
            pltpu.SemaphoreType.DMA((n,)),
            pltpu.SemaphoreType.DMA((n,)),
        ],
        compiler_params=pltpu.CompilerParams(collective_id=0, has_side_effects=True),
    )(parts)
    return out.reshape(n * rows, width)


def scan_steps(n):
    steps, d = [1], 1
    while d < n:
        steps.append(d)
        d *= 2
    return steps


def scan_kernel(n, x_ref, y_ref, xo_ref, yo_ref, recv, win, send_sem, recv_sem):
    me = lax.axis_index("seq")
    col = lax.axis_index("head")
    s = xo_ref.shape[0]
    steps = scan_steps(n)
    spans = sorted(set(steps))
    barrier = pltpu.get_barrier_semaphore()
    for d in spans:
        @pl.when(me + d < n)
        def _():
            pl.semaphore_signal(barrier, inc=1, device_id=(me + d, col), device_id_type=MESH)

        @pl.when(me - d >= 0)
        def _():
            pl.semaphore_signal(barrier, inc=1, device_id=(me - d, col), device_id_type=MESH)
    peers = 0
    for d in spans:
        peers = peers + ((n - 1 - me) // d + n - 1) // n + (me // d + n - 1) // n
    pl.semaphore_wait(barrier, peers)

    def copy(way, r, src, target):
        return pltpu.make_async_remote_copy(
            src_ref=src, dst_ref=recv.at[way, r], send_sem=send_sem.at[way, r],
            recv_sem=recv_sem.at[way, r], device_id=(target, col), device_id_type=MESH)

    for r, d in enumerate(steps):
        for way, sign in ((0, 1), (1, -1)):
            src = (x_ref if way == 0 else y_ref) if r == 0 else win.at[way, r]
            target = me + sign * d

            @pl.when(jnp.logical_and(target >= 0, target < n))
            def _():
                copy(way, r, src, target).start()
        for way, sign in ((0, 1), (1, -1)):
            source = me - sign * d
            got = jnp.logical_and(source >= 0, source < n)

            @pl.when(got)
            def _():
                copy(way, r, win.at[way, r], source).wait_recv()
                if r == 0:
                    win[way, 1] = recv[way, 0]
                else:
                    a = win[way, r, s:, :]
                    win[way, r + 1, :s, :] = win[way, r, :s, :] + jnp.broadcast_to(
                        a[:1], (s, a.shape[1])) * recv[way, r, :s, :]
                    win[way, r + 1, s:, :] = a * recv[way, r, s:, :]

            @pl.when(jnp.logical_not(got))
            def _():
                if r == 0:
                    win[way, 1] = jnp.zeros(win.shape[2:], win.dtype)
                else:
                    win[way, r + 1] = win[way, r]
    for r, d in enumerate(steps):
        for way, sign in ((0, 1), (1, -1)):
            target = me + sign * d
            src = (x_ref if way == 0 else y_ref) if r == 0 else win.at[way, r]

            @pl.when(jnp.logical_and(target >= 0, target < n))
            def _():
                copy(way, r, src, target).wait_send()
    last = len(steps)
    xo_ref[...] = win[0, last, :s, :]
    yo_ref[...] = win[1, last, :s, :]


def exclusive_scans(count, decay_cols, forward, backward):
    s, w = forward.shape
    rounds = len(scan_steps(count))
    decay_rows = jnp.broadcast_to(decay_cols, (8, w))
    x = jnp.concatenate([forward, decay_rows], axis=0)
    y = jnp.concatenate([backward, decay_rows], axis=0)
    return pl.pallas_call(
        functools.partial(scan_kernel, count),
        out_shape=(jax.ShapeDtypeStruct((s, w), jnp.float32),) * 2,
        in_specs=[pl.BlockSpec(memory_space=pltpu.VMEM)] * 2,
        out_specs=(pl.BlockSpec(memory_space=pltpu.VMEM),) * 2,
        scratch_shapes=[
            pltpu.VMEM((2, rounds, s + 8, w), jnp.float32),
            pltpu.VMEM((2, rounds + 1, s + 8, w), jnp.float32),
            pltpu.SemaphoreType.DMA((2, rounds)),
            pltpu.SemaphoreType.DMA((2, rounds)),
        ],
        compiler_params=pltpu.CompilerParams(collective_id=1, has_side_effects=True),
    )(x, y)


def shards(count, groups, token_values, b_inputs, c_inputs, log_decay, grad_out):
    length = token_values.shape[0]
    heads_here = log_decay.shape[0]
    head_dim = token_values.shape[1] // heads_here
    state_size = b_inputs.shape[1]
    cumulative = jnp.cumsum(log_decay, axis=1)
    block_log = cumulative[:, -1]
    into_end = jnp.exp(block_log[:, None] - cumulative)
    from_start = jnp.exp(cumulative)
    block_decay = jnp.exp(block_log)
    b_float = b_inputs.astype(jnp.float32)
    c_float = c_inputs.astype(jnp.float32)
    decayed_b = (into_end[:, :, None] * b_float[None]).astype(jnp.bfloat16)
    decayed_c = (from_start[:, :, None] * c_float[None]).astype(jnp.bfloat16)
    x_heads = token_values.reshape(length, heads_here, head_dim)
    dy_heads = grad_out.reshape(length, heads_here, head_dim)
    state_local = jnp.einsum(
        "htn,thp->nhp", decayed_b, x_heads, preferred_element_type=jnp.float32
    ).reshape(state_size, heads_here * head_dim)
    adjoint_local = jnp.einsum(
        "hsn,shp->nhp", decayed_c, dy_heads, preferred_element_type=jnp.float32
    ).reshape(state_size, heads_here * head_dim)
    decay_cols = jnp.repeat(block_decay, head_dim)[None, :]
    state_in, adjoint_out = exclusive_scans(count, decay_cols, state_local, adjoint_local)
    scores = lax.dot_general(
        c_inputs, b_inputs, (((1,), (1,)), ((), ())), preferred_element_type=jnp.float32
    )
    entry_indices = lax.iota(jnp.int32, length)
    causal = entry_indices[:, None] >= entry_indices[None, :]

    def head_step(head_idx, carried):
        running, dx_local = carried
        cum_head = lax.dynamic_index_in_dim(cumulative, head_idx, 0, keepdims=False)
        log_gaps = cum_head[:, None] - cum_head[None, :]
        decays = jnp.where(causal, jnp.exp(jnp.where(causal, log_gaps, 0.0)), 0.0)
        mixing = (scores * decays).astype(jnp.bfloat16)
        x_head = lax.dynamic_slice_in_dim(token_values, head_idx * head_dim, head_dim, 1)
        dy_head = lax.dynamic_slice_in_dim(grad_out, head_idx * head_dim, head_dim, 1)
        dx_head = lax.dot_general(
            mixing, dy_head, (((0,), (0,)), ((), ())), preferred_element_type=jnp.float32
        )
        dot_pairs = lax.dot_general(
            dy_head, x_head, (((1,), (1,)), ((), ())), preferred_element_type=jnp.float32
        )
        dx_local = lax.dynamic_update_slice_in_dim(dx_local, dx_head, head_idx * head_dim, 1)
        return (running + decays * dot_pairs, dx_local)

    start_pair = (
        jnp.zeros((length, length), jnp.float32),
        jnp.zeros((length, heads_here * head_dim), jnp.float32),
    )
    running, dx_local = lax.fori_loop(0, heads_here, head_step, start_pair)
    weighted = running.astype(jnp.bfloat16)
    db_part = lax.dot_general(
        weighted, c_inputs, (((0,), (0,)), ((), ())), preferred_element_type=jnp.float32
    )
    dc_part = jnp.dot(weighted, b_inputs, preferred_element_type=jnp.float32)
    to_end_cols = jnp.repeat(into_end.T, head_dim, axis=1)
    from_start_cols = jnp.repeat(from_start.T, head_dim, axis=1)
    grad_values = dx_local + to_end_cols * jnp.dot(b_float, adjoint_out, precision=PRECISE)
    db_part = db_part + jnp.dot(
        token_values.astype(jnp.float32) * to_end_cols, adjoint_out.T, precision=PRECISE
    )
    dc_part = dc_part + jnp.dot(
        grad_out.astype(jnp.float32) * from_start_cols, state_in.T, precision=PRECISE
    )
    both = head_sum(
        groups, jnp.concatenate([db_part, dc_part], axis=0).astype(jnp.bfloat16)
    )
    return grad_values.astype(jnp.bfloat16), both[:length], both[length:]


def solution(mesh):
    in_specs = (
        P("seq", "head"),
        P("seq", None),
        P("seq", None),
        P("head", "seq"),
        P("seq", "head"),
    )
    out_specs = (P("seq", "head"), P("seq", None), P("seq", None))
    body = functools.partial(shards, mesh.shape["seq"], mesh.shape["head"])
    return jax.shard_map(body, mesh=mesh, in_specs=in_specs, out_specs=out_specs, check_vma=False)
```

```python
import functools

import jax
import jax.numpy as jnp
from jax import lax
from jax.experimental import pallas as pl
from jax.experimental.pallas import tpu as pltpu
from jax.sharding import PartitionSpec as P

PRECISE = lax.Precision.HIGHEST
MESH = pl.DeviceIdType.MESH


def head_sum_kernel(n, x_ref, o_ref, gather1, gather2, send1, recv1, send2, recv2):
    me = lax.axis_index("head")
    row = lax.axis_index("seq")
    rows = gather1.shape[1]
    barrier = pltpu.get_barrier_semaphore()
    for k in range(1, n):
        peer = lax.rem(me + k, n)
        pl.semaphore_signal(barrier, inc=1, device_id=(row, peer), device_id_type=MESH)
    pl.semaphore_wait(barrier, n - 1)

    def chunk(i):
        return x_ref.at[pl.ds(pl.multiple_of(i * rows, rows), rows)]

    sends = []
    for k in range(1, n):
        peer = lax.rem(me + k, n)
        c = pltpu.make_async_remote_copy(
            src_ref=chunk(peer), dst_ref=gather1.at[me], send_sem=send1.at[k],
            recv_sem=recv1.at[k], device_id=(row, peer), device_id_type=MESH)
        c.start()
        sends.append(c)
    total = x_ref[pl.ds(pl.multiple_of(me * rows, rows), rows), :].astype(jnp.float32)
    for k in range(1, n):
        source = lax.rem(me + n - k, n)
        pltpu.make_async_remote_copy(
            src_ref=chunk(source), dst_ref=gather1.at[source], send_sem=send1.at[k],
            recv_sem=recv1.at[k], device_id=(row, source), device_id_type=MESH).wait_recv()
        total = total + gather1[source].astype(jnp.float32)
    for c in sends:
        c.wait_send()
    gather2[me] = total.astype(gather2.dtype)
    sends = []
    for k in range(1, n):
        peer = lax.rem(me + k, n)
        c = pltpu.make_async_remote_copy(
            src_ref=gather2.at[me], dst_ref=gather2.at[me], send_sem=send2.at[k],
            recv_sem=recv2.at[k], device_id=(row, peer), device_id_type=MESH)
        c.start()
        sends.append(c)
    for k in range(1, n):
        source = lax.rem(me + n - k, n)
        pltpu.make_async_remote_copy(
            src_ref=gather2.at[source], dst_ref=gather2.at[source], send_sem=send2.at[k],
            recv_sem=recv2.at[k], device_id=(row, source), device_id_type=MESH).wait_recv()
    for c in sends:
        c.wait_send()
    o_ref[...] = gather2[...]


def head_sum(n, parts):
    rows = parts.shape[0] // n
    width = parts.shape[1]
    out = pl.pallas_call(
        functools.partial(head_sum_kernel, n),
        out_shape=jax.ShapeDtypeStruct((n, rows, width), parts.dtype),
        in_specs=[pl.BlockSpec(memory_space=pltpu.VMEM)],
        out_specs=pl.BlockSpec(memory_space=pltpu.VMEM),
        scratch_shapes=[
            pltpu.VMEM((n, rows, width), parts.dtype),
            pltpu.VMEM((n, rows, width), parts.dtype),
            pltpu.SemaphoreType.DMA((n,)),
            pltpu.SemaphoreType.DMA((n,)),
            pltpu.SemaphoreType.DMA((n,)),
            pltpu.SemaphoreType.DMA((n,)),
        ],
        compiler_params=pltpu.CompilerParams(collective_id=0, has_side_effects=True),
    )(parts)
    return out.reshape(n * rows, width)


def scan_steps(n):
    steps, d = [1], 1
    while d < n:
        steps.append(d)
        d *= 2
    return steps


def scan_kernel(rows_n, width, pack_ref, o_ref, recv1, win, out3, recv3, send1, rsem1,
                send2, rsem2, send3, rsem3, local):
    me = lax.axis_index("seq")
    col = lax.axis_index("head")
    c = me % width
    y = me // width
    piece = (recv1.shape[1] - 8) // 2
    steps = scan_steps(rows_n)
    spans = sorted(set(steps))

    barrier = pltpu.get_barrier_semaphore()
    for off in range(1, width):
        peer = y * width + (c + off) % width
        pl.semaphore_signal(barrier, inc=1, device_id=(peer, col), device_id_type=MESH)
    for d in spans:
        @pl.when(y + d < rows_n)
        def _():
            pl.semaphore_signal(barrier, inc=1, device_id=(me + d * width, col), device_id_type=MESH)

        @pl.when(y - d >= 0)
        def _():
            pl.semaphore_signal(barrier, inc=1, device_id=(me - d * width, col), device_id_type=MESH)
    peers = width - 1
    for d in spans:
        peers = peers + ((rows_n - 1 - y) // d + rows_n - 1) // rows_n + (y // d + rows_n - 1) // rows_n
    pl.semaphore_wait(barrier, peers)

    own = pltpu.make_async_copy(pack_ref.at[c], recv1.at[c], local.at[0])
    own.start()
    sends = []
    for off in range(1, width):
        k = (c + off) % width
        cp = pltpu.make_async_remote_copy(
            src_ref=pack_ref.at[k], dst_ref=recv1.at[c], send_sem=send1.at[off],
            recv_sem=rsem1.at[off], device_id=(y * width + k, col), device_id_type=MESH)
        cp.start()
        sends.append(cp)
    for off in range(1, width):
        k = (c + width - off) % width
        pltpu.make_async_remote_copy(
            src_ref=pack_ref.at[k], dst_ref=recv1.at[k], send_sem=send1.at[off],
            recv_sem=rsem1.at[off], device_id=(y * width + k, col), device_id_type=MESH).wait_recv()
    own.wait()
    for cp in sends:
        cp.wait_send()

    def decay(i):
        return recv1[i, 2 * piece:2 * piece + 1, :]

    fwd_e, fwd_g = [None] * width, [None] * width
    e = jnp.zeros((piece, recv1.shape[2]), jnp.float32)
    g = jnp.ones((1, recv1.shape[2]), jnp.float32)
    for i in range(width):
        fwd_e[i], fwd_g[i] = e, g
        a = decay(i)
        e = a * e + recv1[i, :piece, :]
        g = g * a
    bwd_e, bwd_g = [None] * width, [None] * width
    f = jnp.zeros((piece, recv1.shape[2]), jnp.float32)
    h = jnp.ones((1, recv1.shape[2]), jnp.float32)
    for i in reversed(range(width)):
        bwd_e[i], bwd_g[i] = f, h
        a = decay(i)
        f = a * f + recv1[i, piece:2 * piece, :]
        h = h * a
    win[0, 0, :piece, :] = e
    win[0, 0, piece:, :] = jnp.broadcast_to(g, (win.shape[2] - piece, g.shape[1]))
    win[1, 0, :piece, :] = f
    win[1, 0, piece:, :] = jnp.broadcast_to(h, (win.shape[2] - piece, h.shape[1]))

    def copy2(way, r, target):
        src = win.at[way, 0] if r == 0 else win.at[way, r]
        return pltpu.make_async_remote_copy(
            src_ref=src, dst_ref=win.at[way, len(steps) + 1 + r],
            send_sem=send2.at[way, r], recv_sem=rsem2.at[way, r],
            device_id=(target, col), device_id_type=MESH)

    base = len(steps) + 1
    for r, d in enumerate(steps):
        for way, sign in ((0, 1), (1, -1)):
            target_row = y + sign * d

            @pl.when(jnp.logical_and(target_row >= 0, target_row < rows_n))
            def _():
                copy2(way, r, me + sign * d * width).start()
        for way, sign in ((0, 1), (1, -1)):
            source_row = y - sign * d
            got = jnp.logical_and(source_row >= 0, source_row < rows_n)
            cur = 0 if r == 0 else r
            nxt = r + 1

            @pl.when(got)
            def _():
                copy2(way, r, me - sign * d * width).wait_recv()
                arrived = win[way, base + r]
                if r == 0:
                    win[way, nxt] = arrived
                else:
                    a = win[way, cur, piece:, :]
                    win[way, nxt, :piece, :] = win[way, cur, :piece, :] + jnp.broadcast_to(
                        a[:1], (piece, a.shape[1])) * arrived[:piece]
                    win[way, nxt, piece:, :] = a * arrived[piece:]

            @pl.when(jnp.logical_not(got))
            def _():
                if r == 0:
                    win[way, nxt] = jnp.zeros(win.shape[2:], win.dtype)
                else:
                    win[way, nxt] = win[way, cur]
    for r, d in enumerate(steps):
        for way, sign in ((0, 1), (1, -1)):
            target_row = y + sign * d

            @pl.when(jnp.logical_and(target_row >= 0, target_row < rows_n))
            def _():
                copy2(way, r, me + sign * d * width).wait_send()
    last = len(steps)
    entering = win[0, last, :piece, :]
    leaving = win[1, last, :piece, :]

    for i in range(width):
        out3[i, :piece, :] = fwd_e[i] + fwd_g[i] * entering
        out3[i, piece:, :] = bwd_e[i] + bwd_g[i] * leaving
    own = pltpu.make_async_copy(out3.at[c], recv3.at[c], local.at[1])
    own.start()
    sends = []
    for off in range(1, width):
        k = (c + off) % width
        cp = pltpu.make_async_remote_copy(
            src_ref=out3.at[k], dst_ref=recv3.at[c], send_sem=send3.at[off],
            recv_sem=rsem3.at[off], device_id=(y * width + k, col), device_id_type=MESH)
        cp.start()
        sends.append(cp)
    for off in range(1, width):
        k = (c + width - off) % width
        pltpu.make_async_remote_copy(
            src_ref=out3.at[k], dst_ref=recv3.at[k], send_sem=send3.at[off],
            recv_sem=rsem3.at[off], device_id=(y * width + k, col), device_id_type=MESH).wait_recv()
    own.wait()
    for cp in sends:
        cp.wait_send()
    o_ref[...] = recv3[...]


def exclusive_scans(count, decay_cols, forward, backward):
    s, w = forward.shape
    width = 8 if count % 8 == 0 else 1
    rows_n = count // width
    piece = s // width
    rounds = len(scan_steps(rows_n))
    pack = jnp.concatenate(
        [
            forward.reshape(width, piece, w),
            backward.reshape(width, piece, w),
            jnp.broadcast_to(decay_cols[None], (width, 8, w)),
        ],
        axis=1,
    )
    out = pl.pallas_call(
        functools.partial(scan_kernel, rows_n, width),
        out_shape=jax.ShapeDtypeStruct((width, 2 * piece, w), jnp.float32),
        in_specs=[pl.BlockSpec(memory_space=pltpu.VMEM)],
        out_specs=pl.BlockSpec(memory_space=pltpu.VMEM),
        scratch_shapes=[
            pltpu.VMEM((width, 2 * piece + 8, w), jnp.float32),
            pltpu.VMEM((2, 2 * rounds + 1, piece + 8, w), jnp.float32),
            pltpu.VMEM((width, 2 * piece, w), jnp.float32),
            pltpu.VMEM((width, 2 * piece, w), jnp.float32),
            pltpu.SemaphoreType.DMA((width,)),
            pltpu.SemaphoreType.DMA((width,)),
            pltpu.SemaphoreType.DMA((2, rounds)),
            pltpu.SemaphoreType.DMA((2, rounds)),
            pltpu.SemaphoreType.DMA((width,)),
            pltpu.SemaphoreType.DMA((width,)),
            pltpu.SemaphoreType.DMA((2,)),
        ],
        compiler_params=pltpu.CompilerParams(collective_id=1, has_side_effects=True),
    )(pack)
    return out[:, :piece].reshape(s, w), out[:, piece:].reshape(s, w)


def shards(count, groups, token_values, b_inputs, c_inputs, log_decay, grad_out):
    length = token_values.shape[0]
    heads_here = log_decay.shape[0]
    head_dim = token_values.shape[1] // heads_here
    state_size = b_inputs.shape[1]
    cumulative = jnp.cumsum(log_decay, axis=1)
    block_log = cumulative[:, -1]
    into_end = jnp.exp(block_log[:, None] - cumulative)
    from_start = jnp.exp(cumulative)
    block_decay = jnp.exp(block_log)
    b_float = b_inputs.astype(jnp.float32)
    c_float = c_inputs.astype(jnp.float32)
    decayed_b = (into_end[:, :, None] * b_float[None]).astype(jnp.bfloat16)
    decayed_c = (from_start[:, :, None] * c_float[None]).astype(jnp.bfloat16)
    x_heads = token_values.reshape(length, heads_here, head_dim)
    dy_heads = grad_out.reshape(length, heads_here, head_dim)
    state_local = jnp.einsum(
        "htn,thp->nhp", decayed_b, x_heads, preferred_element_type=jnp.float32
    ).reshape(state_size, heads_here * head_dim)
    adjoint_local = jnp.einsum(
        "hsn,shp->nhp", decayed_c, dy_heads, preferred_element_type=jnp.float32
    ).reshape(state_size, heads_here * head_dim)
    decay_cols = jnp.repeat(block_decay, head_dim)[None, :]
    state_in, adjoint_out = exclusive_scans(count, decay_cols, state_local, adjoint_local)
    scores = lax.dot_general(
        c_inputs, b_inputs, (((1,), (1,)), ((), ())), preferred_element_type=jnp.float32
    )
    entry_indices = lax.iota(jnp.int32, length)
    causal = entry_indices[:, None] >= entry_indices[None, :]

    def head_step(head_idx, carried):
        running, dx_local = carried
        cum_head = lax.dynamic_index_in_dim(cumulative, head_idx, 0, keepdims=False)
        log_gaps = cum_head[:, None] - cum_head[None, :]
        decays = jnp.where(causal, jnp.exp(jnp.where(causal, log_gaps, 0.0)), 0.0)
        mixing = (scores * decays).astype(jnp.bfloat16)
        x_head = lax.dynamic_slice_in_dim(token_values, head_idx * head_dim, head_dim, 1)
        dy_head = lax.dynamic_slice_in_dim(grad_out, head_idx * head_dim, head_dim, 1)
        dx_head = lax.dot_general(
            mixing, dy_head, (((0,), (0,)), ((), ())), preferred_element_type=jnp.float32
        )
        dot_pairs = lax.dot_general(
            dy_head, x_head, (((1,), (1,)), ((), ())), preferred_element_type=jnp.float32
        )
        dx_local = lax.dynamic_update_slice_in_dim(dx_local, dx_head, head_idx * head_dim, 1)
        return (running + decays * dot_pairs, dx_local)

    start_pair = (
        jnp.zeros((length, length), jnp.float32),
        jnp.zeros((length, heads_here * head_dim), jnp.float32),
    )
    running, dx_local = lax.fori_loop(0, heads_here, head_step, start_pair)
    weighted = running.astype(jnp.bfloat16)
    db_part = lax.dot_general(
        weighted, c_inputs, (((0,), (0,)), ((), ())), preferred_element_type=jnp.float32
    )
    dc_part = jnp.dot(weighted, b_inputs, preferred_element_type=jnp.float32)
    to_end_cols = jnp.repeat(into_end.T, head_dim, axis=1)
    from_start_cols = jnp.repeat(from_start.T, head_dim, axis=1)
    grad_values = dx_local + to_end_cols * jnp.dot(b_float, adjoint_out, precision=PRECISE)
    db_part = db_part + jnp.dot(
        token_values.astype(jnp.float32) * to_end_cols, adjoint_out.T, precision=PRECISE
    )
    dc_part = dc_part + jnp.dot(
        grad_out.astype(jnp.float32) * from_start_cols, state_in.T, precision=PRECISE
    )
    both = head_sum(
        groups, jnp.concatenate([db_part, dc_part], axis=0).astype(jnp.bfloat16)
    )
    return grad_values.astype(jnp.bfloat16), both[:length], both[length:]


def solution(mesh):
    in_specs = (
        P("seq", "head"),
        P("seq", None),
        P("seq", None),
        P("head", "seq"),
        P("seq", "head"),
    )
    out_specs = (P("seq", "head"), P("seq", None), P("seq", None))
    body = functools.partial(shards, mesh.shape["seq"], mesh.shape["head"])
    return jax.shard_map(body, mesh=mesh, in_specs=in_specs, out_specs=out_specs, check_vma=False)
```

```python
import functools

import jax
import jax.numpy as jnp
from jax import lax
from jax.experimental import pallas as pl
from jax.experimental.pallas import tpu as pltpu
from jax.sharding import PartitionSpec as P

PRECISE = lax.Precision.HIGHEST
MESH = pl.DeviceIdType.MESH


def head_sum_kernel(n, x_ref, o_ref, gather1, gather2, send1, recv1, send2, recv2):
    me = lax.axis_index("head")
    row = lax.axis_index("seq")
    rows = gather1.shape[1]
    barrier = pltpu.get_barrier_semaphore()
    for k in range(1, n):
        peer = lax.rem(me + k, n)
        pl.semaphore_signal(barrier, inc=1, device_id=(row, peer), device_id_type=MESH)
    pl.semaphore_wait(barrier, n - 1)

    def chunk(i):
        return x_ref.at[pl.ds(pl.multiple_of(i * rows, rows), rows)]

    sends = []
    for k in range(1, n):
        peer = lax.rem(me + k, n)
        c = pltpu.make_async_remote_copy(
            src_ref=chunk(peer), dst_ref=gather1.at[me], send_sem=send1.at[k],
            recv_sem=recv1.at[k], device_id=(row, peer), device_id_type=MESH)
        c.start()
        sends.append(c)
    total = x_ref[pl.ds(pl.multiple_of(me * rows, rows), rows), :].astype(jnp.float32)
    for k in range(1, n):
        source = lax.rem(me + n - k, n)
        pltpu.make_async_remote_copy(
            src_ref=chunk(source), dst_ref=gather1.at[source], send_sem=send1.at[k],
            recv_sem=recv1.at[k], device_id=(row, source), device_id_type=MESH).wait_recv()
        total = total + gather1[source].astype(jnp.float32)
    for c in sends:
        c.wait_send()
    gather2[me] = total.astype(gather2.dtype)
    sends = []
    for k in range(1, n):
        peer = lax.rem(me + k, n)
        c = pltpu.make_async_remote_copy(
            src_ref=gather2.at[me], dst_ref=gather2.at[me], send_sem=send2.at[k],
            recv_sem=recv2.at[k], device_id=(row, peer), device_id_type=MESH)
        c.start()
        sends.append(c)
    for k in range(1, n):
        source = lax.rem(me + n - k, n)
        pltpu.make_async_remote_copy(
            src_ref=gather2.at[source], dst_ref=gather2.at[source], send_sem=send2.at[k],
            recv_sem=recv2.at[k], device_id=(row, source), device_id_type=MESH).wait_recv()
    for c in sends:
        c.wait_send()
    o_ref[...] = gather2[...]


def head_sum(n, parts):
    if n == 1:
        return parts
    rows = parts.shape[0] // n
    width = parts.shape[1]
    out = pl.pallas_call(
        functools.partial(head_sum_kernel, n),
        out_shape=jax.ShapeDtypeStruct((n, rows, width), parts.dtype),
        in_specs=[pl.BlockSpec(memory_space=pltpu.VMEM)],
        out_specs=pl.BlockSpec(memory_space=pltpu.VMEM),
        scratch_shapes=[
            pltpu.VMEM((n, rows, width), parts.dtype),
            pltpu.VMEM((n, rows, width), parts.dtype),
            pltpu.SemaphoreType.DMA((n,)),
            pltpu.SemaphoreType.DMA((n,)),
            pltpu.SemaphoreType.DMA((n,)),
            pltpu.SemaphoreType.DMA((n,)),
        ],
        compiler_params=pltpu.CompilerParams(collective_id=0, has_side_effects=True),
    )(parts)
    return out.reshape(n * rows, width)


def scan_steps(n):
    steps, d = [1], 1
    while d < n:
        steps.append(d)
        d *= 2
    return steps


def scan_kernel(rows_n, width, pack_ref, x_ref, dy_ref, sc_ref, cr_ref, cc_ref, o_ref, dx_ref,
                run_ref, recv1, win, out3, recv3, send1, rsem1, send2, rsem2, send3, rsem3, local):
    me = lax.axis_index("seq")
    col = lax.axis_index("head")
    c = me % width
    y = me // width
    piece = (recv1.shape[1] - 8) // 2
    steps = scan_steps(rows_n)
    spans = sorted(set(steps))

    length = sc_ref.shape[0]
    later = lax.broadcasted_iota(jnp.int32, (length, length), 1) >= lax.broadcasted_iota(
        jnp.int32, (length, length), 0)
    run_ref[...] = jnp.zeros(run_ref.shape, run_ref.dtype)

    def head(h):
        gaps = cr_ref[h:h + 1, :] - cc_ref[:, h:h + 1]
        dec = jnp.where(later, jnp.exp(jnp.where(later, gaps, 0.0)), 0.0)
        mix = (sc_ref[...] * dec).astype(jnp.bfloat16)
        dx_ref[h] = jnp.dot(mix, dy_ref[h], preferred_element_type=jnp.float32)
        pairs = lax.dot_general(
            x_ref[h], dy_ref[h], (((1,), (1,)), ((), ())), preferred_element_type=jnp.float32)
        run_ref[...] += dec * pairs

    heads_left = list(range(x_ref.shape[0]))

    def heads(k):
        for _ in range(k):
            if heads_left:
                head(heads_left.pop(0))

    barrier = pltpu.get_barrier_semaphore()
    for off in range(1, width):
        peer = y * width + (c + off) % width
        pl.semaphore_signal(barrier, inc=1, device_id=(peer, col), device_id_type=MESH)
    for d in spans:
        @pl.when(y + d < rows_n)
        def _():
            pl.semaphore_signal(barrier, inc=1, device_id=(me + d * width, col), device_id_type=MESH)

        @pl.when(y - d >= 0)
        def _():
            pl.semaphore_signal(barrier, inc=1, device_id=(me - d * width, col), device_id_type=MESH)
    peers = width - 1
    for d in spans:
        peers = peers + ((rows_n - 1 - y) // d + rows_n - 1) // rows_n + (y // d + rows_n - 1) // rows_n
    heads(1)
    pl.semaphore_wait(barrier, peers)

    own = pltpu.make_async_copy(pack_ref.at[c], recv1.at[c], local.at[0])
    own.start()
    sends = []
    for off in range(1, width):
        k = (c + off) % width
        cp = pltpu.make_async_remote_copy(
            src_ref=pack_ref.at[k], dst_ref=recv1.at[c], send_sem=send1.at[off],
            recv_sem=rsem1.at[off], device_id=(y * width + k, col), device_id_type=MESH)
        cp.start()
        sends.append(cp)
    heads(3)
    for off in range(1, width):
        k = (c + width - off) % width
        pltpu.make_async_remote_copy(
            src_ref=pack_ref.at[k], dst_ref=recv1.at[k], send_sem=send1.at[off],
            recv_sem=rsem1.at[off], device_id=(y * width + k, col), device_id_type=MESH).wait_recv()
    own.wait()
    for cp in sends:
        cp.wait_send()

    def decay(i):
        return recv1[i, 2 * piece:2 * piece + 1, :]

    fwd_e, fwd_g = [None] * width, [None] * width
    e = jnp.zeros((piece, recv1.shape[2]), jnp.float32)
    g = jnp.ones((1, recv1.shape[2]), jnp.float32)
    for i in range(width):
        fwd_e[i], fwd_g[i] = e, g
        a = decay(i)
        e = a * e + recv1[i, :piece, :]
        g = g * a
    bwd_e, bwd_g = [None] * width, [None] * width
    f = jnp.zeros((piece, recv1.shape[2]), jnp.float32)
    h = jnp.ones((1, recv1.shape[2]), jnp.float32)
    for i in reversed(range(width)):
        bwd_e[i], bwd_g[i] = f, h
        a = decay(i)
        f = a * f + recv1[i, piece:2 * piece, :]
        h = h * a
    win[0, 0, :piece, :] = e
    win[0, 0, piece:, :] = jnp.broadcast_to(g, (win.shape[2] - piece, g.shape[1]))
    win[1, 0, :piece, :] = f
    win[1, 0, piece:, :] = jnp.broadcast_to(h, (win.shape[2] - piece, h.shape[1]))

    def copy2(way, r, target):
        src = win.at[way, 0] if r == 0 else win.at[way, r]
        return pltpu.make_async_remote_copy(
            src_ref=src, dst_ref=win.at[way, len(steps) + 1 + r],
            send_sem=send2.at[way, r], recv_sem=rsem2.at[way, r],
            device_id=(target, col), device_id_type=MESH)

    base = len(steps) + 1
    for r, d in enumerate(steps):
        for way, sign in ((0, 1), (1, -1)):
            target_row = y + sign * d

            @pl.when(jnp.logical_and(target_row >= 0, target_row < rows_n))
            def _():
                copy2(way, r, me + sign * d * width).start()
        heads(1 if r < len(steps) - 1 else len(heads_left))
        for way, sign in ((0, 1), (1, -1)):
            source_row = y - sign * d
            got = jnp.logical_and(source_row >= 0, source_row < rows_n)
            cur = 0 if r == 0 else r
            nxt = r + 1

            @pl.when(got)
            def _():
                copy2(way, r, me - sign * d * width).wait_recv()
                arrived = win[way, base + r]
                if r == 0:
                    win[way, nxt] = arrived
                else:
                    a = win[way, cur, piece:, :]
                    win[way, nxt, :piece, :] = win[way, cur, :piece, :] + jnp.broadcast_to(
                        a[:1], (piece, a.shape[1])) * arrived[:piece]
                    win[way, nxt, piece:, :] = a * arrived[piece:]

            @pl.when(jnp.logical_not(got))
            def _():
                if r == 0:
                    win[way, nxt] = jnp.zeros(win.shape[2:], win.dtype)
                else:
                    win[way, nxt] = win[way, cur]
    for r, d in enumerate(steps):
        for way, sign in ((0, 1), (1, -1)):
            target_row = y + sign * d

            @pl.when(jnp.logical_and(target_row >= 0, target_row < rows_n))
            def _():
                copy2(way, r, me + sign * d * width).wait_send()
    last = len(steps)
    entering = win[0, last, :piece, :]
    leaving = win[1, last, :piece, :]

    for i in range(width):
        out3[i, :piece, :] = fwd_e[i] + fwd_g[i] * entering
        out3[i, piece:, :] = bwd_e[i] + bwd_g[i] * leaving
    own = pltpu.make_async_copy(out3.at[c], recv3.at[c], local.at[1])
    own.start()
    sends = []
    for off in range(1, width):
        k = (c + off) % width
        cp = pltpu.make_async_remote_copy(
            src_ref=out3.at[k], dst_ref=recv3.at[c], send_sem=send3.at[off],
            recv_sem=rsem3.at[off], device_id=(y * width + k, col), device_id_type=MESH)
        cp.start()
        sends.append(cp)
    for off in range(1, width):
        k = (c + width - off) % width
        pltpu.make_async_remote_copy(
            src_ref=out3.at[k], dst_ref=recv3.at[k], send_sem=send3.at[off],
            recv_sem=rsem3.at[off], device_id=(y * width + k, col), device_id_type=MESH).wait_recv()
    own.wait()
    for cp in sends:
        cp.wait_send()
    o_ref[...] = recv3[...]


def exclusive_scans(count, decay_cols, forward, backward, x_heads, dy_heads, scores_t, cumulative):
    s, w = forward.shape
    width = 8 if count % 8 == 0 else 1
    rows_n = count // width
    piece = s // width
    rounds = len(scan_steps(rows_n))
    pack = jnp.concatenate(
        [
            forward.reshape(width, piece, w),
            backward.reshape(width, piece, w),
            jnp.broadcast_to(decay_cols[None], (width, 8, w)),
        ],
        axis=1,
    )
    length = scores_t.shape[0]
    out, dx, run = pl.pallas_call(
        functools.partial(scan_kernel, rows_n, width),
        out_shape=(
            jax.ShapeDtypeStruct((width, 2 * piece, w), jnp.float32),
            jax.ShapeDtypeStruct(x_heads.shape, jnp.float32),
            jax.ShapeDtypeStruct((length, length), jnp.float32),
        ),
        in_specs=[pl.BlockSpec(memory_space=pltpu.VMEM)] * 6,
        out_specs=(pl.BlockSpec(memory_space=pltpu.VMEM),) * 3,
        scratch_shapes=[
            pltpu.VMEM((width, 2 * piece + 8, w), jnp.float32),
            pltpu.VMEM((2, 2 * rounds + 1, piece + 8, w), jnp.float32),
            pltpu.VMEM((width, 2 * piece, w), jnp.float32),
            pltpu.VMEM((width, 2 * piece, w), jnp.float32),
            pltpu.SemaphoreType.DMA((width,)),
            pltpu.SemaphoreType.DMA((width,)),
            pltpu.SemaphoreType.DMA((2, rounds)),
            pltpu.SemaphoreType.DMA((2, rounds)),
            pltpu.SemaphoreType.DMA((width,)),
            pltpu.SemaphoreType.DMA((width,)),
            pltpu.SemaphoreType.DMA((2,)),
        ],
        compiler_params=pltpu.CompilerParams(collective_id=1, has_side_effects=True),
    )(pack, x_heads, dy_heads, scores_t, cumulative, cumulative.T)
    return out[:, :piece].reshape(s, w), out[:, piece:].reshape(s, w), dx, run


def shards(count, groups, token_values, b_inputs, c_inputs, log_decay, grad_out):
    length = token_values.shape[0]
    heads_here = log_decay.shape[0]
    head_dim = token_values.shape[1] // heads_here
    state_size = b_inputs.shape[1]
    cumulative = jnp.cumsum(log_decay, axis=1)
    block_log = cumulative[:, -1]
    into_end = jnp.exp(block_log[:, None] - cumulative)
    from_start = jnp.exp(cumulative)
    block_decay = jnp.exp(block_log)
    b_float = b_inputs.astype(jnp.float32)
    c_float = c_inputs.astype(jnp.float32)
    decayed_b = (into_end[:, :, None] * b_float[None]).astype(jnp.bfloat16)
    decayed_c = (from_start[:, :, None] * c_float[None]).astype(jnp.bfloat16)
    x_heads = token_values.reshape(length, heads_here, head_dim)
    dy_heads = grad_out.reshape(length, heads_here, head_dim)
    state_local = jnp.einsum(
        "htn,thp->nhp", decayed_b, x_heads, preferred_element_type=jnp.float32
    ).reshape(state_size, heads_here * head_dim)
    adjoint_local = jnp.einsum(
        "hsn,shp->nhp", decayed_c, dy_heads, preferred_element_type=jnp.float32
    ).reshape(state_size, heads_here * head_dim)
    decay_cols = jnp.repeat(block_decay, head_dim)[None, :]
    scores_t = lax.dot_general(
        b_inputs, c_inputs, (((1,), (1,)), ((), ())), preferred_element_type=jnp.float32
    )
    x_split = jnp.transpose(x_heads, (1, 0, 2))
    dy_split = jnp.transpose(dy_heads, (1, 0, 2))
    state_in, adjoint_out, dx_split, running_t = exclusive_scans(
        count, decay_cols, state_local, adjoint_local, x_split, dy_split, scores_t, cumulative
    )
    dx_local = jnp.transpose(dx_split, (1, 0, 2)).reshape(length, heads_here * head_dim)
    weighted_t = running_t.astype(jnp.bfloat16)
    db_part = jnp.dot(weighted_t, c_inputs, preferred_element_type=jnp.float32)
    dc_part = lax.dot_general(
        weighted_t, b_inputs, (((0,), (0,)), ((), ())), preferred_element_type=jnp.float32
    )
    to_end_cols = jnp.repeat(into_end.T, head_dim, axis=1)
    from_start_cols = jnp.repeat(from_start.T, head_dim, axis=1)
    grad_values = dx_local + to_end_cols * jnp.dot(b_float, adjoint_out, precision=PRECISE)
    db_part = db_part + jnp.dot(
        token_values.astype(jnp.float32) * to_end_cols, adjoint_out.T, precision=PRECISE
    )
    dc_part = dc_part + jnp.dot(
        grad_out.astype(jnp.float32) * from_start_cols, state_in.T, precision=PRECISE
    )
    both = head_sum(
        groups, jnp.concatenate([db_part, dc_part], axis=0).astype(jnp.bfloat16)
    )
    return grad_values.astype(jnp.bfloat16), both[:length], both[length:]


def solution(mesh):
    in_specs = (
        P("seq", "head"),
        P("seq", None),
        P("seq", None),
        P("head", "seq"),
        P("seq", "head"),
    )
    out_specs = (P("seq", "head"), P("seq", None), P("seq", None))
    body = functools.partial(shards, mesh.shape["seq"], mesh.shape["head"])
    return jax.shard_map(body, mesh=mesh, in_specs=in_specs, out_specs=out_specs, check_vma=False)
```

```python
import functools

import jax
import jax.numpy as jnp
from jax import lax
from jax.experimental import pallas as pl
from jax.experimental.pallas import tpu as pltpu
from jax.sharding import PartitionSpec as P

PRECISE = lax.Precision.HIGHEST
MESH = pl.DeviceIdType.MESH


def head_sum_kernel(n, x_ref, o_ref, gather1, gather2, send1, recv1, send2, recv2):
    me = lax.axis_index("head")
    row = lax.axis_index("seq")
    rows = gather1.shape[1]
    barrier = pltpu.get_barrier_semaphore()
    for k in range(1, n):
        peer = lax.rem(me + k, n)
        pl.semaphore_signal(barrier, inc=1, device_id=(row, peer), device_id_type=MESH)
    pl.semaphore_wait(barrier, n - 1)

    def chunk(i):
        return x_ref.at[pl.ds(pl.multiple_of(i * rows, rows), rows)]

    sends = []
    for k in range(1, n):
        peer = lax.rem(me + k, n)
        c = pltpu.make_async_remote_copy(
            src_ref=chunk(peer), dst_ref=gather1.at[me], send_sem=send1.at[k],
            recv_sem=recv1.at[k], device_id=(row, peer), device_id_type=MESH)
        c.start()
        sends.append(c)
    total = x_ref[pl.ds(pl.multiple_of(me * rows, rows), rows), :].astype(jnp.float32)
    for k in range(1, n):
        source = lax.rem(me + n - k, n)
        pltpu.make_async_remote_copy(
            src_ref=chunk(source), dst_ref=gather1.at[source], send_sem=send1.at[k],
            recv_sem=recv1.at[k], device_id=(row, source), device_id_type=MESH).wait_recv()
        total = total + gather1[source].astype(jnp.float32)
    for c in sends:
        c.wait_send()
    gather2[me] = total.astype(gather2.dtype)
    sends = []
    for k in range(1, n):
        peer = lax.rem(me + k, n)
        c = pltpu.make_async_remote_copy(
            src_ref=gather2.at[me], dst_ref=gather2.at[me], send_sem=send2.at[k],
            recv_sem=recv2.at[k], device_id=(row, peer), device_id_type=MESH)
        c.start()
        sends.append(c)
    for k in range(1, n):
        source = lax.rem(me + n - k, n)
        pltpu.make_async_remote_copy(
            src_ref=gather2.at[source], dst_ref=gather2.at[source], send_sem=send2.at[k],
            recv_sem=recv2.at[k], device_id=(row, source), device_id_type=MESH).wait_recv()
    for c in sends:
        c.wait_send()
    o_ref[...] = gather2[...]


def head_sum(n, parts):
    if n == 1:
        return parts
    rows = parts.shape[0] // n
    width = parts.shape[1]
    out = pl.pallas_call(
        functools.partial(head_sum_kernel, n),
        out_shape=jax.ShapeDtypeStruct((n, rows, width), parts.dtype),
        in_specs=[pl.BlockSpec(memory_space=pltpu.VMEM)],
        out_specs=pl.BlockSpec(memory_space=pltpu.VMEM),
        scratch_shapes=[
            pltpu.VMEM((n, rows, width), parts.dtype),
            pltpu.VMEM((n, rows, width), parts.dtype),
            pltpu.SemaphoreType.DMA((n,)),
            pltpu.SemaphoreType.DMA((n,)),
            pltpu.SemaphoreType.DMA((n,)),
            pltpu.SemaphoreType.DMA((n,)),
        ],
        compiler_params=pltpu.CompilerParams(collective_id=0, has_side_effects=True),
    )(parts)
    return out.reshape(n * rows, width)


def scan_steps(n):
    steps, d = [1], 1
    while d < n:
        steps.append(d)
        d *= 2
    return steps


def scan_kernel(rows_n, width, pack_ref, x_ref, dy_ref, sc_ref, cr_ref, cc_ref, o_ref, dx_ref,
                run_ref, recv1, win, out3, recv3, send1, rsem1, send2, rsem2, send3, rsem3, local):
    me = lax.axis_index("seq")
    col = lax.axis_index("head")
    c = me % width
    y = me // width
    piece = (recv1.shape[1] - 8) // 2
    steps = scan_steps(rows_n)
    spans = sorted(set(steps))

    length = sc_ref.shape[0]
    later = lax.broadcasted_iota(jnp.int32, (length, length), 1) >= lax.broadcasted_iota(
        jnp.int32, (length, length), 0)
    run_ref[...] = jnp.zeros(run_ref.shape, run_ref.dtype)

    def head(h):
        gaps = cr_ref[h:h + 1, :] - cc_ref[:, h:h + 1]
        dec = jnp.where(later, jnp.exp(jnp.where(later, gaps, 0.0)), 0.0)
        mix = (sc_ref[...] * dec).astype(jnp.bfloat16)
        lanes = slice(h * hd, (h + 1) * hd)
        dy_h = dy_ref[:, lanes]
        dx_ref[:, lanes] = jnp.dot(mix, dy_h, preferred_element_type=jnp.float32)
        pairs = lax.dot_general(
            x_ref[:, lanes], dy_h, (((1,), (1,)), ((), ())), preferred_element_type=jnp.float32)
        run_ref[...] += dec * pairs

    heads_left = list(range(cr_ref.shape[0]))
    hd = x_ref.shape[1] // cr_ref.shape[0]

    def heads(k):
        for _ in range(k):
            if heads_left:
                head(heads_left.pop(0))

    barrier = pltpu.get_barrier_semaphore()
    for off in range(1, width):
        peer = y * width + (c + off) % width
        pl.semaphore_signal(barrier, inc=1, device_id=(peer, col), device_id_type=MESH)
    for d in spans:
        @pl.when(y + d < rows_n)
        def _():
            pl.semaphore_signal(barrier, inc=1, device_id=(me + d * width, col), device_id_type=MESH)

        @pl.when(y - d >= 0)
        def _():
            pl.semaphore_signal(barrier, inc=1, device_id=(me - d * width, col), device_id_type=MESH)
    peers = width - 1
    for d in spans:
        peers = peers + ((rows_n - 1 - y) // d + rows_n - 1) // rows_n + (y // d + rows_n - 1) // rows_n
    heads(1)
    pl.semaphore_wait(barrier, peers)

    own = pltpu.make_async_copy(pack_ref.at[c], recv1.at[c], local.at[0])
    own.start()
    sends = []
    for off in range(1, width):
        k = (c + off) % width
        cp = pltpu.make_async_remote_copy(
            src_ref=pack_ref.at[k], dst_ref=recv1.at[c], send_sem=send1.at[off],
            recv_sem=rsem1.at[off], device_id=(y * width + k, col), device_id_type=MESH)
        cp.start()
        sends.append(cp)
    heads(3)
    for off in range(1, width):
        k = (c + width - off) % width
        pltpu.make_async_remote_copy(
            src_ref=pack_ref.at[k], dst_ref=recv1.at[k], send_sem=send1.at[off],
            recv_sem=rsem1.at[off], device_id=(y * width + k, col), device_id_type=MESH).wait_recv()
    own.wait()
    for cp in sends:
        cp.wait_send()

    def decay(i):
        return recv1[i, 2 * piece:2 * piece + 1, :]

    fwd_e, fwd_g = [None] * width, [None] * width
    e = jnp.zeros((piece, recv1.shape[2]), jnp.float32)
    g = jnp.ones((1, recv1.shape[2]), jnp.float32)
    for i in range(width):
        fwd_e[i], fwd_g[i] = e, g
        a = decay(i)
        e = a * e + recv1[i, :piece, :]
        g = g * a
    bwd_e, bwd_g = [None] * width, [None] * width
    f = jnp.zeros((piece, recv1.shape[2]), jnp.float32)
    h = jnp.ones((1, recv1.shape[2]), jnp.float32)
    for i in reversed(range(width)):
        bwd_e[i], bwd_g[i] = f, h
        a = decay(i)
        f = a * f + recv1[i, piece:2 * piece, :]
        h = h * a
    win[0, 0, :piece, :] = e
    win[0, 0, piece:, :] = jnp.broadcast_to(g, (win.shape[2] - piece, g.shape[1]))
    win[1, 0, :piece, :] = f
    win[1, 0, piece:, :] = jnp.broadcast_to(h, (win.shape[2] - piece, h.shape[1]))

    def copy2(way, r, target):
        src = win.at[way, 0] if r == 0 else win.at[way, r]
        return pltpu.make_async_remote_copy(
            src_ref=src, dst_ref=win.at[way, len(steps) + 1 + r],
            send_sem=send2.at[way, r], recv_sem=rsem2.at[way, r],
            device_id=(target, col), device_id_type=MESH)

    base = len(steps) + 1
    for r, d in enumerate(steps):
        for way, sign in ((0, 1), (1, -1)):
            target_row = y + sign * d

            @pl.when(jnp.logical_and(target_row >= 0, target_row < rows_n))
            def _():
                copy2(way, r, me + sign * d * width).start()
        heads(1 if r < len(steps) - 1 else len(heads_left))
        for way, sign in ((0, 1), (1, -1)):
            source_row = y - sign * d
            got = jnp.logical_and(source_row >= 0, source_row < rows_n)
            cur = 0 if r == 0 else r
            nxt = r + 1

            @pl.when(got)
            def _():
                copy2(way, r, me - sign * d * width).wait_recv()
                arrived = win[way, base + r]
                if r == 0:
                    win[way, nxt] = arrived
                else:
                    a = win[way, cur, piece:, :]
                    win[way, nxt, :piece, :] = win[way, cur, :piece, :] + jnp.broadcast_to(
                        a[:1], (piece, a.shape[1])) * arrived[:piece]
                    win[way, nxt, piece:, :] = a * arrived[piece:]

            @pl.when(jnp.logical_not(got))
            def _():
                if r == 0:
                    win[way, nxt] = jnp.zeros(win.shape[2:], win.dtype)
                else:
                    win[way, nxt] = win[way, cur]
    for r, d in enumerate(steps):
        for way, sign in ((0, 1), (1, -1)):
            target_row = y + sign * d

            @pl.when(jnp.logical_and(target_row >= 0, target_row < rows_n))
            def _():
                copy2(way, r, me + sign * d * width).wait_send()
    last = len(steps)
    entering = win[0, last, :piece, :]
    leaving = win[1, last, :piece, :]

    for i in range(width):
        out3[i, :piece, :] = fwd_e[i] + fwd_g[i] * entering
        out3[i, piece:, :] = bwd_e[i] + bwd_g[i] * leaving
    own = pltpu.make_async_copy(out3.at[c], recv3.at[c], local.at[1])
    own.start()
    sends = []
    for off in range(1, width):
        k = (c + off) % width
        cp = pltpu.make_async_remote_copy(
            src_ref=out3.at[k], dst_ref=recv3.at[c], send_sem=send3.at[off],
            recv_sem=rsem3.at[off], device_id=(y * width + k, col), device_id_type=MESH)
        cp.start()
        sends.append(cp)
    for off in range(1, width):
        k = (c + width - off) % width
        pltpu.make_async_remote_copy(
            src_ref=out3.at[k], dst_ref=recv3.at[k], send_sem=send3.at[off],
            recv_sem=rsem3.at[off], device_id=(y * width + k, col), device_id_type=MESH).wait_recv()
    own.wait()
    for cp in sends:
        cp.wait_send()
    o_ref[...] = recv3[...]


def exclusive_scans(count, decay_cols, forward, backward, x_heads, dy_heads, scores_t, cumulative):
    s, w = forward.shape
    width = 8 if count % 8 == 0 else 1
    rows_n = count // width
    piece = s // width
    rounds = len(scan_steps(rows_n))
    pack = jnp.concatenate(
        [
            forward.reshape(width, piece, w),
            backward.reshape(width, piece, w),
            jnp.broadcast_to(decay_cols[None], (width, 8, w)),
        ],
        axis=1,
    )
    length = scores_t.shape[0]
    out, dx, run = pl.pallas_call(
        functools.partial(scan_kernel, rows_n, width),
        out_shape=(
            jax.ShapeDtypeStruct((width, 2 * piece, w), jnp.float32),
            jax.ShapeDtypeStruct(x_heads.shape, jnp.float32),
            jax.ShapeDtypeStruct((length, length), jnp.float32),
        ),
        in_specs=[pl.BlockSpec(memory_space=pltpu.VMEM)] * 6,
        out_specs=(pl.BlockSpec(memory_space=pltpu.VMEM),) * 3,
        scratch_shapes=[
            pltpu.VMEM((width, 2 * piece + 8, w), jnp.float32),
            pltpu.VMEM((2, 2 * rounds + 1, piece + 8, w), jnp.float32),
            pltpu.VMEM((width, 2 * piece, w), jnp.float32),
            pltpu.VMEM((width, 2 * piece, w), jnp.float32),
            pltpu.SemaphoreType.DMA((width,)),
            pltpu.SemaphoreType.DMA((width,)),
            pltpu.SemaphoreType.DMA((2, rounds)),
            pltpu.SemaphoreType.DMA((2, rounds)),
            pltpu.SemaphoreType.DMA((width,)),
            pltpu.SemaphoreType.DMA((width,)),
            pltpu.SemaphoreType.DMA((2,)),
        ],
        compiler_params=pltpu.CompilerParams(collective_id=1, has_side_effects=True),
    )(pack, x_heads, dy_heads, scores_t, cumulative, cumulative.T)
    return out[:, :piece].reshape(s, w), out[:, piece:].reshape(s, w), dx, run


def shards(count, groups, token_values, b_inputs, c_inputs, log_decay, grad_out):
    length = token_values.shape[0]
    heads_here = log_decay.shape[0]
    head_dim = token_values.shape[1] // heads_here
    state_size = b_inputs.shape[1]
    cumulative = jnp.cumsum(log_decay, axis=1)
    block_log = cumulative[:, -1]
    into_end = jnp.exp(block_log[:, None] - cumulative)
    from_start = jnp.exp(cumulative)
    block_decay = jnp.exp(block_log)
    b_float = b_inputs.astype(jnp.float32)
    c_float = c_inputs.astype(jnp.float32)
    decayed_b = (into_end[:, :, None] * b_float[None]).astype(jnp.bfloat16)
    decayed_c = (from_start[:, :, None] * c_float[None]).astype(jnp.bfloat16)
    x_heads = token_values.reshape(length, heads_here, head_dim)
    dy_heads = grad_out.reshape(length, heads_here, head_dim)
    state_local = jnp.einsum(
        "htn,thp->nhp", decayed_b, x_heads, preferred_element_type=jnp.float32
    ).reshape(state_size, heads_here * head_dim)
    adjoint_local = jnp.einsum(
        "hsn,shp->nhp", decayed_c, dy_heads, preferred_element_type=jnp.float32
    ).reshape(state_size, heads_here * head_dim)
    decay_cols = jnp.repeat(block_decay, head_dim)[None, :]
    scores_t = lax.dot_general(
        b_inputs, c_inputs, (((1,), (1,)), ((), ())), preferred_element_type=jnp.float32
    )
    state_in, adjoint_out, dx_local, running_t = exclusive_scans(
        count, decay_cols, state_local, adjoint_local, token_values, grad_out, scores_t, cumulative
    )
    weighted_t = running_t.astype(jnp.bfloat16)
    db_part = jnp.dot(weighted_t, c_inputs, preferred_element_type=jnp.float32)
    dc_part = lax.dot_general(
        weighted_t, b_inputs, (((0,), (0,)), ((), ())), preferred_element_type=jnp.float32
    )
    to_end_cols = jnp.repeat(into_end.T, head_dim, axis=1)
    from_start_cols = jnp.repeat(from_start.T, head_dim, axis=1)
    grad_values = dx_local + to_end_cols * jnp.dot(b_float, adjoint_out, precision=PRECISE)
    db_part = db_part + jnp.dot(
        token_values.astype(jnp.float32) * to_end_cols, adjoint_out.T, precision=PRECISE
    )
    dc_part = dc_part + jnp.dot(
        grad_out.astype(jnp.float32) * from_start_cols, state_in.T, precision=PRECISE
    )
    both = head_sum(
        groups, jnp.concatenate([db_part, dc_part], axis=0).astype(jnp.bfloat16)
    )
    return grad_values.astype(jnp.bfloat16), both[:length], both[length:]


def solution(mesh):
    in_specs = (
        P("seq", "head"),
        P("seq", None),
        P("seq", None),
        P("head", "seq"),
        P("seq", "head"),
    )
    out_specs = (P("seq", "head"), P("seq", None), P("seq", None))
    body = functools.partial(shards, mesh.shape["seq"], mesh.shape["head"])
    return jax.shard_map(body, mesh=mesh, in_specs=in_specs, out_specs=out_specs, check_vma=False)
```

```python
import functools

import jax
import jax.numpy as jnp
from jax import lax
from jax.experimental import pallas as pl
from jax.experimental.pallas import tpu as pltpu
from jax.sharding import PartitionSpec as P

PRECISE = lax.Precision.HIGHEST
MESH = pl.DeviceIdType.MESH


def scan_steps(n):
    steps, d = [1], 1
    while d < n:
        steps.append(d)
        d *= 2
    return steps


def nt_dot(p, q):
    return lax.dot_general(p, q, (((1,), (1,)), ((), ())), preferred_element_type=jnp.float32)


def nt_dot_f32(p, q):
    ph = p.astype(jnp.bfloat16)
    pl_ = (p - ph.astype(jnp.float32)).astype(jnp.bfloat16)
    qh = q.astype(jnp.bfloat16)
    ql = (q - qh.astype(jnp.float32)).astype(jnp.bfloat16)
    return nt_dot(ph, qh) + (nt_dot(ph, ql) + nt_dot(pl_, qh))


def scan_kernel(rows_n, width, groups, pack_ref, x_ref, dy_ref, sc_ref, cr_ref, cc_ref, xs_ref,
                ds_ref, b_ref, c_ref, o_ref, dx_ref, sum_ref, run_ref, recv1, win, out3, recv3,
                full, parts, gather1, gather2, send1, rsem1, send2, rsem2, send3, rsem3, local,
                hsend1, hrecv1, hsend2, hrecv2):
    me = lax.axis_index("seq")
    col = lax.axis_index("head")
    c = me % width
    y = me // width
    piece = (recv1.shape[1] - 8) // 2
    steps = scan_steps(rows_n)
    spans = sorted(set(steps))

    length = sc_ref.shape[0]
    later = lax.broadcasted_iota(jnp.int32, (length, length), 1) >= lax.broadcasted_iota(
        jnp.int32, (length, length), 0)
    run_ref[...] = jnp.zeros(run_ref.shape, run_ref.dtype)

    def head(h):
        gaps = cr_ref[h:h + 1, :] - cc_ref[:, h:h + 1]
        dec = jnp.where(later, jnp.exp(jnp.where(later, gaps, 0.0)), 0.0)
        mix = (sc_ref[...] * dec).astype(jnp.bfloat16)
        lanes = slice(h * hd, (h + 1) * hd)
        dy_h = dy_ref[:, lanes]
        dx_ref[:, lanes] = jnp.dot(mix, dy_h, preferred_element_type=jnp.float32)
        pairs = lax.dot_general(
            x_ref[:, lanes], dy_h, (((1,), (1,)), ((), ())), preferred_element_type=jnp.float32)
        run_ref[...] += dec * pairs

    heads_left = list(range(cr_ref.shape[0]))
    hd = x_ref.shape[1] // cr_ref.shape[0]

    def heads(k):
        for _ in range(k):
            if heads_left:
                head(heads_left.pop(0))

    barrier = pltpu.get_barrier_semaphore()
    for off in range(1, width):
        peer = y * width + (c + off) % width
        pl.semaphore_signal(barrier, inc=1, device_id=(peer, col), device_id_type=MESH)
    for d in spans:
        @pl.when(y + d < rows_n)
        def _():
            pl.semaphore_signal(barrier, inc=1, device_id=(me + d * width, col), device_id_type=MESH)

        @pl.when(y - d >= 0)
        def _():
            pl.semaphore_signal(barrier, inc=1, device_id=(me - d * width, col), device_id_type=MESH)
    z = lax.axis_index("head")
    for off in range(1, groups):
        pl.semaphore_signal(
            barrier, inc=1, device_id=(me, (z + off) % groups), device_id_type=MESH)
    peers = width - 1 + groups - 1
    for d in spans:
        peers = peers + ((rows_n - 1 - y) // d + rows_n - 1) // rows_n + (y // d + rows_n - 1) // rows_n
    heads(1)
    pl.semaphore_wait(barrier, peers)

    own = pltpu.make_async_copy(pack_ref.at[c], recv1.at[c], local.at[0])
    own.start()
    sends = []
    for off in range(1, width):
        k = (c + off) % width
        cp = pltpu.make_async_remote_copy(
            src_ref=pack_ref.at[k], dst_ref=recv1.at[c], send_sem=send1.at[off],
            recv_sem=rsem1.at[off], device_id=(y * width + k, col), device_id_type=MESH)
        cp.start()
        sends.append(cp)
    heads(3)
    for off in range(1, width):
        k = (c + width - off) % width
        pltpu.make_async_remote_copy(
            src_ref=pack_ref.at[k], dst_ref=recv1.at[k], send_sem=send1.at[off],
            recv_sem=rsem1.at[off], device_id=(y * width + k, col), device_id_type=MESH).wait_recv()
    own.wait()
    for cp in sends:
        cp.wait_send()

    def decay(i):
        return recv1[i, 2 * piece:2 * piece + 1, :]

    fwd_e, fwd_g = [None] * width, [None] * width
    e = jnp.zeros((piece, recv1.shape[2]), jnp.float32)
    g = jnp.ones((1, recv1.shape[2]), jnp.float32)
    for i in range(width):
        fwd_e[i], fwd_g[i] = e, g
        a = decay(i)
        e = a * e + recv1[i, :piece, :]
        g = g * a
    bwd_e, bwd_g = [None] * width, [None] * width
    f = jnp.zeros((piece, recv1.shape[2]), jnp.float32)
    h = jnp.ones((1, recv1.shape[2]), jnp.float32)
    for i in reversed(range(width)):
        bwd_e[i], bwd_g[i] = f, h
        a = decay(i)
        f = a * f + recv1[i, piece:2 * piece, :]
        h = h * a
    win[0, 0, :piece, :] = e
    win[0, 0, piece:, :] = jnp.broadcast_to(g, (win.shape[2] - piece, g.shape[1]))
    win[1, 0, :piece, :] = f
    win[1, 0, piece:, :] = jnp.broadcast_to(h, (win.shape[2] - piece, h.shape[1]))

    def copy2(way, r, target):
        src = win.at[way, 0] if r == 0 else win.at[way, r]
        return pltpu.make_async_remote_copy(
            src_ref=src, dst_ref=win.at[way, len(steps) + 1 + r],
            send_sem=send2.at[way, r], recv_sem=rsem2.at[way, r],
            device_id=(target, col), device_id_type=MESH)

    base = len(steps) + 1
    for r, d in enumerate(steps):
        for way, sign in ((0, 1), (1, -1)):
            target_row = y + sign * d

            @pl.when(jnp.logical_and(target_row >= 0, target_row < rows_n))
            def _():
                copy2(way, r, me + sign * d * width).start()
        heads(1 if r < len(steps) - 1 else len(heads_left))
        for way, sign in ((0, 1), (1, -1)):
            source_row = y - sign * d
            got = jnp.logical_and(source_row >= 0, source_row < rows_n)
            cur = 0 if r == 0 else r
            nxt = r + 1

            @pl.when(got)
            def _():
                copy2(way, r, me - sign * d * width).wait_recv()
                arrived = win[way, base + r]
                if r == 0:
                    win[way, nxt] = arrived
                else:
                    a = win[way, cur, piece:, :]
                    win[way, nxt, :piece, :] = win[way, cur, :piece, :] + jnp.broadcast_to(
                        a[:1], (piece, a.shape[1])) * arrived[:piece]
                    win[way, nxt, piece:, :] = a * arrived[piece:]

            @pl.when(jnp.logical_not(got))
            def _():
                if r == 0:
                    win[way, nxt] = jnp.zeros(win.shape[2:], win.dtype)
                else:
                    win[way, nxt] = win[way, cur]
    for r, d in enumerate(steps):
        for way, sign in ((0, 1), (1, -1)):
            target_row = y + sign * d

            @pl.when(jnp.logical_and(target_row >= 0, target_row < rows_n))
            def _():
                copy2(way, r, me + sign * d * width).wait_send()
    last = len(steps)
    entering = win[0, last, :piece, :]
    leaving = win[1, last, :piece, :]

    for i in range(width):
        out3[i, :piece, :] = fwd_e[i] + fwd_g[i] * entering
        out3[i, piece:, :] = bwd_e[i] + bwd_g[i] * leaving
    own = pltpu.make_async_copy(out3.at[c], recv3.at[c], local.at[1])
    own.start()
    sends = []
    for off in range(1, width):
        k = (c + off) % width
        cp = pltpu.make_async_remote_copy(
            src_ref=out3.at[k], dst_ref=recv3.at[c], send_sem=send3.at[off],
            recv_sem=rsem3.at[off], device_id=(y * width + k, col), device_id_type=MESH)
        cp.start()
        sends.append(cp)
    for off in range(1, width):
        k = (c + width - off) % width
        pltpu.make_async_remote_copy(
            src_ref=out3.at[k], dst_ref=recv3.at[k], send_sem=send3.at[off],
            recv_sem=rsem3.at[off], device_id=(y * width + k, col), device_id_type=MESH).wait_recv()
    own.wait()
    for cp in sends:
        cp.wait_send()
    o_ref[...] = recv3[...]

    s = width * piece
    for k in range(width):
        full[0, k * piece:(k + 1) * piece, :] = recv3[k, :piece, :]
        full[1, k * piece:(k + 1) * piece, :] = recv3[k, piece:, :]
    weighted = run_ref[...].astype(jnp.bfloat16)
    part_b = jnp.dot(weighted, c_ref[...], preferred_element_type=jnp.float32) + nt_dot_f32(
        xs_ref[...], full[1])
    part_c = lax.dot_general(
        weighted, b_ref[...], (((0,), (0,)), ((), ())), preferred_element_type=jnp.float32
    ) + nt_dot_f32(ds_ref[...], full[0])
    n_rows = part_b.shape[0]
    parts[:n_rows, :] = part_b.astype(parts.dtype)
    parts[n_rows:, :] = part_c.astype(parts.dtype)
    rows = gather1.shape[1]

    def chunk(i):
        return parts.at[pl.ds(pl.multiple_of(i * rows, rows), rows)]

    sends = []
    for k in range(1, groups):
        peer = (z + k) % groups
        cp = pltpu.make_async_remote_copy(
            src_ref=chunk(peer), dst_ref=gather1.at[z], send_sem=hsend1.at[k],
            recv_sem=hrecv1.at[k], device_id=(me, peer), device_id_type=MESH)
        cp.start()
        sends.append(cp)
    total = parts[pl.ds(pl.multiple_of(z * rows, rows), rows), :].astype(jnp.float32)
    for k in range(1, groups):
        source = (z + groups - k) % groups
        pltpu.make_async_remote_copy(
            src_ref=chunk(source), dst_ref=gather1.at[source], send_sem=hsend1.at[k],
            recv_sem=hrecv1.at[k], device_id=(me, source), device_id_type=MESH).wait_recv()
        total = total + gather1[source].astype(jnp.float32)
    for cp in sends:
        cp.wait_send()
    gather2[z] = total.astype(gather2.dtype)
    sends = []
    for k in range(1, groups):
        peer = (z + k) % groups
        cp = pltpu.make_async_remote_copy(
            src_ref=gather2.at[z], dst_ref=gather2.at[z], send_sem=hsend2.at[k],
            recv_sem=hrecv2.at[k], device_id=(me, peer), device_id_type=MESH)
        cp.start()
        sends.append(cp)
    for k in range(1, groups):
        source = (z + groups - k) % groups
        pltpu.make_async_remote_copy(
            src_ref=gather2.at[source], dst_ref=gather2.at[source], send_sem=hsend2.at[k],
            recv_sem=hrecv2.at[k], device_id=(me, source), device_id_type=MESH).wait_recv()
    for cp in sends:
        cp.wait_send()
    sum_ref[...] = gather2[...]


def exclusive_scans(count, groups, decay_cols, forward, backward, x, dy, scores_t, cumulative,
                    x_scaled, dy_scaled, b_inputs, c_inputs):
    s, w = forward.shape
    width = 8 if count % 8 == 0 else 1
    rows_n = count // width
    piece = s // width
    rounds = len(scan_steps(rows_n))
    pack = jnp.concatenate(
        [
            forward.reshape(width, piece, w),
            backward.reshape(width, piece, w),
            jnp.broadcast_to(decay_cols[None], (width, 8, w)),
        ],
        axis=1,
    )
    length = scores_t.shape[0]
    chunk_rows = 2 * length // groups
    out, dx, sums = pl.pallas_call(
        functools.partial(scan_kernel, rows_n, width, groups),
        out_shape=(
            jax.ShapeDtypeStruct((width, 2 * piece, w), jnp.float32),
            jax.ShapeDtypeStruct(x.shape, jnp.float32),
            jax.ShapeDtypeStruct((groups, chunk_rows, s), jnp.bfloat16),
        ),
        in_specs=[pl.BlockSpec(memory_space=pltpu.VMEM)] * 10,
        out_specs=(pl.BlockSpec(memory_space=pltpu.VMEM),) * 3,
        scratch_shapes=[
            pltpu.VMEM((length, length), jnp.float32),
            pltpu.VMEM((width, 2 * piece + 8, w), jnp.float32),
            pltpu.VMEM((2, 2 * rounds + 1, piece + 8, w), jnp.float32),
            pltpu.VMEM((width, 2 * piece, w), jnp.float32),
            pltpu.VMEM((width, 2 * piece, w), jnp.float32),
            pltpu.VMEM((2, s, w), jnp.float32),
            pltpu.VMEM((2 * length, s), jnp.bfloat16),
            pltpu.VMEM((groups, chunk_rows, s), jnp.bfloat16),
            pltpu.VMEM((groups, chunk_rows, s), jnp.bfloat16),
            pltpu.SemaphoreType.DMA((width,)),
            pltpu.SemaphoreType.DMA((width,)),
            pltpu.SemaphoreType.DMA((2, rounds)),
            pltpu.SemaphoreType.DMA((2, rounds)),
            pltpu.SemaphoreType.DMA((width,)),
            pltpu.SemaphoreType.DMA((width,)),
            pltpu.SemaphoreType.DMA((2,)),
            pltpu.SemaphoreType.DMA((groups,)),
            pltpu.SemaphoreType.DMA((groups,)),
            pltpu.SemaphoreType.DMA((groups,)),
            pltpu.SemaphoreType.DMA((groups,)),
        ],
        compiler_params=pltpu.CompilerParams(collective_id=1, has_side_effects=True),
    )(pack, x, dy, scores_t, cumulative, cumulative.T, x_scaled, dy_scaled, b_inputs, c_inputs)
    sums = sums.reshape(2 * length, s)
    return out[:, :piece].reshape(s, w), out[:, piece:].reshape(s, w), dx, sums[:length], sums[length:]


def shards(count, groups, token_values, b_inputs, c_inputs, log_decay, grad_out):
    length = token_values.shape[0]
    heads_here = log_decay.shape[0]
    head_dim = token_values.shape[1] // heads_here
    state_size = b_inputs.shape[1]
    cumulative = jnp.cumsum(log_decay, axis=1)
    block_log = cumulative[:, -1]
    into_end = jnp.exp(block_log[:, None] - cumulative)
    from_start = jnp.exp(cumulative)
    block_decay = jnp.exp(block_log)
    b_float = b_inputs.astype(jnp.float32)
    c_float = c_inputs.astype(jnp.float32)
    decayed_b = (into_end[:, :, None] * b_float[None]).astype(jnp.bfloat16)
    decayed_c = (from_start[:, :, None] * c_float[None]).astype(jnp.bfloat16)
    x_heads = token_values.reshape(length, heads_here, head_dim)
    dy_heads = grad_out.reshape(length, heads_here, head_dim)
    state_local = jnp.einsum(
        "htn,thp->nhp", decayed_b, x_heads, preferred_element_type=jnp.float32
    ).reshape(state_size, heads_here * head_dim)
    adjoint_local = jnp.einsum(
        "hsn,shp->nhp", decayed_c, dy_heads, preferred_element_type=jnp.float32
    ).reshape(state_size, heads_here * head_dim)
    decay_cols = jnp.repeat(block_decay, head_dim)[None, :]
    scores_t = lax.dot_general(
        b_inputs, c_inputs, (((1,), (1,)), ((), ())), preferred_element_type=jnp.float32
    )
    to_end_cols = jnp.repeat(into_end.T, head_dim, axis=1)
    from_start_cols = jnp.repeat(from_start.T, head_dim, axis=1)
    state_in, adjoint_out, dx_local, grad_b, grad_c = exclusive_scans(
        count, groups, decay_cols, state_local, adjoint_local, token_values, grad_out, scores_t,
        cumulative, token_values.astype(jnp.float32) * to_end_cols,
        grad_out.astype(jnp.float32) * from_start_cols, b_inputs, c_inputs,
    )
    grad_values = dx_local + to_end_cols * jnp.dot(b_float, adjoint_out, precision=PRECISE)
    return grad_values.astype(jnp.bfloat16), grad_b, grad_c


def solution(mesh):
    in_specs = (
        P("seq", "head"),
        P("seq", None),
        P("seq", None),
        P("head", "seq"),
        P("seq", "head"),
    )
    out_specs = (P("seq", "head"), P("seq", None), P("seq", None))
    body = functools.partial(shards, mesh.shape["seq"], mesh.shape["head"])
    return jax.shard_map(body, mesh=mesh, in_specs=in_specs, out_specs=out_specs, check_vma=False)
```

```python
import functools

import jax
import jax.numpy as jnp
from jax import lax
from jax.experimental import pallas as pl
from jax.experimental.pallas import tpu as pltpu
from jax.sharding import PartitionSpec as P

PRECISE = lax.Precision.HIGHEST
MESH = pl.DeviceIdType.MESH


def scan_steps(n):
    steps, d = [1], 1
    while d < n:
        steps.append(d)
        d *= 2
    return steps


def nt_dot(p, q):
    return lax.dot_general(p, q, (((1,), (1,)), ((), ())), preferred_element_type=jnp.float32)


def nt_dot_f32(p, q):
    ph = p.astype(jnp.bfloat16)
    pl_ = (p - ph.astype(jnp.float32)).astype(jnp.bfloat16)
    qh = q.astype(jnp.bfloat16)
    ql = (q - qh.astype(jnp.float32)).astype(jnp.bfloat16)
    return nt_dot(ph, qh) + (nt_dot(ph, ql) + nt_dot(pl_, qh))


def scan_kernel(rows_n, width, groups, pack_ref, x_ref, dy_ref, sc_ref, cr_ref, cc_ref, ie_ref,
                fs_ref, b_ref, c_ref, gv_ref, sum_ref, run_ref, dx_ref, xs_ref, ds_ref, recv1, win,
                out3, recv3, full, parts, gather1, gather2, send1, rsem1, send2, rsem2, send3, rsem3, local,
                hsend1, hrecv1, hsend2, hrecv2):
    me = lax.axis_index("seq")
    col = lax.axis_index("head")
    c = me % width
    y = me // width
    piece = (recv1.shape[1] - 8) // 2
    steps = scan_steps(rows_n)
    spans = sorted(set(steps))

    length = sc_ref.shape[0]
    later = lax.broadcasted_iota(jnp.int32, (length, length), 1) >= lax.broadcasted_iota(
        jnp.int32, (length, length), 0)
    run_ref[...] = jnp.zeros(run_ref.shape, run_ref.dtype)

    def head(h):
        gaps = cr_ref[h:h + 1, :] - cc_ref[:, h:h + 1]
        dec = jnp.where(later, jnp.exp(jnp.where(later, gaps, 0.0)), 0.0)
        mix = (sc_ref[...] * dec).astype(jnp.bfloat16)
        lanes = slice(h * hd, (h + 1) * hd)
        dy_h = dy_ref[:, lanes]
        x_h = x_ref[:, lanes]
        xs_ref[:, lanes] = x_h.astype(jnp.float32) * ie_ref[:, h:h + 1]
        ds_ref[:, lanes] = dy_h.astype(jnp.float32) * fs_ref[:, h:h + 1]
        dx_ref[:, lanes] = jnp.dot(mix, dy_h, preferred_element_type=jnp.float32)
        pairs = lax.dot_general(
            x_h, dy_h, (((1,), (1,)), ((), ())), preferred_element_type=jnp.float32)
        run_ref[...] += dec * pairs

    heads_left = list(range(cr_ref.shape[0]))
    hd = x_ref.shape[1] // cr_ref.shape[0]

    def heads(k):
        for _ in range(k):
            if heads_left:
                head(heads_left.pop(0))

    barrier = pltpu.get_barrier_semaphore()
    for off in range(1, width):
        peer = y * width + (c + off) % width
        pl.semaphore_signal(barrier, inc=1, device_id=(peer, col), device_id_type=MESH)
    for d in spans:
        @pl.when(y + d < rows_n)
        def _():
            pl.semaphore_signal(barrier, inc=1, device_id=(me + d * width, col), device_id_type=MESH)

        @pl.when(y - d >= 0)
        def _():
            pl.semaphore_signal(barrier, inc=1, device_id=(me - d * width, col), device_id_type=MESH)
    z = lax.axis_index("head")
    for off in range(1, groups):
        pl.semaphore_signal(
            barrier, inc=1, device_id=(me, (z + off) % groups), device_id_type=MESH)
    peers = width - 1 + groups - 1
    for d in spans:
        peers = peers + ((rows_n - 1 - y) // d + rows_n - 1) // rows_n + (y // d + rows_n - 1) // rows_n
    heads(1)
    pl.semaphore_wait(barrier, peers)

    own = pltpu.make_async_copy(pack_ref.at[c], recv1.at[c], local.at[0])
    own.start()
    sends = []
    for off in range(1, width):
        k = (c + off) % width
        cp = pltpu.make_async_remote_copy(
            src_ref=pack_ref.at[k], dst_ref=recv1.at[c], send_sem=send1.at[off],
            recv_sem=rsem1.at[off], device_id=(y * width + k, col), device_id_type=MESH)
        cp.start()
        sends.append(cp)
    heads(3)
    for off in range(1, width):
        k = (c + width - off) % width
        pltpu.make_async_remote_copy(
            src_ref=pack_ref.at[k], dst_ref=recv1.at[k], send_sem=send1.at[off],
            recv_sem=rsem1.at[off], device_id=(y * width + k, col), device_id_type=MESH).wait_recv()
    own.wait()
    for cp in sends:
        cp.wait_send()

    def decay(i):
        return recv1[i, 2 * piece:2 * piece + 1, :]

    fwd_e, fwd_g = [None] * width, [None] * width
    e = jnp.zeros((piece, recv1.shape[2]), jnp.float32)
    g = jnp.ones((1, recv1.shape[2]), jnp.float32)
    for i in range(width):
        fwd_e[i], fwd_g[i] = e, g
        a = decay(i)
        e = a * e + recv1[i, :piece, :]
        g = g * a
    bwd_e, bwd_g = [None] * width, [None] * width
    f = jnp.zeros((piece, recv1.shape[2]), jnp.float32)
    h = jnp.ones((1, recv1.shape[2]), jnp.float32)
    for i in reversed(range(width)):
        bwd_e[i], bwd_g[i] = f, h
        a = decay(i)
        f = a * f + recv1[i, piece:2 * piece, :]
        h = h * a
    win[0, 0, :piece, :] = e
    win[0, 0, piece:, :] = jnp.broadcast_to(g, (win.shape[2] - piece, g.shape[1]))
    win[1, 0, :piece, :] = f
    win[1, 0, piece:, :] = jnp.broadcast_to(h, (win.shape[2] - piece, h.shape[1]))

    def copy2(way, r, target):
        src = win.at[way, 0] if r == 0 else win.at[way, r]
        return pltpu.make_async_remote_copy(
            src_ref=src, dst_ref=win.at[way, len(steps) + 1 + r],
            send_sem=send2.at[way, r], recv_sem=rsem2.at[way, r],
            device_id=(target, col), device_id_type=MESH)

    base = len(steps) + 1
    for r, d in enumerate(steps):
        for way, sign in ((0, 1), (1, -1)):
            target_row = y + sign * d

            @pl.when(jnp.logical_and(target_row >= 0, target_row < rows_n))
            def _():
                copy2(way, r, me + sign * d * width).start()
        heads(1 if r < len(steps) - 1 else len(heads_left))
        for way, sign in ((0, 1), (1, -1)):
            source_row = y - sign * d
            got = jnp.logical_and(source_row >= 0, source_row < rows_n)
            cur = 0 if r == 0 else r
            nxt = r + 1

            @pl.when(got)
            def _():
                copy2(way, r, me - sign * d * width).wait_recv()
                arrived = win[way, base + r]
                if r == 0:
                    win[way, nxt] = arrived
                else:
                    a = win[way, cur, piece:, :]
                    win[way, nxt, :piece, :] = win[way, cur, :piece, :] + jnp.broadcast_to(
                        a[:1], (piece, a.shape[1])) * arrived[:piece]
                    win[way, nxt, piece:, :] = a * arrived[piece:]

            @pl.when(jnp.logical_not(got))
            def _():
                if r == 0:
                    win[way, nxt] = jnp.zeros(win.shape[2:], win.dtype)
                else:
                    win[way, nxt] = win[way, cur]
    for r, d in enumerate(steps):
        for way, sign in ((0, 1), (1, -1)):
            target_row = y + sign * d

            @pl.when(jnp.logical_and(target_row >= 0, target_row < rows_n))
            def _():
                copy2(way, r, me + sign * d * width).wait_send()
    last = len(steps)
    entering = win[0, last, :piece, :]
    leaving = win[1, last, :piece, :]

    for i in range(width):
        out3[i, :piece, :] = fwd_e[i] + fwd_g[i] * entering
        out3[i, piece:, :] = bwd_e[i] + bwd_g[i] * leaving
    own = pltpu.make_async_copy(out3.at[c], recv3.at[c], local.at[1])
    own.start()
    sends = []
    for off in range(1, width):
        k = (c + off) % width
        cp = pltpu.make_async_remote_copy(
            src_ref=out3.at[k], dst_ref=recv3.at[c], send_sem=send3.at[off],
            recv_sem=rsem3.at[off], device_id=(y * width + k, col), device_id_type=MESH)
        cp.start()
        sends.append(cp)
    for off in range(1, width):
        k = (c + width - off) % width
        pltpu.make_async_remote_copy(
            src_ref=out3.at[k], dst_ref=recv3.at[k], send_sem=send3.at[off],
            recv_sem=rsem3.at[off], device_id=(y * width + k, col), device_id_type=MESH).wait_recv()
    own.wait()
    for cp in sends:
        cp.wait_send()

    s = width * piece
    for k in range(width):
        full[0, k * piece:(k + 1) * piece, :] = recv3[k, :piece, :]
        full[1, k * piece:(k + 1) * piece, :] = recv3[k, piece:, :]
    weighted = run_ref[...].astype(jnp.bfloat16)
    part_b = jnp.dot(weighted, c_ref[...], preferred_element_type=jnp.float32) + nt_dot_f32(
        xs_ref[...], full[1])
    part_c = lax.dot_general(
        weighted, b_ref[...], (((0,), (0,)), ((), ())), preferred_element_type=jnp.float32
    ) + nt_dot_f32(ds_ref[...], full[0])
    n_rows = part_b.shape[0]
    adj = full[1]
    adj_hi = adj.astype(jnp.bfloat16)
    adj_lo = (adj - adj_hi.astype(jnp.float32)).astype(jnp.bfloat16)
    b_adj = jnp.dot(b_ref[...], adj_hi, preferred_element_type=jnp.float32) + jnp.dot(
        b_ref[...], adj_lo, preferred_element_type=jnp.float32)
    for h in range(cr_ref.shape[0]):
        lanes = slice(h * hd, (h + 1) * hd)
        gv_ref[:, lanes] = (dx_ref[:, lanes] + ie_ref[:, h:h + 1] * b_adj[:, lanes]).astype(
            gv_ref.dtype)
    parts[:n_rows, :] = part_b.astype(parts.dtype)
    parts[n_rows:, :] = part_c.astype(parts.dtype)
    rows = gather1.shape[1]

    def chunk(i):
        return parts.at[pl.ds(pl.multiple_of(i * rows, rows), rows)]

    sends = []
    for k in range(1, groups):
        peer = (z + k) % groups
        cp = pltpu.make_async_remote_copy(
            src_ref=chunk(peer), dst_ref=gather1.at[z], send_sem=hsend1.at[k],
            recv_sem=hrecv1.at[k], device_id=(me, peer), device_id_type=MESH)
        cp.start()
        sends.append(cp)
    total = parts[pl.ds(pl.multiple_of(z * rows, rows), rows), :].astype(jnp.float32)
    for k in range(1, groups):
        source = (z + groups - k) % groups
        pltpu.make_async_remote_copy(
            src_ref=chunk(source), dst_ref=gather1.at[source], send_sem=hsend1.at[k],
            recv_sem=hrecv1.at[k], device_id=(me, source), device_id_type=MESH).wait_recv()
        total = total + gather1[source].astype(jnp.float32)
    for cp in sends:
        cp.wait_send()
    gather2[z] = total.astype(gather2.dtype)
    sends = []
    for k in range(1, groups):
        peer = (z + k) % groups
        cp = pltpu.make_async_remote_copy(
            src_ref=gather2.at[z], dst_ref=gather2.at[z], send_sem=hsend2.at[k],
            recv_sem=hrecv2.at[k], device_id=(me, peer), device_id_type=MESH)
        cp.start()
        sends.append(cp)
    for k in range(1, groups):
        source = (z + groups - k) % groups
        pltpu.make_async_remote_copy(
            src_ref=gather2.at[source], dst_ref=gather2.at[source], send_sem=hsend2.at[k],
            recv_sem=hrecv2.at[k], device_id=(me, source), device_id_type=MESH).wait_recv()
    for cp in sends:
        cp.wait_send()
    sum_ref[...] = gather2[...]


def exclusive_scans(count, groups, decay_cols, forward, backward, x, dy, scores_t, cumulative,
                    into_end, from_start, b_inputs, c_inputs):
    s, w = forward.shape
    width = 8 if count % 8 == 0 else 1
    rows_n = count // width
    piece = s // width
    rounds = len(scan_steps(rows_n))
    pack = jnp.concatenate(
        [
            forward.reshape(width, piece, w),
            backward.reshape(width, piece, w),
            jnp.broadcast_to(decay_cols[None], (width, 8, w)),
        ],
        axis=1,
    )
    length = scores_t.shape[0]
    chunk_rows = 2 * length // groups
    grad_values, sums = pl.pallas_call(
        functools.partial(scan_kernel, rows_n, width, groups),
        out_shape=(
            jax.ShapeDtypeStruct(x.shape, jnp.bfloat16),
            jax.ShapeDtypeStruct((groups, chunk_rows, s), jnp.bfloat16),
        ),
        in_specs=[pl.BlockSpec(memory_space=pltpu.VMEM)] * 10,
        out_specs=(pl.BlockSpec(memory_space=pltpu.VMEM),) * 2,
        scratch_shapes=[
            pltpu.VMEM((length, length), jnp.float32),
            pltpu.VMEM(x.shape, jnp.float32),
            pltpu.VMEM(x.shape, jnp.float32),
            pltpu.VMEM(x.shape, jnp.float32),
            pltpu.VMEM((width, 2 * piece + 8, w), jnp.float32),
            pltpu.VMEM((2, 2 * rounds + 1, piece + 8, w), jnp.float32),
            pltpu.VMEM((width, 2 * piece, w), jnp.float32),
            pltpu.VMEM((width, 2 * piece, w), jnp.float32),
            pltpu.VMEM((2, s, w), jnp.float32),
            pltpu.VMEM((2 * length, s), jnp.bfloat16),
            pltpu.VMEM((groups, chunk_rows, s), jnp.bfloat16),
            pltpu.VMEM((groups, chunk_rows, s), jnp.bfloat16),
            pltpu.SemaphoreType.DMA((width,)),
            pltpu.SemaphoreType.DMA((width,)),
            pltpu.SemaphoreType.DMA((2, rounds)),
            pltpu.SemaphoreType.DMA((2, rounds)),
            pltpu.SemaphoreType.DMA((width,)),
            pltpu.SemaphoreType.DMA((width,)),
            pltpu.SemaphoreType.DMA((2,)),
            pltpu.SemaphoreType.DMA((groups,)),
            pltpu.SemaphoreType.DMA((groups,)),
            pltpu.SemaphoreType.DMA((groups,)),
            pltpu.SemaphoreType.DMA((groups,)),
        ],
        compiler_params=pltpu.CompilerParams(collective_id=1, has_side_effects=True),
    )(pack, x, dy, scores_t, cumulative, cumulative.T, into_end.T, from_start.T, b_inputs, c_inputs)
    sums = sums.reshape(2 * length, s)
    return grad_values, sums[:length], sums[length:]


def shards(count, groups, token_values, b_inputs, c_inputs, log_decay, grad_out):
    length = token_values.shape[0]
    heads_here = log_decay.shape[0]
    head_dim = token_values.shape[1] // heads_here
    state_size = b_inputs.shape[1]
    cumulative = jnp.cumsum(log_decay, axis=1)
    block_log = cumulative[:, -1]
    into_end = jnp.exp(block_log[:, None] - cumulative)
    from_start = jnp.exp(cumulative)
    block_decay = jnp.exp(block_log)
    b_float = b_inputs.astype(jnp.float32)
    c_float = c_inputs.astype(jnp.float32)
    decayed_b = (into_end[:, :, None] * b_float[None]).astype(jnp.bfloat16)
    decayed_c = (from_start[:, :, None] * c_float[None]).astype(jnp.bfloat16)
    x_heads = token_values.reshape(length, heads_here, head_dim)
    dy_heads = grad_out.reshape(length, heads_here, head_dim)
    state_local = jnp.einsum(
        "htn,thp->nhp", decayed_b, x_heads, preferred_element_type=jnp.float32
    ).reshape(state_size, heads_here * head_dim)
    adjoint_local = jnp.einsum(
        "hsn,shp->nhp", decayed_c, dy_heads, preferred_element_type=jnp.float32
    ).reshape(state_size, heads_here * head_dim)
    decay_cols = jnp.repeat(block_decay, head_dim)[None, :]
    scores_t = lax.dot_general(
        b_inputs, c_inputs, (((1,), (1,)), ((), ())), preferred_element_type=jnp.float32
    )
    grad_values, grad_b, grad_c = exclusive_scans(
        count, groups, decay_cols, state_local, adjoint_local, token_values, grad_out, scores_t,
        cumulative, into_end, from_start, b_inputs, c_inputs,
    )
    return grad_values, grad_b, grad_c


def solution(mesh):
    in_specs = (
        P("seq", "head"),
        P("seq", None),
        P("seq", None),
        P("head", "seq"),
        P("seq", "head"),
    )
    out_specs = (P("seq", "head"), P("seq", None), P("seq", None))
    body = functools.partial(shards, mesh.shape["seq"], mesh.shape["head"])
    return jax.shard_map(body, mesh=mesh, in_specs=in_specs, out_specs=out_specs, check_vma=False)
```

```python
import functools

import jax
import jax.numpy as jnp
from jax import lax
from jax.experimental import pallas as pl
from jax.experimental.pallas import tpu as pltpu
from jax.sharding import PartitionSpec as P

PRECISE = lax.Precision.HIGHEST
MESH = pl.DeviceIdType.MESH


def scan_steps(n):
    steps, d = [1], 1
    while d < n:
        steps.append(d)
        d *= 2
    return steps


def nt_dot(p, q):
    return lax.dot_general(p, q, (((1,), (1,)), ((), ())), preferred_element_type=jnp.float32)


def nt_dot_f32(p, q):
    ph = p.astype(jnp.bfloat16)
    pl_ = (p - ph.astype(jnp.float32)).astype(jnp.bfloat16)
    qh = q.astype(jnp.bfloat16)
    ql = (q - qh.astype(jnp.float32)).astype(jnp.bfloat16)
    return nt_dot(ph, qh) + (nt_dot(ph, ql) + nt_dot(pl_, qh))


def scan_kernel(rows_n, width, groups, pack_ref, x_ref, dy_ref, sc_ref, cr_ref, cc_ref, ie_ref,
                fs_ref, b_ref, c_ref, gv_ref, sum_ref, run_ref, dx_ref, xs_ref, ds_ref, recv1, win,
                out3, recv3, full, parts, gather1, gather2, send1, rsem1, send2, rsem2, send3, rsem3, local,
                hsend1, hrecv1, hsend2, hrecv2):
    me = lax.axis_index("seq")
    col = lax.axis_index("head")
    c = me % width
    y = me // width
    piece = (recv1.shape[1] - 8) // 2
    steps = scan_steps(rows_n)
    spans = sorted(set(steps))

    length = sc_ref.shape[0]
    later = lax.broadcasted_iota(jnp.int32, (length, length), 1) >= lax.broadcasted_iota(
        jnp.int32, (length, length), 0)
    run_ref[...] = jnp.zeros(run_ref.shape, run_ref.dtype)

    def head(h):
        gaps = cr_ref[h:h + 1, :] - cc_ref[:, h:h + 1]
        dec = jnp.where(later, jnp.exp(jnp.where(later, gaps, 0.0)), 0.0)
        mix = (sc_ref[...] * dec).astype(jnp.bfloat16)
        lanes = slice(h * hd, (h + 1) * hd)
        dy_h = dy_ref[:, lanes]
        x_h = x_ref[:, lanes]
        xs_ref[:, lanes] = x_h.astype(jnp.float32) * ie_ref[:, h:h + 1]
        ds_ref[:, lanes] = dy_h.astype(jnp.float32) * fs_ref[:, h:h + 1]
        dx_ref[:, lanes] = jnp.dot(mix, dy_h, preferred_element_type=jnp.float32)
        pairs = lax.dot_general(
            x_h, dy_h, (((1,), (1,)), ((), ())), preferred_element_type=jnp.float32)
        run_ref[...] += dec * pairs

    heads_left = list(range(cr_ref.shape[0]))
    hd = x_ref.shape[1] // cr_ref.shape[0]

    def heads(k):
        for _ in range(k):
            if heads_left:
                head(heads_left.pop(0))

    barrier = pltpu.get_barrier_semaphore()
    for off in range(1, width):
        peer = y * width + (c + off) % width
        pl.semaphore_signal(barrier, inc=1, device_id=(peer, col), device_id_type=MESH)
    for d in spans:
        @pl.when(y + d < rows_n)
        def _():
            pl.semaphore_signal(barrier, inc=1, device_id=(me + d * width, col), device_id_type=MESH)

        @pl.when(y - d >= 0)
        def _():
            pl.semaphore_signal(barrier, inc=1, device_id=(me - d * width, col), device_id_type=MESH)
    z = lax.axis_index("head")
    for off in range(1, groups):
        pl.semaphore_signal(
            barrier, inc=1, device_id=(me, (z + off) % groups), device_id_type=MESH)
    peers = width - 1 + groups - 1
    for d in spans:
        peers = peers + ((rows_n - 1 - y) // d + rows_n - 1) // rows_n + (y // d + rows_n - 1) // rows_n
    heads(1)
    pl.semaphore_wait(barrier, peers)

    own = pltpu.make_async_copy(pack_ref.at[c], recv1.at[c], local.at[0])
    own.start()
    sends = []
    for off in range(1, width):
        k = (c + off) % width
        cp = pltpu.make_async_remote_copy(
            src_ref=pack_ref.at[k], dst_ref=recv1.at[c], send_sem=send1.at[off],
            recv_sem=rsem1.at[off], device_id=(y * width + k, col), device_id_type=MESH)
        cp.start()
        sends.append(cp)
    heads(3)
    for off in range(1, width):
        k = (c + width - off) % width
        pltpu.make_async_remote_copy(
            src_ref=pack_ref.at[k], dst_ref=recv1.at[k], send_sem=send1.at[off],
            recv_sem=rsem1.at[off], device_id=(y * width + k, col), device_id_type=MESH).wait_recv()
    own.wait()
    for cp in sends:
        cp.wait_send()

    def decay(i):
        return recv1[i, 2 * piece:2 * piece + 1, :]

    fwd_e, fwd_g = [None] * width, [None] * width
    e = jnp.zeros((piece, recv1.shape[2]), jnp.float32)
    g = jnp.ones((1, recv1.shape[2]), jnp.float32)
    for i in range(width):
        fwd_e[i], fwd_g[i] = e, g
        a = decay(i)
        e = a * e + recv1[i, :piece, :]
        g = g * a
    bwd_e, bwd_g = [None] * width, [None] * width
    f = jnp.zeros((piece, recv1.shape[2]), jnp.float32)
    h = jnp.ones((1, recv1.shape[2]), jnp.float32)
    for i in reversed(range(width)):
        bwd_e[i], bwd_g[i] = f, h
        a = decay(i)
        f = a * f + recv1[i, piece:2 * piece, :]
        h = h * a
    win[0, 0, :piece, :] = e
    win[0, 0, piece:, :] = jnp.broadcast_to(g, (win.shape[2] - piece, g.shape[1]))
    win[1, 0, :piece, :] = f
    win[1, 0, piece:, :] = jnp.broadcast_to(h, (win.shape[2] - piece, h.shape[1]))

    def copy2(way, r, target):
        src = win.at[way, 0] if r == 0 else win.at[way, r]
        return pltpu.make_async_remote_copy(
            src_ref=src, dst_ref=win.at[way, len(steps) + 1 + r],
            send_sem=send2.at[way, r], recv_sem=rsem2.at[way, r],
            device_id=(target, col), device_id_type=MESH)

    base = len(steps) + 1
    for r, d in enumerate(steps):
        for way, sign in ((0, 1), (1, -1)):
            target_row = y + sign * d

            @pl.when(jnp.logical_and(target_row >= 0, target_row < rows_n))
            def _():
                copy2(way, r, me + sign * d * width).start()
        heads(1 if r < len(steps) - 1 else len(heads_left))
        for way, sign in ((0, 1), (1, -1)):
            source_row = y - sign * d
            got = jnp.logical_and(source_row >= 0, source_row < rows_n)
            cur = 0 if r == 0 else r
            nxt = r + 1

            @pl.when(got)
            def _():
                copy2(way, r, me - sign * d * width).wait_recv()
                arrived = win[way, base + r]
                if r == 0:
                    win[way, nxt] = arrived
                else:
                    a = win[way, cur, piece:, :]
                    win[way, nxt, :piece, :] = win[way, cur, :piece, :] + jnp.broadcast_to(
                        a[:1], (piece, a.shape[1])) * arrived[:piece]
                    win[way, nxt, piece:, :] = a * arrived[piece:]

            @pl.when(jnp.logical_not(got))
            def _():
                if r == 0:
                    win[way, nxt] = jnp.zeros(win.shape[2:], win.dtype)
                else:
                    win[way, nxt] = win[way, cur]
    for r, d in enumerate(steps):
        for way, sign in ((0, 1), (1, -1)):
            target_row = y + sign * d

            @pl.when(jnp.logical_and(target_row >= 0, target_row < rows_n))
            def _():
                copy2(way, r, me + sign * d * width).wait_send()
    last = len(steps)
    entering = win[0, last, :piece, :]
    leaving = win[1, last, :piece, :]

    for i in range(width):
        out3[i, :piece, :] = fwd_e[i] + fwd_g[i] * entering
        out3[i, piece:, :] = bwd_e[i] + bwd_g[i] * leaving
    own = pltpu.make_async_copy(out3.at[c], recv3.at[c], local.at[1])
    own.start()
    sends = []
    for off in range(1, width):
        k = (c + off) % width
        cp = pltpu.make_async_remote_copy(
            src_ref=out3.at[k], dst_ref=recv3.at[c], send_sem=send3.at[off],
            recv_sem=rsem3.at[off], device_id=(y * width + k, col), device_id_type=MESH)
        cp.start()
        sends.append(cp)
    for off in range(1, width):
        k = (c + width - off) % width
        pltpu.make_async_remote_copy(
            src_ref=out3.at[k], dst_ref=recv3.at[k], send_sem=send3.at[off],
            recv_sem=rsem3.at[off], device_id=(y * width + k, col), device_id_type=MESH).wait_recv()
    own.wait()
    for cp in sends:
        cp.wait_send()

    s = width * piece
    for k in range(width):
        full[0, k * piece:(k + 1) * piece, :] = recv3[k, :piece, :]
        full[1, k * piece:(k + 1) * piece, :] = recv3[k, piece:, :]
    weighted = run_ref[...].astype(jnp.bfloat16)
    part_b = jnp.dot(weighted, c_ref[...], preferred_element_type=jnp.float32) + nt_dot_f32(
        xs_ref[...], full[1])
    part_c = lax.dot_general(
        weighted, b_ref[...], (((0,), (0,)), ((), ())), preferred_element_type=jnp.float32
    ) + nt_dot_f32(ds_ref[...], full[0])
    n_rows = part_b.shape[0]
    parts[:n_rows, :] = part_b.astype(parts.dtype)
    parts[n_rows:, :] = part_c.astype(parts.dtype)
    rows = gather1.shape[1]

    def chunk(i):
        return parts.at[pl.ds(pl.multiple_of(i * rows, rows), rows)]

    sends = []
    for k in range(1, groups):
        peer = (z + k) % groups
        cp = pltpu.make_async_remote_copy(
            src_ref=chunk(peer), dst_ref=gather1.at[z], send_sem=hsend1.at[k],
            recv_sem=hrecv1.at[k], device_id=(me, peer), device_id_type=MESH)
        cp.start()
        sends.append(cp)
    adj = full[1]
    adj_hi = adj.astype(jnp.bfloat16)
    adj_lo = (adj - adj_hi.astype(jnp.float32)).astype(jnp.bfloat16)
    b_adj = jnp.dot(b_ref[...], adj_hi, preferred_element_type=jnp.float32) + jnp.dot(
        b_ref[...], adj_lo, preferred_element_type=jnp.float32)
    for h in range(cr_ref.shape[0]):
        lanes = slice(h * hd, (h + 1) * hd)
        gv_ref[:, lanes] = (dx_ref[:, lanes] + ie_ref[:, h:h + 1] * b_adj[:, lanes]).astype(
            gv_ref.dtype)
    total = parts[pl.ds(pl.multiple_of(z * rows, rows), rows), :].astype(jnp.float32)
    for k in range(1, groups):
        source = (z + groups - k) % groups
        pltpu.make_async_remote_copy(
            src_ref=chunk(source), dst_ref=gather1.at[source], send_sem=hsend1.at[k],
            recv_sem=hrecv1.at[k], device_id=(me, source), device_id_type=MESH).wait_recv()
        total = total + gather1[source].astype(jnp.float32)
    for cp in sends:
        cp.wait_send()
    gather2[z] = total.astype(gather2.dtype)
    sends = []
    for k in range(1, groups):
        peer = (z + k) % groups
        cp = pltpu.make_async_remote_copy(
            src_ref=gather2.at[z], dst_ref=gather2.at[z], send_sem=hsend2.at[k],
            recv_sem=hrecv2.at[k], device_id=(me, peer), device_id_type=MESH)
        cp.start()
        sends.append(cp)
    for k in range(1, groups):
        source = (z + groups - k) % groups
        pltpu.make_async_remote_copy(
            src_ref=gather2.at[source], dst_ref=gather2.at[source], send_sem=hsend2.at[k],
            recv_sem=hrecv2.at[k], device_id=(me, source), device_id_type=MESH).wait_recv()
    for cp in sends:
        cp.wait_send()
    sum_ref[...] = gather2[...]


def exclusive_scans(count, groups, decay_cols, forward, backward, x, dy, scores_t, cumulative,
                    into_end, from_start, b_inputs, c_inputs):
    s, w = forward.shape
    width = 8 if count % 8 == 0 else 1
    rows_n = count // width
    piece = s // width
    rounds = len(scan_steps(rows_n))
    pack = jnp.concatenate(
        [
            forward.reshape(width, piece, w),
            backward.reshape(width, piece, w),
            jnp.broadcast_to(decay_cols[None], (width, 8, w)),
        ],
        axis=1,
    )
    length = scores_t.shape[0]
    chunk_rows = 2 * length // groups
    grad_values, sums = pl.pallas_call(
        functools.partial(scan_kernel, rows_n, width, groups),
        out_shape=(
            jax.ShapeDtypeStruct(x.shape, jnp.bfloat16),
            jax.ShapeDtypeStruct((groups, chunk_rows, s), jnp.bfloat16),
        ),
        in_specs=[pl.BlockSpec(memory_space=pltpu.VMEM)] * 10,
        out_specs=(pl.BlockSpec(memory_space=pltpu.VMEM),) * 2,
        scratch_shapes=[
            pltpu.VMEM((length, length), jnp.float32),
            pltpu.VMEM(x.shape, jnp.float32),
            pltpu.VMEM(x.shape, jnp.float32),
            pltpu.VMEM(x.shape, jnp.float32),
            pltpu.VMEM((width, 2 * piece + 8, w), jnp.float32),
            pltpu.VMEM((2, 2 * rounds + 1, piece + 8, w), jnp.float32),
            pltpu.VMEM((width, 2 * piece, w), jnp.float32),
            pltpu.VMEM((width, 2 * piece, w), jnp.float32),
            pltpu.VMEM((2, s, w), jnp.float32),
            pltpu.VMEM((2 * length, s), jnp.bfloat16),
            pltpu.VMEM((groups, chunk_rows, s), jnp.bfloat16),
            pltpu.VMEM((groups, chunk_rows, s), jnp.bfloat16),
            pltpu.SemaphoreType.DMA((width,)),
            pltpu.SemaphoreType.DMA((width,)),
            pltpu.SemaphoreType.DMA((2, rounds)),
            pltpu.SemaphoreType.DMA((2, rounds)),
            pltpu.SemaphoreType.DMA((width,)),
            pltpu.SemaphoreType.DMA((width,)),
            pltpu.SemaphoreType.DMA((2,)),
            pltpu.SemaphoreType.DMA((groups,)),
            pltpu.SemaphoreType.DMA((groups,)),
            pltpu.SemaphoreType.DMA((groups,)),
            pltpu.SemaphoreType.DMA((groups,)),
        ],
        compiler_params=pltpu.CompilerParams(collective_id=1, has_side_effects=True),
    )(pack, x, dy, scores_t, cumulative, cumulative.T, into_end.T, from_start.T, b_inputs, c_inputs)
    sums = sums.reshape(2 * length, s)
    return grad_values, sums[:length], sums[length:]


def shards(count, groups, token_values, b_inputs, c_inputs, log_decay, grad_out):
    length = token_values.shape[0]
    heads_here = log_decay.shape[0]
    head_dim = token_values.shape[1] // heads_here
    state_size = b_inputs.shape[1]
    positions = lax.iota(jnp.int32, length)
    upto = (positions[:, None] <= positions[None, :]).astype(jnp.float32)
    cumulative = jnp.dot(log_decay, upto, precision=PRECISE)
    block_log = cumulative[:, -1]
    into_end = jnp.exp(block_log[:, None] - cumulative)
    from_start = jnp.exp(cumulative)
    block_decay = jnp.exp(block_log)
    b_float = b_inputs.astype(jnp.float32)
    c_float = c_inputs.astype(jnp.float32)
    decayed_b = (into_end[:, :, None] * b_float[None]).astype(jnp.bfloat16)
    decayed_c = (from_start[:, :, None] * c_float[None]).astype(jnp.bfloat16)
    x_heads = token_values.reshape(length, heads_here, head_dim)
    dy_heads = grad_out.reshape(length, heads_here, head_dim)
    state_local = jnp.einsum(
        "htn,thp->nhp", decayed_b, x_heads, preferred_element_type=jnp.float32
    ).reshape(state_size, heads_here * head_dim)
    adjoint_local = jnp.einsum(
        "hsn,shp->nhp", decayed_c, dy_heads, preferred_element_type=jnp.float32
    ).reshape(state_size, heads_here * head_dim)
    decay_cols = jnp.repeat(block_decay, head_dim)[None, :]
    scores_t = lax.dot_general(
        b_inputs, c_inputs, (((1,), (1,)), ((), ())), preferred_element_type=jnp.float32
    )
    grad_values, grad_b, grad_c = exclusive_scans(
        count, groups, decay_cols, state_local, adjoint_local, token_values, grad_out, scores_t,
        cumulative, into_end, from_start, b_inputs, c_inputs,
    )
    return grad_values, grad_b, grad_c


def solution(mesh):
    in_specs = (
        P("seq", "head"),
        P("seq", None),
        P("seq", None),
        P("head", "seq"),
        P("seq", "head"),
    )
    out_specs = (P("seq", "head"), P("seq", None), P("seq", None))
    body = functools.partial(shards, mesh.shape["seq"], mesh.shape["head"])
    return jax.shard_map(body, mesh=mesh, in_specs=in_specs, out_specs=out_specs, check_vma=False)
```

```python
import functools

import jax
import jax.numpy as jnp
from jax import lax
from jax.experimental import pallas as pl
from jax.experimental.pallas import tpu as pltpu
from jax.sharding import PartitionSpec as P

PRECISE = lax.Precision.HIGHEST
MESH = pl.DeviceIdType.MESH


def scan_steps(n):
    steps, d = [1], 1
    while d < n:
        steps.append(d)
        d *= 2
    return steps


def nt_dot(p, q):
    return lax.dot_general(p, q, (((1,), (1,)), ((), ())), preferred_element_type=jnp.float32)


def nt_dot_f32(p, q):
    ph = p.astype(jnp.bfloat16)
    pl_ = (p - ph.astype(jnp.float32)).astype(jnp.bfloat16)
    qh = q.astype(jnp.bfloat16)
    ql = (q - qh.astype(jnp.float32)).astype(jnp.bfloat16)
    return nt_dot(ph, qh) + (nt_dot(ph, ql) + nt_dot(pl_, qh))


def scan_kernel(rows_n, width, groups, pack_ref, pdec_ref, x_ref, dy_ref, sc_ref, cr_ref, cc_ref, ie_ref,
                fs_ref, b_ref, c_ref, gv_ref, sum_ref, run_ref, dx_ref, xs_ref, ds_ref, recv1, rdec,
                win, out3, recv3, full, parts, gather1, gather2, send1, rsem1, send2, rsem2, send3, rsem3,
                local, dsend, drecv, hsend1, hrecv1, hsend2, hrecv2):
    me = lax.axis_index("seq")
    col = lax.axis_index("head")
    c = me % width
    y = me // width
    piece = recv1.shape[1] // 2
    steps = scan_steps(rows_n)
    spans = sorted(set(steps))

    length = sc_ref.shape[0]
    later = lax.broadcasted_iota(jnp.int32, (length, length), 1) >= lax.broadcasted_iota(
        jnp.int32, (length, length), 0)
    run_ref[...] = jnp.zeros(run_ref.shape, run_ref.dtype)

    def head(h):
        gaps = cr_ref[h:h + 1, :] - cc_ref[:, h:h + 1]
        dec = jnp.where(later, jnp.exp(jnp.where(later, gaps, 0.0)), 0.0)
        mix = (sc_ref[...] * dec).astype(jnp.bfloat16)
        lanes = slice(h * hd, (h + 1) * hd)
        dy_h = dy_ref[:, lanes]
        x_h = x_ref[:, lanes]
        xs_ref[:, lanes] = x_h.astype(jnp.float32) * ie_ref[:, h:h + 1]
        ds_ref[:, lanes] = dy_h.astype(jnp.float32) * fs_ref[:, h:h + 1]
        dx_ref[:, lanes] = jnp.dot(mix, dy_h, preferred_element_type=jnp.float32)
        pairs = lax.dot_general(
            x_h, dy_h, (((1,), (1,)), ((), ())), preferred_element_type=jnp.float32)
        run_ref[...] += dec * pairs

    heads_left = list(range(cr_ref.shape[0]))
    hd = x_ref.shape[1] // cr_ref.shape[0]

    def heads(k):
        for _ in range(k):
            if heads_left:
                head(heads_left.pop(0))

    barrier = pltpu.get_barrier_semaphore()
    for off in range(1, width):
        peer = y * width + (c + off) % width
        pl.semaphore_signal(barrier, inc=1, device_id=(peer, col), device_id_type=MESH)
    for d in spans:
        @pl.when(y + d < rows_n)
        def _():
            pl.semaphore_signal(barrier, inc=1, device_id=(me + d * width, col), device_id_type=MESH)

        @pl.when(y - d >= 0)
        def _():
            pl.semaphore_signal(barrier, inc=1, device_id=(me - d * width, col), device_id_type=MESH)
    z = lax.axis_index("head")
    for off in range(1, groups):
        pl.semaphore_signal(
            barrier, inc=1, device_id=(me, (z + off) % groups), device_id_type=MESH)
    peers = width - 1 + groups - 1
    for d in spans:
        peers = peers + ((rows_n - 1 - y) // d + rows_n - 1) // rows_n + (y // d + rows_n - 1) // rows_n
    heads(1)
    pl.semaphore_wait(barrier, peers)

    own = pltpu.make_async_copy(pack_ref.at[c], recv1.at[c], local.at[0])
    own.start()
    own_dec = pltpu.make_async_copy(pdec_ref, rdec.at[c], local.at[2])
    own_dec.start()
    sends = []
    for off in range(1, width):
        k = (c + off) % width
        cp = pltpu.make_async_remote_copy(
            src_ref=pack_ref.at[k], dst_ref=recv1.at[c], send_sem=send1.at[off],
            recv_sem=rsem1.at[off], device_id=(y * width + k, col), device_id_type=MESH)
        cp.start()
        sends.append(cp)
        cp = pltpu.make_async_remote_copy(
            src_ref=pdec_ref, dst_ref=rdec.at[c], send_sem=dsend.at[off],
            recv_sem=drecv.at[off], device_id=(y * width + k, col), device_id_type=MESH)
        cp.start()
        sends.append(cp)
    heads(3)
    for off in range(1, width):
        k = (c + width - off) % width
        pltpu.make_async_remote_copy(
            src_ref=pack_ref.at[k], dst_ref=recv1.at[k], send_sem=send1.at[off],
            recv_sem=rsem1.at[off], device_id=(y * width + k, col), device_id_type=MESH).wait_recv()
        pltpu.make_async_remote_copy(
            src_ref=pdec_ref, dst_ref=rdec.at[k], send_sem=dsend.at[off],
            recv_sem=drecv.at[off], device_id=(y * width + k, col), device_id_type=MESH).wait_recv()
    own.wait()
    own_dec.wait()
    for cp in sends:
        cp.wait_send()

    def decay(i):
        return rdec[i, 0:1, :]

    fwd_e, fwd_g = [None] * width, [None] * width
    e = jnp.zeros((piece, recv1.shape[2]), jnp.float32)
    g = jnp.ones((1, recv1.shape[2]), jnp.float32)
    for i in range(width):
        fwd_e[i], fwd_g[i] = e, g
        a = decay(i)
        e = a * e + recv1[i, :piece, :].astype(jnp.float32)
        g = g * a
    bwd_e, bwd_g = [None] * width, [None] * width
    f = jnp.zeros((piece, recv1.shape[2]), jnp.float32)
    h = jnp.ones((1, recv1.shape[2]), jnp.float32)
    for i in reversed(range(width)):
        bwd_e[i], bwd_g[i] = f, h
        a = decay(i)
        f = a * f + recv1[i, piece:2 * piece, :].astype(jnp.float32)
        h = h * a
    win[0, 0, :piece, :] = e
    win[0, 0, piece:, :] = jnp.broadcast_to(g, (win.shape[2] - piece, g.shape[1]))
    win[1, 0, :piece, :] = f
    win[1, 0, piece:, :] = jnp.broadcast_to(h, (win.shape[2] - piece, h.shape[1]))

    def copy2(way, r, target):
        src = win.at[way, 0] if r == 0 else win.at[way, r]
        return pltpu.make_async_remote_copy(
            src_ref=src, dst_ref=win.at[way, len(steps) + 1 + r],
            send_sem=send2.at[way, r], recv_sem=rsem2.at[way, r],
            device_id=(target, col), device_id_type=MESH)

    base = len(steps) + 1
    for r, d in enumerate(steps):
        for way, sign in ((0, 1), (1, -1)):
            target_row = y + sign * d

            @pl.when(jnp.logical_and(target_row >= 0, target_row < rows_n))
            def _():
                copy2(way, r, me + sign * d * width).start()
        heads(1 if r < len(steps) - 1 else len(heads_left))
        for way, sign in ((0, 1), (1, -1)):
            source_row = y - sign * d
            got = jnp.logical_and(source_row >= 0, source_row < rows_n)
            cur = 0 if r == 0 else r
            nxt = r + 1

            @pl.when(got)
            def _():
                copy2(way, r, me - sign * d * width).wait_recv()
                arrived = win[way, base + r]
                if r == 0:
                    win[way, nxt] = arrived
                else:
                    a = win[way, cur, piece:, :]
                    win[way, nxt, :piece, :] = win[way, cur, :piece, :] + jnp.broadcast_to(
                        a[:1], (piece, a.shape[1])) * arrived[:piece]
                    win[way, nxt, piece:, :] = a * arrived[piece:]

            @pl.when(jnp.logical_not(got))
            def _():
                if r == 0:
                    win[way, nxt] = jnp.zeros(win.shape[2:], win.dtype)
                else:
                    win[way, nxt] = win[way, cur]
    for r, d in enumerate(steps):
        for way, sign in ((0, 1), (1, -1)):
            target_row = y + sign * d

            @pl.when(jnp.logical_and(target_row >= 0, target_row < rows_n))
            def _():
                copy2(way, r, me + sign * d * width).wait_send()
    last = len(steps)
    entering = win[0, last, :piece, :]
    leaving = win[1, last, :piece, :]

    for i in range(width):
        out3[i, :piece, :] = (fwd_e[i] + fwd_g[i] * entering).astype(out3.dtype)
        out3[i, piece:, :] = (bwd_e[i] + bwd_g[i] * leaving).astype(out3.dtype)
    own = pltpu.make_async_copy(out3.at[c], recv3.at[c], local.at[1])
    own.start()
    sends = []
    for off in range(1, width):
        k = (c + off) % width
        cp = pltpu.make_async_remote_copy(
            src_ref=out3.at[k], dst_ref=recv3.at[c], send_sem=send3.at[off],
            recv_sem=rsem3.at[off], device_id=(y * width + k, col), device_id_type=MESH)
        cp.start()
        sends.append(cp)
    for off in range(1, width):
        k = (c + width - off) % width
        pltpu.make_async_remote_copy(
            src_ref=out3.at[k], dst_ref=recv3.at[k], send_sem=send3.at[off],
            recv_sem=rsem3.at[off], device_id=(y * width + k, col), device_id_type=MESH).wait_recv()
    own.wait()
    for cp in sends:
        cp.wait_send()

    s = width * piece
    for k in range(width):
        full[0, k * piece:(k + 1) * piece, :] = recv3[k, :piece, :].astype(jnp.float32)
        full[1, k * piece:(k + 1) * piece, :] = recv3[k, piece:, :].astype(jnp.float32)
    weighted = run_ref[...].astype(jnp.bfloat16)
    part_b = jnp.dot(weighted, c_ref[...], preferred_element_type=jnp.float32) + nt_dot_f32(
        xs_ref[...], full[1])
    part_c = lax.dot_general(
        weighted, b_ref[...], (((0,), (0,)), ((), ())), preferred_element_type=jnp.float32
    ) + nt_dot_f32(ds_ref[...], full[0])
    n_rows = part_b.shape[0]
    parts[:n_rows, :] = part_b.astype(parts.dtype)
    parts[n_rows:, :] = part_c.astype(parts.dtype)
    rows = gather1.shape[1]

    def chunk(i):
        return parts.at[pl.ds(pl.multiple_of(i * rows, rows), rows)]

    sends = []
    for k in range(1, groups):
        peer = (z + k) % groups
        cp = pltpu.make_async_remote_copy(
            src_ref=chunk(peer), dst_ref=gather1.at[z], send_sem=hsend1.at[k],
            recv_sem=hrecv1.at[k], device_id=(me, peer), device_id_type=MESH)
        cp.start()
        sends.append(cp)
    adj = full[1]
    adj_hi = adj.astype(jnp.bfloat16)
    adj_lo = (adj - adj_hi.astype(jnp.float32)).astype(jnp.bfloat16)
    b_adj = jnp.dot(b_ref[...], adj_hi, preferred_element_type=jnp.float32) + jnp.dot(
        b_ref[...], adj_lo, preferred_element_type=jnp.float32)
    for h in range(cr_ref.shape[0]):
        lanes = slice(h * hd, (h + 1) * hd)
        gv_ref[:, lanes] = (dx_ref[:, lanes] + ie_ref[:, h:h + 1] * b_adj[:, lanes]).astype(
            gv_ref.dtype)
    total = parts[pl.ds(pl.multiple_of(z * rows, rows), rows), :].astype(jnp.float32)
    for k in range(1, groups):
        source = (z + groups - k) % groups
        pltpu.make_async_remote_copy(
            src_ref=chunk(source), dst_ref=gather1.at[source], send_sem=hsend1.at[k],
            recv_sem=hrecv1.at[k], device_id=(me, source), device_id_type=MESH).wait_recv()
        total = total + gather1[source].astype(jnp.float32)
    for cp in sends:
        cp.wait_send()
    gather2[z] = total.astype(gather2.dtype)
    sends = []
    for k in range(1, groups):
        peer = (z + k) % groups
        cp = pltpu.make_async_remote_copy(
            src_ref=gather2.at[z], dst_ref=gather2.at[z], send_sem=hsend2.at[k],
            recv_sem=hrecv2.at[k], device_id=(me, peer), device_id_type=MESH)
        cp.start()
        sends.append(cp)
    for k in range(1, groups):
        source = (z + groups - k) % groups
        pltpu.make_async_remote_copy(
            src_ref=gather2.at[source], dst_ref=gather2.at[source], send_sem=hsend2.at[k],
            recv_sem=hrecv2.at[k], device_id=(me, source), device_id_type=MESH).wait_recv()
    for cp in sends:
        cp.wait_send()
    sum_ref[...] = gather2[...]


def exclusive_scans(count, groups, decay_cols, forward, backward, x, dy, scores_t, cumulative,
                    into_end, from_start, b_inputs, c_inputs):
    s, w = forward.shape
    width = 8 if count % 8 == 0 else 1
    rows_n = count // width
    piece = s // width
    rounds = len(scan_steps(rows_n))
    pack = jnp.concatenate(
        [forward.reshape(width, piece, w), backward.reshape(width, piece, w)], axis=1
    ).astype(jnp.bfloat16)
    decay_rows = jnp.broadcast_to(decay_cols, (8, w))
    length = scores_t.shape[0]
    chunk_rows = 2 * length // groups
    grad_values, sums = pl.pallas_call(
        functools.partial(scan_kernel, rows_n, width, groups),
        out_shape=(
            jax.ShapeDtypeStruct(x.shape, jnp.bfloat16),
            jax.ShapeDtypeStruct((groups, chunk_rows, s), jnp.bfloat16),
        ),
        in_specs=[pl.BlockSpec(memory_space=pltpu.VMEM)] * 11,
        out_specs=(pl.BlockSpec(memory_space=pltpu.VMEM),) * 2,
        scratch_shapes=[
            pltpu.VMEM((length, length), jnp.float32),
            pltpu.VMEM(x.shape, jnp.float32),
            pltpu.VMEM(x.shape, jnp.float32),
            pltpu.VMEM(x.shape, jnp.float32),
            pltpu.VMEM((width, 2 * piece, w), jnp.bfloat16),
            pltpu.VMEM((width, 8, w), jnp.float32),
            pltpu.VMEM((2, 2 * rounds + 1, piece + 8, w), jnp.float32),
            pltpu.VMEM((width, 2 * piece, w), jnp.bfloat16),
            pltpu.VMEM((width, 2 * piece, w), jnp.bfloat16),
            pltpu.VMEM((2, s, w), jnp.float32),
            pltpu.VMEM((2 * length, s), jnp.bfloat16),
            pltpu.VMEM((groups, chunk_rows, s), jnp.bfloat16),
            pltpu.VMEM((groups, chunk_rows, s), jnp.bfloat16),
            pltpu.SemaphoreType.DMA((width,)),
            pltpu.SemaphoreType.DMA((width,)),
            pltpu.SemaphoreType.DMA((2, rounds)),
            pltpu.SemaphoreType.DMA((2, rounds)),
            pltpu.SemaphoreType.DMA((width,)),
            pltpu.SemaphoreType.DMA((width,)),
            pltpu.SemaphoreType.DMA((3,)),
            pltpu.SemaphoreType.DMA((width,)),
            pltpu.SemaphoreType.DMA((width,)),
            pltpu.SemaphoreType.DMA((groups,)),
            pltpu.SemaphoreType.DMA((groups,)),
            pltpu.SemaphoreType.DMA((groups,)),
            pltpu.SemaphoreType.DMA((groups,)),
        ],
        compiler_params=pltpu.CompilerParams(collective_id=1, has_side_effects=True),
    )(pack, decay_rows, x, dy, scores_t, cumulative, cumulative.T, into_end.T, from_start.T, b_inputs, c_inputs)
    sums = sums.reshape(2 * length, s)
    return grad_values, sums[:length], sums[length:]


def shards(count, groups, token_values, b_inputs, c_inputs, log_decay, grad_out):
    length = token_values.shape[0]
    heads_here = log_decay.shape[0]
    head_dim = token_values.shape[1] // heads_here
    state_size = b_inputs.shape[1]
    positions = lax.iota(jnp.int32, length)
    upto = (positions[:, None] <= positions[None, :]).astype(jnp.float32)
    cumulative = jnp.dot(log_decay, upto, precision=PRECISE)
    block_log = cumulative[:, -1]
    into_end = jnp.exp(block_log[:, None] - cumulative)
    from_start = jnp.exp(cumulative)
    block_decay = jnp.exp(block_log)
    b_float = b_inputs.astype(jnp.float32)
    c_float = c_inputs.astype(jnp.float32)
    decayed_b = (into_end[:, :, None] * b_float[None]).astype(jnp.bfloat16)
    decayed_c = (from_start[:, :, None] * c_float[None]).astype(jnp.bfloat16)
    x_heads = token_values.reshape(length, heads_here, head_dim)
    dy_heads = grad_out.reshape(length, heads_here, head_dim)
    state_local = jnp.einsum(
        "htn,thp->nhp", decayed_b, x_heads, preferred_element_type=jnp.float32
    ).reshape(state_size, heads_here * head_dim)
    adjoint_local = jnp.einsum(
        "hsn,shp->nhp", decayed_c, dy_heads, preferred_element_type=jnp.float32
    ).reshape(state_size, heads_here * head_dim)
    decay_cols = jnp.repeat(block_decay, head_dim)[None, :]
    scores_t = lax.dot_general(
        b_inputs, c_inputs, (((1,), (1,)), ((), ())), preferred_element_type=jnp.float32
    )
    grad_values, grad_b, grad_c = exclusive_scans(
        count, groups, decay_cols, state_local, adjoint_local, token_values, grad_out, scores_t,
        cumulative, into_end, from_start, b_inputs, c_inputs,
    )
    return grad_values, grad_b, grad_c


def solution(mesh):
    in_specs = (
        P("seq", "head"),
        P("seq", None),
        P("seq", None),
        P("head", "seq"),
        P("seq", "head"),
    )
    out_specs = (P("seq", "head"), P("seq", None), P("seq", None))
    body = functools.partial(shards, mesh.shape["seq"], mesh.shape["head"])
    return jax.shard_map(body, mesh=mesh, in_specs=in_specs, out_specs=out_specs, check_vma=False)
```

```python
import functools

import jax
import jax.numpy as jnp
from jax import lax
from jax.experimental import pallas as pl
from jax.experimental.pallas import tpu as pltpu
from jax.sharding import PartitionSpec as P

PRECISE = lax.Precision.HIGHEST
MESH = pl.DeviceIdType.MESH


def nt_dot(p, q):
    return lax.dot_general(p, q, (((1,), (1,)), ((), ())), preferred_element_type=jnp.float32)


def nt_dot_f32(p, q):
    ph = p.astype(jnp.bfloat16)
    pl_ = (p - ph.astype(jnp.float32)).astype(jnp.bfloat16)
    qh = q.astype(jnp.bfloat16)
    ql = (q - qh.astype(jnp.float32)).astype(jnp.bfloat16)
    return nt_dot(ph, qh) + (nt_dot(ph, ql) + nt_dot(pl_, qh))


def scan_kernel(rows_n, width, groups, pack_ref, pdec_ref, x_ref, dy_ref, sc_ref, cr_ref, cc_ref, ie_ref,
                fs_ref, b_ref, c_ref, gv_ref, sum_ref, run_ref, dx_ref, xs_ref, ds_ref, recv1, rdec,
                win, out3, recv3, full, parts, gather1, gather2, send1, rsem1, send2, rsem2, send3, rsem3,
                local, dsend, drecv, hsend1, hrecv1, hsend2, hrecv2):
    me = lax.axis_index("seq")
    col = lax.axis_index("head")
    c = me % width
    y = me // width
    piece = recv1.shape[1] // 2
    spans = [1, 2, 3, 4]

    length = sc_ref.shape[0]
    later = lax.broadcasted_iota(jnp.int32, (length, length), 1) >= lax.broadcasted_iota(
        jnp.int32, (length, length), 0)
    run_ref[...] = jnp.zeros(run_ref.shape, run_ref.dtype)

    def head(h):
        gaps = cr_ref[h:h + 1, :] - cc_ref[:, h:h + 1]
        dec = jnp.where(later, jnp.exp(jnp.where(later, gaps, 0.0)), 0.0)
        mix = (sc_ref[...] * dec).astype(jnp.bfloat16)
        lanes = slice(h * hd, (h + 1) * hd)
        dy_h = dy_ref[:, lanes]
        x_h = x_ref[:, lanes]
        xs_ref[:, lanes] = x_h.astype(jnp.float32) * ie_ref[:, h:h + 1]
        ds_ref[:, lanes] = dy_h.astype(jnp.float32) * fs_ref[:, h:h + 1]
        dx_ref[:, lanes] = jnp.dot(mix, dy_h, preferred_element_type=jnp.float32)
        pairs = lax.dot_general(
            x_h, dy_h, (((1,), (1,)), ((), ())), preferred_element_type=jnp.float32)
        run_ref[...] += dec * pairs

    heads_left = list(range(cr_ref.shape[0]))
    hd = x_ref.shape[1] // cr_ref.shape[0]

    def heads(k):
        for _ in range(k):
            if heads_left:
                head(heads_left.pop(0))

    barrier = pltpu.get_barrier_semaphore()
    for off in range(1, width):
        peer = y * width + (c + off) % width
        pl.semaphore_signal(barrier, inc=1, device_id=(peer, col), device_id_type=MESH)
    for d in spans:
        @pl.when(y + d < rows_n)
        def _():
            pl.semaphore_signal(barrier, inc=1, device_id=(me + d * width, col), device_id_type=MESH)

        @pl.when(y - d >= 0)
        def _():
            pl.semaphore_signal(barrier, inc=1, device_id=(me - d * width, col), device_id_type=MESH)
    z = lax.axis_index("head")
    for off in range(1, groups):
        pl.semaphore_signal(
            barrier, inc=1, device_id=(me, (z + off) % groups), device_id_type=MESH)
    peers = width - 1 + groups - 1
    for d in spans:
        peers = peers + ((rows_n - 1 - y) // d + rows_n - 1) // rows_n + (y // d + rows_n - 1) // rows_n
    heads(1)
    pl.semaphore_wait(barrier, peers)

    own = pltpu.make_async_copy(pack_ref.at[c], recv1.at[c], local.at[0])
    own.start()
    own_dec = pltpu.make_async_copy(pdec_ref, rdec.at[c], local.at[2])
    own_dec.start()
    sends = []
    for off in range(1, width):
        k = (c + off) % width
        cp = pltpu.make_async_remote_copy(
            src_ref=pack_ref.at[k], dst_ref=recv1.at[c], send_sem=send1.at[off],
            recv_sem=rsem1.at[off], device_id=(y * width + k, col), device_id_type=MESH)
        cp.start()
        sends.append(cp)
        cp = pltpu.make_async_remote_copy(
            src_ref=pdec_ref, dst_ref=rdec.at[c], send_sem=dsend.at[off],
            recv_sem=drecv.at[off], device_id=(y * width + k, col), device_id_type=MESH)
        cp.start()
        sends.append(cp)
    heads(3)
    for off in range(1, width):
        k = (c + width - off) % width
        pltpu.make_async_remote_copy(
            src_ref=pack_ref.at[k], dst_ref=recv1.at[k], send_sem=send1.at[off],
            recv_sem=rsem1.at[off], device_id=(y * width + k, col), device_id_type=MESH).wait_recv()
        pltpu.make_async_remote_copy(
            src_ref=pdec_ref, dst_ref=rdec.at[k], send_sem=dsend.at[off],
            recv_sem=drecv.at[off], device_id=(y * width + k, col), device_id_type=MESH).wait_recv()
    own.wait()
    own_dec.wait()
    for cp in sends:
        cp.wait_send()

    def decay(i):
        return rdec[i, 0:1, :]

    fwd_e, fwd_g = [None] * width, [None] * width
    e = jnp.zeros((piece, recv1.shape[2]), jnp.float32)
    g = jnp.ones((1, recv1.shape[2]), jnp.float32)
    for i in range(width):
        fwd_e[i], fwd_g[i] = e, g
        a = decay(i)
        e = a * e + recv1[i, :piece, :].astype(jnp.float32)
        g = g * a
    bwd_e, bwd_g = [None] * width, [None] * width
    f = jnp.zeros((piece, recv1.shape[2]), jnp.float32)
    h = jnp.ones((1, recv1.shape[2]), jnp.float32)
    for i in reversed(range(width)):
        bwd_e[i], bwd_g[i] = f, h
        a = decay(i)
        f = a * f + recv1[i, piece:2 * piece, :].astype(jnp.float32)
        h = h * a
    win[0, 0, :piece, :] = e
    win[0, 0, piece:, :] = jnp.broadcast_to(g, (win.shape[2] - piece, g.shape[1]))
    win[1, 0, :piece, :] = f
    win[1, 0, piece:, :] = jnp.broadcast_to(h, (win.shape[2] - piece, h.shape[1]))

    def combine(w_near, w_far):
        a = w_near[piece:, :]
        return w_near[:piece, :] + jnp.broadcast_to(a[:1], (piece, a.shape[1])) * w_far[:piece, :], a * w_far[piece:, :]

    def copy2(way, slot, src_slot, target, sem):
        return pltpu.make_async_remote_copy(
            src_ref=win.at[way, src_slot], dst_ref=win.at[way, slot], send_sem=send2.at[way, sem],
            recv_sem=rsem2.at[way, sem], device_id=(target, col), device_id_type=MESH)

    def exists(row):
        return jnp.logical_and(row >= 0, row < rows_n)

    near = [1, 2, 3]
    for way, sign in ((0, 1), (1, -1)):
        for k in near:
            @pl.when(exists(y + sign * k))
            def _():
                copy2(way, k, 0, me + sign * k * width, k - 1).start()
    heads(2)
    for way, sign in ((0, 1), (1, -1)):
        win[way, 4] = jnp.zeros(win.shape[2:], win.dtype)
        for k in near:
            @pl.when(exists(y - sign * k))
            def _():
                copy2(way, k, 0, me - sign * k * width, k - 1).wait_recv()
                s_new, a_new = combine(win[way, 4], win[way, k])
                if k == 1:
                    win[way, 4] = win[way, 1]
                else:
                    win[way, 4, :piece, :] = s_new
                    win[way, 4, piece:, :] = a_new
        s_inc, a_inc = combine(win[way, 0], win[way, 4])
        win[way, 5, :piece, :] = s_inc
        win[way, 5, piece:, :] = a_inc

        @pl.when(exists(y + sign * 4))
        def _():
            copy2(way, 6, 5, me + sign * 4 * width, 3).start()
    heads(len(heads_left))
    for way, sign in ((0, 1), (1, -1)):
        @pl.when(exists(y - sign * 4))
        def _():
            copy2(way, 6, 5, me - sign * 4 * width, 3).wait_recv()
            s_new, a_new = combine(win[way, 4], win[way, 6])
            win[way, 7, :piece, :] = s_new
            win[way, 7, piece:, :] = a_new

        @pl.when(jnp.logical_not(exists(y - sign * 4)))
        def _():
            win[way, 7] = win[way, 4]
    for way, sign in ((0, 1), (1, -1)):
        for k in near:
            @pl.when(exists(y + sign * k))
            def _():
                copy2(way, k, 0, me + sign * k * width, k - 1).wait_send()

        @pl.when(exists(y + sign * 4))
        def _():
            copy2(way, 6, 5, me + sign * 4 * width, 3).wait_send()
    entering = win[0, 7, :piece, :]
    leaving = win[1, 7, :piece, :]

    for i in range(width):
        out3[i, :piece, :] = (fwd_e[i] + fwd_g[i] * entering).astype(out3.dtype)
        out3[i, piece:, :] = (bwd_e[i] + bwd_g[i] * leaving).astype(out3.dtype)
    own = pltpu.make_async_copy(out3.at[c], recv3.at[c], local.at[1])
    own.start()
    sends = []
    for off in range(1, width):
        k = (c + off) % width
        cp = pltpu.make_async_remote_copy(
            src_ref=out3.at[k], dst_ref=recv3.at[c], send_sem=send3.at[off],
            recv_sem=rsem3.at[off], device_id=(y * width + k, col), device_id_type=MESH)
        cp.start()
        sends.append(cp)
    for off in range(1, width):
        k = (c + width - off) % width
        pltpu.make_async_remote_copy(
            src_ref=out3.at[k], dst_ref=recv3.at[k], send_sem=send3.at[off],
            recv_sem=rsem3.at[off], device_id=(y * width + k, col), device_id_type=MESH).wait_recv()
    own.wait()
    for cp in sends:
        cp.wait_send()

    s = width * piece
    for k in range(width):
        full[0, k * piece:(k + 1) * piece, :] = recv3[k, :piece, :].astype(jnp.float32)
        full[1, k * piece:(k + 1) * piece, :] = recv3[k, piece:, :].astype(jnp.float32)
    weighted = run_ref[...].astype(jnp.bfloat16)
    part_b = jnp.dot(weighted, c_ref[...], preferred_element_type=jnp.float32) + nt_dot_f32(
        xs_ref[...], full[1])
    part_c = lax.dot_general(
        weighted, b_ref[...], (((0,), (0,)), ((), ())), preferred_element_type=jnp.float32
    ) + nt_dot_f32(ds_ref[...], full[0])
    n_rows = part_b.shape[0]
    parts[:n_rows, :] = part_b.astype(parts.dtype)
    parts[n_rows:, :] = part_c.astype(parts.dtype)
    rows = gather1.shape[1]

    def chunk(i):
        return parts.at[pl.ds(pl.multiple_of(i * rows, rows), rows)]

    sends = []
    for k in range(1, groups):
        peer = (z + k) % groups
        cp = pltpu.make_async_remote_copy(
            src_ref=chunk(peer), dst_ref=gather1.at[z], send_sem=hsend1.at[k],
            recv_sem=hrecv1.at[k], device_id=(me, peer), device_id_type=MESH)
        cp.start()
        sends.append(cp)
    adj = full[1]
    adj_hi = adj.astype(jnp.bfloat16)
    adj_lo = (adj - adj_hi.astype(jnp.float32)).astype(jnp.bfloat16)
    b_adj = jnp.dot(b_ref[...], adj_hi, preferred_element_type=jnp.float32) + jnp.dot(
        b_ref[...], adj_lo, preferred_element_type=jnp.float32)
    for h in range(cr_ref.shape[0]):
        lanes = slice(h * hd, (h + 1) * hd)
        gv_ref[:, lanes] = (dx_ref[:, lanes] + ie_ref[:, h:h + 1] * b_adj[:, lanes]).astype(
            gv_ref.dtype)
    total = parts[pl.ds(pl.multiple_of(z * rows, rows), rows), :].astype(jnp.float32)
    for k in range(1, groups):
        source = (z + groups - k) % groups
        pltpu.make_async_remote_copy(
            src_ref=chunk(source), dst_ref=gather1.at[source], send_sem=hsend1.at[k],
            recv_sem=hrecv1.at[k], device_id=(me, source), device_id_type=MESH).wait_recv()
        total = total + gather1[source].astype(jnp.float32)
    for cp in sends:
        cp.wait_send()
    gather2[z] = total.astype(gather2.dtype)
    sends = []
    for k in range(1, groups):
        peer = (z + k) % groups
        cp = pltpu.make_async_remote_copy(
            src_ref=gather2.at[z], dst_ref=gather2.at[z], send_sem=hsend2.at[k],
            recv_sem=hrecv2.at[k], device_id=(me, peer), device_id_type=MESH)
        cp.start()
        sends.append(cp)
    for k in range(1, groups):
        source = (z + groups - k) % groups
        pltpu.make_async_remote_copy(
            src_ref=gather2.at[source], dst_ref=gather2.at[source], send_sem=hsend2.at[k],
            recv_sem=hrecv2.at[k], device_id=(me, source), device_id_type=MESH).wait_recv()
    for cp in sends:
        cp.wait_send()
    sum_ref[...] = gather2[...]


def exclusive_scans(count, groups, decay_cols, forward, backward, x, dy, scores_t, cumulative,
                    into_end, from_start, b_inputs, c_inputs):
    s, w = forward.shape
    width = 8 if count % 8 == 0 else 1
    rows_n = count // width
    piece = s // width
    assert rows_n <= 8
    pack = jnp.concatenate(
        [forward.reshape(width, piece, w), backward.reshape(width, piece, w)], axis=1
    ).astype(jnp.bfloat16)
    decay_rows = jnp.broadcast_to(decay_cols, (8, w))
    length = scores_t.shape[0]
    chunk_rows = 2 * length // groups
    grad_values, sums = pl.pallas_call(
        functools.partial(scan_kernel, rows_n, width, groups),
        out_shape=(
            jax.ShapeDtypeStruct(x.shape, jnp.bfloat16),
            jax.ShapeDtypeStruct((groups, chunk_rows, s), jnp.bfloat16),
        ),
        in_specs=[pl.BlockSpec(memory_space=pltpu.VMEM)] * 11,
        out_specs=(pl.BlockSpec(memory_space=pltpu.VMEM),) * 2,
        scratch_shapes=[
            pltpu.VMEM((length, length), jnp.float32),
            pltpu.VMEM(x.shape, jnp.float32),
            pltpu.VMEM(x.shape, jnp.float32),
            pltpu.VMEM(x.shape, jnp.float32),
            pltpu.VMEM((width, 2 * piece, w), jnp.bfloat16),
            pltpu.VMEM((width, 8, w), jnp.float32),
            pltpu.VMEM((2, 8, piece + 8, w), jnp.float32),
            pltpu.VMEM((width, 2 * piece, w), jnp.bfloat16),
            pltpu.VMEM((width, 2 * piece, w), jnp.bfloat16),
            pltpu.VMEM((2, s, w), jnp.float32),
            pltpu.VMEM((2 * length, s), jnp.bfloat16),
            pltpu.VMEM((groups, chunk_rows, s), jnp.bfloat16),
            pltpu.VMEM((groups, chunk_rows, s), jnp.bfloat16),
            pltpu.SemaphoreType.DMA((width,)),
            pltpu.SemaphoreType.DMA((width,)),
            pltpu.SemaphoreType.DMA((2, 4)),
            pltpu.SemaphoreType.DMA((2, 4)),
            pltpu.SemaphoreType.DMA((width,)),
            pltpu.SemaphoreType.DMA((width,)),
            pltpu.SemaphoreType.DMA((3,)),
            pltpu.SemaphoreType.DMA((width,)),
            pltpu.SemaphoreType.DMA((width,)),
            pltpu.SemaphoreType.DMA((groups,)),
            pltpu.SemaphoreType.DMA((groups,)),
            pltpu.SemaphoreType.DMA((groups,)),
            pltpu.SemaphoreType.DMA((groups,)),
        ],
        compiler_params=pltpu.CompilerParams(collective_id=1, has_side_effects=True),
    )(pack, decay_rows, x, dy, scores_t, cumulative, cumulative.T, into_end.T, from_start.T, b_inputs, c_inputs)
    sums = sums.reshape(2 * length, s)
    return grad_values, sums[:length], sums[length:]


def shards(count, groups, token_values, b_inputs, c_inputs, log_decay, grad_out):
    length = token_values.shape[0]
    heads_here = log_decay.shape[0]
    head_dim = token_values.shape[1] // heads_here
    state_size = b_inputs.shape[1]
    positions = lax.iota(jnp.int32, length)
    upto = (positions[:, None] <= positions[None, :]).astype(jnp.float32)
    cumulative = jnp.dot(log_decay, upto, precision=PRECISE)
    block_log = cumulative[:, -1]
    into_end = jnp.exp(block_log[:, None] - cumulative)
    from_start = jnp.exp(cumulative)
    block_decay = jnp.exp(block_log)
    b_float = b_inputs.astype(jnp.float32)
    c_float = c_inputs.astype(jnp.float32)
    decayed_b = (into_end[:, :, None] * b_float[None]).astype(jnp.bfloat16)
    decayed_c = (from_start[:, :, None] * c_float[None]).astype(jnp.bfloat16)
    x_heads = token_values.reshape(length, heads_here, head_dim)
    dy_heads = grad_out.reshape(length, heads_here, head_dim)
    state_local = jnp.einsum(
        "htn,thp->nhp", decayed_b, x_heads, preferred_element_type=jnp.float32
    ).reshape(state_size, heads_here * head_dim)
    adjoint_local = jnp.einsum(
        "hsn,shp->nhp", decayed_c, dy_heads, preferred_element_type=jnp.float32
    ).reshape(state_size, heads_here * head_dim)
    decay_cols = jnp.repeat(block_decay, head_dim)[None, :]
    scores_t = lax.dot_general(
        b_inputs, c_inputs, (((1,), (1,)), ((), ())), preferred_element_type=jnp.float32
    )
    grad_values, grad_b, grad_c = exclusive_scans(
        count, groups, decay_cols, state_local, adjoint_local, token_values, grad_out, scores_t,
        cumulative, into_end, from_start, b_inputs, c_inputs,
    )
    return grad_values, grad_b, grad_c


def solution(mesh):
    in_specs = (
        P("seq", "head"),
        P("seq", None),
        P("seq", None),
        P("head", "seq"),
        P("seq", "head"),
    )
    out_specs = (P("seq", "head"), P("seq", None), P("seq", None))
    body = functools.partial(shards, mesh.shape["seq"], mesh.shape["head"])
    return jax.shard_map(body, mesh=mesh, in_specs=in_specs, out_specs=out_specs, check_vma=False)
```

```python
import functools

import jax
import jax.numpy as jnp
from jax import lax
from jax.experimental import pallas as pl
from jax.experimental.pallas import tpu as pltpu
from jax.sharding import PartitionSpec as P

PRECISE = lax.Precision.HIGHEST
MESH = pl.DeviceIdType.MESH


def nt_dot(p, q):
    return lax.dot_general(p, q, (((1,), (1,)), ((), ())), preferred_element_type=jnp.float32)


def nt_dot_f32(p, q):
    ph = p.astype(jnp.bfloat16)
    pl_ = (p - ph.astype(jnp.float32)).astype(jnp.bfloat16)
    qh = q.astype(jnp.bfloat16)
    ql = (q - qh.astype(jnp.float32)).astype(jnp.bfloat16)
    return nt_dot(ph, qh) + (nt_dot(ph, ql) + nt_dot(pl_, qh))


def scan_kernel(rows_n, width, groups, pack_ref, pdec_ref, x_ref, dy_ref, sc_ref, cr_ref, cc_ref,
                b_ref, c_ref, gv_ref, sum_ref, run_ref, dx_ref, xs_ref, ds_ref, recv1, rdec,
                win, out3, recv3, full, parts, gather1, gather2, send1, rsem1, send2, rsem2, send3, rsem3,
                local, dsend, drecv, hsend1, hrecv1, hsend2, hrecv2):
    me = lax.axis_index("seq")
    col = lax.axis_index("head")
    c = me % width
    y = me // width
    piece = recv1.shape[1] // 2
    spans = [1, 2, 3, 4]

    length = sc_ref.shape[0]
    later = lax.broadcasted_iota(jnp.int32, (length, length), 1) >= lax.broadcasted_iota(
        jnp.int32, (length, length), 0)
    run_ref[...] = jnp.zeros(run_ref.shape, run_ref.dtype)

    def head(h):
        gaps = cr_ref[h:h + 1, :] - cc_ref[:, h:h + 1]

        dec = jnp.where(later, jnp.exp(jnp.where(later, gaps, 0.0)), 0.0)
        mix = (sc_ref[...] * dec).astype(jnp.bfloat16)
        lanes = slice(h * hd, (h + 1) * hd)
        dy_h = dy_ref[:, lanes]
        x_h = x_ref[:, lanes]
        xs_ref[:, lanes] = x_h.astype(jnp.float32) * cc_ref[:, nh + h:nh + h + 1]
        ds_ref[:, lanes] = dy_h.astype(jnp.float32) * cc_ref[:, 2 * nh + h:2 * nh + h + 1]
        dx_ref[:, lanes] = jnp.dot(mix, dy_h, preferred_element_type=jnp.float32)
        pairs = lax.dot_general(
            x_h, dy_h, (((1,), (1,)), ((), ())), preferred_element_type=jnp.float32)
        run_ref[...] += dec * pairs

    nh = cr_ref.shape[0]
    heads_left = list(range(nh))
    hd = x_ref.shape[1] // cr_ref.shape[0]

    def heads(k):
        for _ in range(k):
            if heads_left:
                head(heads_left.pop(0))

    barrier = pltpu.get_barrier_semaphore()
    for off in range(1, width):
        peer = y * width + (c + off) % width
        pl.semaphore_signal(barrier, inc=1, device_id=(peer, col), device_id_type=MESH)
    for d in spans:
        @pl.when(y + d < rows_n)
        def _():
            pl.semaphore_signal(barrier, inc=1, device_id=(me + d * width, col), device_id_type=MESH)

        @pl.when(y - d >= 0)
        def _():
            pl.semaphore_signal(barrier, inc=1, device_id=(me - d * width, col), device_id_type=MESH)
    z = lax.axis_index("head")
    for off in range(1, groups):
        pl.semaphore_signal(
            barrier, inc=1, device_id=(me, (z + off) % groups), device_id_type=MESH)
    peers = width - 1 + groups - 1
    for d in spans:
        peers = peers + ((rows_n - 1 - y) // d + rows_n - 1) // rows_n + (y // d + rows_n - 1) // rows_n
    heads(2)
    pl.semaphore_wait(barrier, peers)

    own = pltpu.make_async_copy(pack_ref.at[c], recv1.at[c], local.at[0])
    own.start()
    own_dec = pltpu.make_async_copy(pdec_ref, rdec.at[c], local.at[2])
    own_dec.start()
    sends = []
    for off in range(1, width):
        k = (c + off) % width
        cp = pltpu.make_async_remote_copy(
            src_ref=pack_ref.at[k], dst_ref=recv1.at[c], send_sem=send1.at[off],
            recv_sem=rsem1.at[off], device_id=(y * width + k, col), device_id_type=MESH)
        cp.start()
        sends.append(cp)
        cp = pltpu.make_async_remote_copy(
            src_ref=pdec_ref, dst_ref=rdec.at[c], send_sem=dsend.at[off],
            recv_sem=drecv.at[off], device_id=(y * width + k, col), device_id_type=MESH)
        cp.start()
        sends.append(cp)
    heads(3)
    for off in range(1, width):
        k = (c + width - off) % width
        pltpu.make_async_remote_copy(
            src_ref=pack_ref.at[k], dst_ref=recv1.at[k], send_sem=send1.at[off],
            recv_sem=rsem1.at[off], device_id=(y * width + k, col), device_id_type=MESH).wait_recv()
        pltpu.make_async_remote_copy(
            src_ref=pdec_ref, dst_ref=rdec.at[k], send_sem=dsend.at[off],
            recv_sem=drecv.at[off], device_id=(y * width + k, col), device_id_type=MESH).wait_recv()
    own.wait()
    own_dec.wait()
    for cp in sends:
        cp.wait_send()

    def decay(i):
        return rdec[i, 0:1, :]

    fwd_e, fwd_g = [None] * width, [None] * width
    e = jnp.zeros((piece, recv1.shape[2]), jnp.float32)
    g = jnp.ones((1, recv1.shape[2]), jnp.float32)
    for i in range(width):
        fwd_e[i], fwd_g[i] = e, g
        a = decay(i)
        e = a * e + recv1[i, :piece, :].astype(jnp.float32)
        g = g * a
    bwd_e, bwd_g = [None] * width, [None] * width
    f = jnp.zeros((piece, recv1.shape[2]), jnp.float32)
    h = jnp.ones((1, recv1.shape[2]), jnp.float32)
    for i in reversed(range(width)):
        bwd_e[i], bwd_g[i] = f, h
        a = decay(i)
        f = a * f + recv1[i, piece:2 * piece, :].astype(jnp.float32)
        h = h * a
    win[0, 0, :piece, :] = e
    win[0, 0, piece:, :] = jnp.broadcast_to(g, (win.shape[2] - piece, g.shape[1]))
    win[1, 0, :piece, :] = f
    win[1, 0, piece:, :] = jnp.broadcast_to(h, (win.shape[2] - piece, h.shape[1]))

    def combine(w_near, w_far):
        a = w_near[piece:, :]
        return w_near[:piece, :] + jnp.broadcast_to(a[:1], (piece, a.shape[1])) * w_far[:piece, :], a * w_far[piece:, :]

    def copy2(way, slot, src_slot, target, sem):
        return pltpu.make_async_remote_copy(
            src_ref=win.at[way, src_slot], dst_ref=win.at[way, slot], send_sem=send2.at[way, sem],
            recv_sem=rsem2.at[way, sem], device_id=(target, col), device_id_type=MESH)

    def exists(row):
        return jnp.logical_and(row >= 0, row < rows_n)

    near = [1, 2, 3]
    for way, sign in ((0, 1), (1, -1)):
        for k in near:
            @pl.when(exists(y + sign * k))
            def _():
                copy2(way, k, 0, me + sign * k * width, k - 1).start()
    heads(2)
    for way, sign in ((0, 1), (1, -1)):
        win[way, 4] = jnp.zeros(win.shape[2:], win.dtype)
        for k in near:
            @pl.when(exists(y - sign * k))
            def _():
                copy2(way, k, 0, me - sign * k * width, k - 1).wait_recv()
                s_new, a_new = combine(win[way, 4], win[way, k])
                if k == 1:
                    win[way, 4] = win[way, 1]
                else:
                    win[way, 4, :piece, :] = s_new
                    win[way, 4, piece:, :] = a_new
        s_inc, a_inc = combine(win[way, 0], win[way, 4])
        win[way, 5, :piece, :] = s_inc
        win[way, 5, piece:, :] = a_inc

        @pl.when(exists(y + sign * 4))
        def _():
            copy2(way, 6, 5, me + sign * 4 * width, 3).start()
    heads(len(heads_left))
    for way, sign in ((0, 1), (1, -1)):
        @pl.when(exists(y - sign * 4))
        def _():
            copy2(way, 6, 5, me - sign * 4 * width, 3).wait_recv()
            s_new, a_new = combine(win[way, 4], win[way, 6])
            win[way, 7, :piece, :] = s_new
            win[way, 7, piece:, :] = a_new

        @pl.when(jnp.logical_not(exists(y - sign * 4)))
        def _():
            win[way, 7] = win[way, 4]
    for way, sign in ((0, 1), (1, -1)):
        for k in near:
            @pl.when(exists(y + sign * k))
            def _():
                copy2(way, k, 0, me + sign * k * width, k - 1).wait_send()

        @pl.when(exists(y + sign * 4))
        def _():
            copy2(way, 6, 5, me + sign * 4 * width, 3).wait_send()
    entering = win[0, 7, :piece, :]
    leaving = win[1, 7, :piece, :]

    for i in range(width):
        out3[i, :piece, :] = (fwd_e[i] + fwd_g[i] * entering).astype(out3.dtype)
        out3[i, piece:, :] = (bwd_e[i] + bwd_g[i] * leaving).astype(out3.dtype)
    own = pltpu.make_async_copy(out3.at[c], recv3.at[c], local.at[1])
    own.start()
    sends = []
    for off in range(1, width):
        k = (c + off) % width
        cp = pltpu.make_async_remote_copy(
            src_ref=out3.at[k], dst_ref=recv3.at[c], send_sem=send3.at[off],
            recv_sem=rsem3.at[off], device_id=(y * width + k, col), device_id_type=MESH)
        cp.start()
        sends.append(cp)
    for off in range(1, width):
        k = (c + width - off) % width
        pltpu.make_async_remote_copy(
            src_ref=out3.at[k], dst_ref=recv3.at[k], send_sem=send3.at[off],
            recv_sem=rsem3.at[off], device_id=(y * width + k, col), device_id_type=MESH).wait_recv()
    own.wait()
    for cp in sends:
        cp.wait_send()

    s = width * piece
    for k in range(width):
        full[0, k * piece:(k + 1) * piece, :] = recv3[k, :piece, :].astype(jnp.float32)
        full[1, k * piece:(k + 1) * piece, :] = recv3[k, piece:, :].astype(jnp.float32)
    weighted = run_ref[...].astype(jnp.bfloat16)
    part_b = jnp.dot(weighted, c_ref[...], preferred_element_type=jnp.float32) + nt_dot_f32(
        xs_ref[...], full[1])
    part_c = lax.dot_general(
        weighted, b_ref[...], (((0,), (0,)), ((), ())), preferred_element_type=jnp.float32
    ) + nt_dot_f32(ds_ref[...], full[0])
    n_rows = part_b.shape[0]
    parts[:n_rows, :] = part_b.astype(parts.dtype)
    parts[n_rows:, :] = part_c.astype(parts.dtype)
    rows = gather1.shape[1]

    def chunk(i):
        return parts.at[pl.ds(pl.multiple_of(i * rows, rows), rows)]

    sends = []
    for k in range(1, groups):
        peer = (z + k) % groups
        cp = pltpu.make_async_remote_copy(
            src_ref=chunk(peer), dst_ref=gather1.at[z], send_sem=hsend1.at[k],
            recv_sem=hrecv1.at[k], device_id=(me, peer), device_id_type=MESH)
        cp.start()
        sends.append(cp)
    adj = full[1]
    adj_hi = adj.astype(jnp.bfloat16)
    adj_lo = (adj - adj_hi.astype(jnp.float32)).astype(jnp.bfloat16)
    b_adj = jnp.dot(b_ref[...], adj_hi, preferred_element_type=jnp.float32) + jnp.dot(
        b_ref[...], adj_lo, preferred_element_type=jnp.float32)
    for h in range(cr_ref.shape[0]):
        lanes = slice(h * hd, (h + 1) * hd)
        gv_ref[:, lanes] = (dx_ref[:, lanes] + cc_ref[:, nh + h:nh + h + 1] * b_adj[:, lanes]).astype(
            gv_ref.dtype)
    total = parts[pl.ds(pl.multiple_of(z * rows, rows), rows), :].astype(jnp.float32)
    for k in range(1, groups):
        source = (z + groups - k) % groups
        pltpu.make_async_remote_copy(
            src_ref=chunk(source), dst_ref=gather1.at[source], send_sem=hsend1.at[k],
            recv_sem=hrecv1.at[k], device_id=(me, source), device_id_type=MESH).wait_recv()
        total = total + gather1[source].astype(jnp.float32)
    for cp in sends:
        cp.wait_send()
    gather2[z] = total.astype(gather2.dtype)
    sends = []
    for k in range(1, groups):
        peer = (z + k) % groups
        cp = pltpu.make_async_remote_copy(
            src_ref=gather2.at[z], dst_ref=gather2.at[z], send_sem=hsend2.at[k],
            recv_sem=hrecv2.at[k], device_id=(me, peer), device_id_type=MESH)
        cp.start()
        sends.append(cp)
    for k in range(1, groups):
        source = (z + groups - k) % groups
        pltpu.make_async_remote_copy(
            src_ref=gather2.at[source], dst_ref=gather2.at[source], send_sem=hsend2.at[k],
            recv_sem=hrecv2.at[k], device_id=(me, source), device_id_type=MESH).wait_recv()
    for cp in sends:
        cp.wait_send()
    sum_ref[...] = gather2[...]


def exclusive_scans(count, groups, decay_cols, forward, backward, x, dy, scores_t, cumulative,
                    into_end, from_start, b_inputs, c_inputs):
    s, w = forward.shape
    width = 8 if count % 8 == 0 else 1
    rows_n = count // width
    piece = s // width
    assert rows_n <= 8
    pack = jnp.concatenate(
        [forward.reshape(width, piece, w), backward.reshape(width, piece, w)], axis=1
    ).astype(jnp.bfloat16)
    decay_rows = jnp.broadcast_to(decay_cols, (8, w))
    length = scores_t.shape[0]
    chunk_rows = 2 * length // groups
    columns = jnp.concatenate([cumulative, into_end, from_start], axis=0).T
    grad_values, sums = pl.pallas_call(
        functools.partial(scan_kernel, rows_n, width, groups),
        out_shape=(
            jax.ShapeDtypeStruct(x.shape, jnp.bfloat16),
            jax.ShapeDtypeStruct((groups, chunk_rows, s), jnp.bfloat16),
        ),
        in_specs=[pl.BlockSpec(memory_space=pltpu.VMEM)] * 9,
        out_specs=(pl.BlockSpec(memory_space=pltpu.VMEM),) * 2,
        scratch_shapes=[
            pltpu.VMEM((length, length), jnp.float32),
            pltpu.VMEM(x.shape, jnp.float32),
            pltpu.VMEM(x.shape, jnp.float32),
            pltpu.VMEM(x.shape, jnp.float32),
            pltpu.VMEM((width, 2 * piece, w), jnp.bfloat16),
            pltpu.VMEM((width, 8, w), jnp.float32),
            pltpu.VMEM((2, 8, piece + 8, w), jnp.float32),
            pltpu.VMEM((width, 2 * piece, w), jnp.bfloat16),
            pltpu.VMEM((width, 2 * piece, w), jnp.bfloat16),
            pltpu.VMEM((2, s, w), jnp.float32),
            pltpu.VMEM((2 * length, s), jnp.bfloat16),
            pltpu.VMEM((groups, chunk_rows, s), jnp.bfloat16),
            pltpu.VMEM((groups, chunk_rows, s), jnp.bfloat16),
            pltpu.SemaphoreType.DMA((width,)),
            pltpu.SemaphoreType.DMA((width,)),
            pltpu.SemaphoreType.DMA((2, 4)),
            pltpu.SemaphoreType.DMA((2, 4)),
            pltpu.SemaphoreType.DMA((width,)),
            pltpu.SemaphoreType.DMA((width,)),
            pltpu.SemaphoreType.DMA((3,)),
            pltpu.SemaphoreType.DMA((width,)),
            pltpu.SemaphoreType.DMA((width,)),
            pltpu.SemaphoreType.DMA((groups,)),
            pltpu.SemaphoreType.DMA((groups,)),
            pltpu.SemaphoreType.DMA((groups,)),
            pltpu.SemaphoreType.DMA((groups,)),
        ],
        compiler_params=pltpu.CompilerParams(collective_id=1, has_side_effects=True),
    )(pack, decay_rows, x, dy, scores_t, cumulative, columns, b_inputs, c_inputs)
    sums = sums.reshape(2 * length, s)
    return grad_values, sums[:length], sums[length:]


def shards(count, groups, token_values, b_inputs, c_inputs, log_decay, grad_out):
    length = token_values.shape[0]
    heads_here = log_decay.shape[0]
    head_dim = token_values.shape[1] // heads_here
    state_size = b_inputs.shape[1]
    positions = lax.iota(jnp.int32, length)
    upto = (positions[:, None] <= positions[None, :]).astype(jnp.float32)
    cumulative = jnp.dot(log_decay, upto, precision=PRECISE)
    block_log = cumulative[:, -1]
    into_end = jnp.exp(block_log[:, None] - cumulative)
    from_start = jnp.exp(cumulative)
    block_decay = jnp.exp(block_log)
    b_float = b_inputs.astype(jnp.float32)
    c_float = c_inputs.astype(jnp.float32)
    decayed_b = (into_end[:, :, None] * b_float[None]).astype(jnp.bfloat16)
    decayed_c = (from_start[:, :, None] * c_float[None]).astype(jnp.bfloat16)
    x_heads = token_values.reshape(length, heads_here, head_dim)
    dy_heads = grad_out.reshape(length, heads_here, head_dim)
    state_local = jnp.einsum(
        "htn,thp->nhp", decayed_b, x_heads, preferred_element_type=jnp.float32
    ).reshape(state_size, heads_here * head_dim)
    adjoint_local = jnp.einsum(
        "hsn,shp->nhp", decayed_c, dy_heads, preferred_element_type=jnp.float32
    ).reshape(state_size, heads_here * head_dim)
    decay_cols = jnp.repeat(block_decay, head_dim)[None, :]
    scores_t = lax.dot_general(
        b_inputs, c_inputs, (((1,), (1,)), ((), ())), preferred_element_type=jnp.float32
    )
    grad_values, grad_b, grad_c = exclusive_scans(
        count, groups, decay_cols, state_local, adjoint_local, token_values, grad_out, scores_t,
        cumulative, into_end, from_start, b_inputs, c_inputs,
    )
    return grad_values, grad_b, grad_c


def solution(mesh):
    in_specs = (
        P("seq", "head"),
        P("seq", None),
        P("seq", None),
        P("head", "seq"),
        P("seq", "head"),
    )
    out_specs = (P("seq", "head"), P("seq", None), P("seq", None))
    body = functools.partial(shards, mesh.shape["seq"], mesh.shape["head"])
    return jax.shard_map(body, mesh=mesh, in_specs=in_specs, out_specs=out_specs, check_vma=False)
```

```python
import functools

import jax
import jax.numpy as jnp
from jax import lax
from jax.experimental import pallas as pl
from jax.experimental.pallas import tpu as pltpu
from jax.sharding import PartitionSpec as P

PRECISE = lax.Precision.HIGHEST
MESH = pl.DeviceIdType.MESH


def nt_dot(p, q):
    return lax.dot_general(p, q, (((1,), (1,)), ((), ())), preferred_element_type=jnp.float32)


def nt_dot_f32(p, q):
    ph = p.astype(jnp.bfloat16)
    pl_ = (p - ph.astype(jnp.float32)).astype(jnp.bfloat16)
    qh = q.astype(jnp.bfloat16)
    ql = (q - qh.astype(jnp.float32)).astype(jnp.bfloat16)
    return nt_dot(ph, qh) + (nt_dot(ph, ql) + nt_dot(pl_, qh))


def scan_kernel(rows_n, width, groups, pack_ref, dcol_ref, x_ref, dy_ref, cr_ref, cc_ref,
                b_ref, c_ref, gv_ref, sum_ref, run_ref, dx_ref, xs_ref, ds_ref, recv1, rdec,
                win, out3, recv3, full, parts, gather1, gather2, send1, rsem1, send2, rsem2, send3, rsem3,
                local, dsend, drecv, hsend1, hrecv1, hsend2, hrecv2, sc_ref, pdec_ref):
    me = lax.axis_index("seq")
    col = lax.axis_index("head")
    c = me % width
    y = me // width
    piece = recv1.shape[1] // 2
    spans = [1, 2, 3, 4]

    length = x_ref.shape[0]
    pdec_ref[...] = jnp.broadcast_to(dcol_ref[...], pdec_ref.shape)
    later = lax.broadcasted_iota(jnp.int32, (length, length), 1) >= lax.broadcasted_iota(
        jnp.int32, (length, length), 0)
    run_ref[...] = jnp.zeros(run_ref.shape, run_ref.dtype)

    def head(h):
        gaps = cr_ref[h:h + 1, :] - cc_ref[:, h:h + 1]

        dec = jnp.where(later, jnp.exp(jnp.where(later, gaps, 0.0)), 0.0)
        mix = (sc_ref[...] * dec).astype(jnp.bfloat16)
        lanes = slice(h * hd, (h + 1) * hd)
        dy_h = dy_ref[:, lanes]
        x_h = x_ref[:, lanes]
        xs_ref[:, lanes] = x_h.astype(jnp.float32) * cc_ref[:, nh + h:nh + h + 1]
        ds_ref[:, lanes] = dy_h.astype(jnp.float32) * cc_ref[:, 2 * nh + h:2 * nh + h + 1]
        dx_ref[:, lanes] = jnp.dot(mix, dy_h, preferred_element_type=jnp.float32)
        pairs = lax.dot_general(
            x_h, dy_h, (((1,), (1,)), ((), ())), preferred_element_type=jnp.float32)
        run_ref[...] += dec * pairs

    nh = cr_ref.shape[0]
    heads_left = list(range(nh))
    hd = x_ref.shape[1] // cr_ref.shape[0]

    def heads(k):
        for _ in range(k):
            if heads_left:
                head(heads_left.pop(0))

    barrier = pltpu.get_barrier_semaphore()
    for off in range(1, width):
        peer = y * width + (c + off) % width
        pl.semaphore_signal(barrier, inc=1, device_id=(peer, col), device_id_type=MESH)
    for d in spans:
        @pl.when(y + d < rows_n)
        def _():
            pl.semaphore_signal(barrier, inc=1, device_id=(me + d * width, col), device_id_type=MESH)

        @pl.when(y - d >= 0)
        def _():
            pl.semaphore_signal(barrier, inc=1, device_id=(me - d * width, col), device_id_type=MESH)
    z = lax.axis_index("head")
    for off in range(1, groups):
        pl.semaphore_signal(
            barrier, inc=1, device_id=(me, (z + off) % groups), device_id_type=MESH)
    peers = width - 1 + groups - 1
    for d in spans:
        peers = peers + ((rows_n - 1 - y) // d + rows_n - 1) // rows_n + (y // d + rows_n - 1) // rows_n
    sc_ref[...] = nt_dot(b_ref[...], c_ref[...])
    heads(2)
    pl.semaphore_wait(barrier, peers)

    own = pltpu.make_async_copy(pack_ref.at[c], recv1.at[c], local.at[0])
    own.start()
    own_dec = pltpu.make_async_copy(pdec_ref, rdec.at[c], local.at[2])
    own_dec.start()
    sends = []
    for off in range(1, width):
        k = (c + off) % width
        cp = pltpu.make_async_remote_copy(
            src_ref=pack_ref.at[k], dst_ref=recv1.at[c], send_sem=send1.at[off],
            recv_sem=rsem1.at[off], device_id=(y * width + k, col), device_id_type=MESH)
        cp.start()
        sends.append(cp)
        cp = pltpu.make_async_remote_copy(
            src_ref=pdec_ref, dst_ref=rdec.at[c], send_sem=dsend.at[off],
            recv_sem=drecv.at[off], device_id=(y * width + k, col), device_id_type=MESH)
        cp.start()
        sends.append(cp)
    heads(3)
    for off in range(1, width):
        k = (c + width - off) % width
        pltpu.make_async_remote_copy(
            src_ref=pack_ref.at[k], dst_ref=recv1.at[k], send_sem=send1.at[off],
            recv_sem=rsem1.at[off], device_id=(y * width + k, col), device_id_type=MESH).wait_recv()
        pltpu.make_async_remote_copy(
            src_ref=pdec_ref, dst_ref=rdec.at[k], send_sem=dsend.at[off],
            recv_sem=drecv.at[off], device_id=(y * width + k, col), device_id_type=MESH).wait_recv()
    own.wait()
    own_dec.wait()
    for cp in sends:
        cp.wait_send()

    def decay(i):
        return rdec[i, 0:1, :]

    fwd_e, fwd_g = [None] * width, [None] * width
    e = jnp.zeros((piece, recv1.shape[2]), jnp.float32)
    g = jnp.ones((1, recv1.shape[2]), jnp.float32)
    for i in range(width):
        fwd_e[i], fwd_g[i] = e, g
        a = decay(i)
        e = a * e + recv1[i, :piece, :].astype(jnp.float32)
        g = g * a
    bwd_e, bwd_g = [None] * width, [None] * width
    f = jnp.zeros((piece, recv1.shape[2]), jnp.float32)
    h = jnp.ones((1, recv1.shape[2]), jnp.float32)
    for i in reversed(range(width)):
        bwd_e[i], bwd_g[i] = f, h
        a = decay(i)
        f = a * f + recv1[i, piece:2 * piece, :].astype(jnp.float32)
        h = h * a
    win[0, 0, :piece, :] = e
    win[0, 0, piece:, :] = jnp.broadcast_to(g, (win.shape[2] - piece, g.shape[1]))
    win[1, 0, :piece, :] = f
    win[1, 0, piece:, :] = jnp.broadcast_to(h, (win.shape[2] - piece, h.shape[1]))

    def combine(w_near, w_far):
        a = w_near[piece:, :]
        return w_near[:piece, :] + jnp.broadcast_to(a[:1], (piece, a.shape[1])) * w_far[:piece, :], a * w_far[piece:, :]

    def copy2(way, slot, src_slot, target, sem):
        return pltpu.make_async_remote_copy(
            src_ref=win.at[way, src_slot], dst_ref=win.at[way, slot], send_sem=send2.at[way, sem],
            recv_sem=rsem2.at[way, sem], device_id=(target, col), device_id_type=MESH)

    def exists(row):
        return jnp.logical_and(row >= 0, row < rows_n)

    near = [1, 2, 3]
    for way, sign in ((0, 1), (1, -1)):
        for k in near:
            @pl.when(exists(y + sign * k))
            def _():
                copy2(way, k, 0, me + sign * k * width, k - 1).start()
    heads(2)
    for way, sign in ((0, 1), (1, -1)):
        win[way, 4] = jnp.zeros(win.shape[2:], win.dtype)
        for k in near:
            @pl.when(exists(y - sign * k))
            def _():
                copy2(way, k, 0, me - sign * k * width, k - 1).wait_recv()
                s_new, a_new = combine(win[way, 4], win[way, k])
                if k == 1:
                    win[way, 4] = win[way, 1]
                else:
                    win[way, 4, :piece, :] = s_new
                    win[way, 4, piece:, :] = a_new
        s_inc, a_inc = combine(win[way, 0], win[way, 4])
        win[way, 5, :piece, :] = s_inc
        win[way, 5, piece:, :] = a_inc

        @pl.when(exists(y + sign * 4))
        def _():
            copy2(way, 6, 5, me + sign * 4 * width, 3).start()
    heads(len(heads_left))
    for way, sign in ((0, 1), (1, -1)):
        @pl.when(exists(y - sign * 4))
        def _():
            copy2(way, 6, 5, me - sign * 4 * width, 3).wait_recv()
            s_new, a_new = combine(win[way, 4], win[way, 6])
            win[way, 7, :piece, :] = s_new
            win[way, 7, piece:, :] = a_new

        @pl.when(jnp.logical_not(exists(y - sign * 4)))
        def _():
            win[way, 7] = win[way, 4]
    for way, sign in ((0, 1), (1, -1)):
        for k in near:
            @pl.when(exists(y + sign * k))
            def _():
                copy2(way, k, 0, me + sign * k * width, k - 1).wait_send()

        @pl.when(exists(y + sign * 4))
        def _():
            copy2(way, 6, 5, me + sign * 4 * width, 3).wait_send()
    entering = win[0, 7, :piece, :]
    leaving = win[1, 7, :piece, :]

    for i in range(width):
        out3[i, :piece, :] = (fwd_e[i] + fwd_g[i] * entering).astype(out3.dtype)
        out3[i, piece:, :] = (bwd_e[i] + bwd_g[i] * leaving).astype(out3.dtype)
    own = pltpu.make_async_copy(out3.at[c], recv3.at[c], local.at[1])
    own.start()
    sends = []
    for off in range(1, width):
        k = (c + off) % width
        cp = pltpu.make_async_remote_copy(
            src_ref=out3.at[k], dst_ref=recv3.at[c], send_sem=send3.at[off],
            recv_sem=rsem3.at[off], device_id=(y * width + k, col), device_id_type=MESH)
        cp.start()
        sends.append(cp)
    for off in range(1, width):
        k = (c + width - off) % width
        pltpu.make_async_remote_copy(
            src_ref=out3.at[k], dst_ref=recv3.at[k], send_sem=send3.at[off],
            recv_sem=rsem3.at[off], device_id=(y * width + k, col), device_id_type=MESH).wait_recv()
    own.wait()
    for cp in sends:
        cp.wait_send()

    s = width * piece
    for k in range(width):
        full[0, k * piece:(k + 1) * piece, :] = recv3[k, :piece, :].astype(jnp.float32)
        full[1, k * piece:(k + 1) * piece, :] = recv3[k, piece:, :].astype(jnp.float32)
    weighted = run_ref[...].astype(jnp.bfloat16)
    part_b = jnp.dot(weighted, c_ref[...], preferred_element_type=jnp.float32) + nt_dot_f32(
        xs_ref[...], full[1])
    part_c = lax.dot_general(
        weighted, b_ref[...], (((0,), (0,)), ((), ())), preferred_element_type=jnp.float32
    ) + nt_dot_f32(ds_ref[...], full[0])
    n_rows = part_b.shape[0]
    parts[:n_rows, :] = part_b.astype(parts.dtype)
    parts[n_rows:, :] = part_c.astype(parts.dtype)
    rows = gather1.shape[1]

    def chunk(i):
        return parts.at[pl.ds(pl.multiple_of(i * rows, rows), rows)]

    sends = []
    for k in range(1, groups):
        peer = (z + k) % groups
        cp = pltpu.make_async_remote_copy(
            src_ref=chunk(peer), dst_ref=gather1.at[z], send_sem=hsend1.at[k],
            recv_sem=hrecv1.at[k], device_id=(me, peer), device_id_type=MESH)
        cp.start()
        sends.append(cp)
    adj = full[1]
    adj_hi = adj.astype(jnp.bfloat16)
    adj_lo = (adj - adj_hi.astype(jnp.float32)).astype(jnp.bfloat16)
    b_adj = jnp.dot(b_ref[...], adj_hi, preferred_element_type=jnp.float32) + jnp.dot(
        b_ref[...], adj_lo, preferred_element_type=jnp.float32)
    for h in range(cr_ref.shape[0]):
        lanes = slice(h * hd, (h + 1) * hd)
        gv_ref[:, lanes] = (dx_ref[:, lanes] + cc_ref[:, nh + h:nh + h + 1] * b_adj[:, lanes]).astype(
            gv_ref.dtype)
    total = parts[pl.ds(pl.multiple_of(z * rows, rows), rows), :].astype(jnp.float32)
    for k in range(1, groups):
        source = (z + groups - k) % groups
        pltpu.make_async_remote_copy(
            src_ref=chunk(source), dst_ref=gather1.at[source], send_sem=hsend1.at[k],
            recv_sem=hrecv1.at[k], device_id=(me, source), device_id_type=MESH).wait_recv()
        total = total + gather1[source].astype(jnp.float32)
    for cp in sends:
        cp.wait_send()
    gather2[z] = total.astype(gather2.dtype)
    sends = []
    for k in range(1, groups):
        peer = (z + k) % groups
        cp = pltpu.make_async_remote_copy(
            src_ref=gather2.at[z], dst_ref=gather2.at[z], send_sem=hsend2.at[k],
            recv_sem=hrecv2.at[k], device_id=(me, peer), device_id_type=MESH)
        cp.start()
        sends.append(cp)
    for k in range(1, groups):
        source = (z + groups - k) % groups
        pltpu.make_async_remote_copy(
            src_ref=gather2.at[source], dst_ref=gather2.at[source], send_sem=hsend2.at[k],
            recv_sem=hrecv2.at[k], device_id=(me, source), device_id_type=MESH).wait_recv()
    for cp in sends:
        cp.wait_send()
    sum_ref[...] = gather2[...]


def exclusive_scans(count, groups, decay_cols, forward, backward, x, dy, cumulative,
                    into_end, from_start, b_inputs, c_inputs):
    s, w = forward.shape
    width = 8 if count % 8 == 0 else 1
    rows_n = count // width
    piece = s // width
    assert rows_n <= 8
    pack = jnp.concatenate(
        [forward.reshape(width, piece, w), backward.reshape(width, piece, w)], axis=1
    ).astype(jnp.bfloat16)
    length = x.shape[0]
    chunk_rows = 2 * length // groups
    columns = jnp.concatenate([cumulative, into_end, from_start], axis=0).T
    grad_values, sums = pl.pallas_call(
        functools.partial(scan_kernel, rows_n, width, groups),
        out_shape=(
            jax.ShapeDtypeStruct(x.shape, jnp.bfloat16),
            jax.ShapeDtypeStruct((groups, chunk_rows, s), jnp.bfloat16),
        ),
        in_specs=[pl.BlockSpec(memory_space=pltpu.VMEM)] * 8,
        out_specs=(pl.BlockSpec(memory_space=pltpu.VMEM),) * 2,
        scratch_shapes=[
            pltpu.VMEM((length, length), jnp.float32),
            pltpu.VMEM(x.shape, jnp.float32),
            pltpu.VMEM(x.shape, jnp.float32),
            pltpu.VMEM(x.shape, jnp.float32),
            pltpu.VMEM((width, 2 * piece, w), jnp.bfloat16),
            pltpu.VMEM((width, 8, w), jnp.float32),
            pltpu.VMEM((2, 8, piece + 8, w), jnp.float32),
            pltpu.VMEM((width, 2 * piece, w), jnp.bfloat16),
            pltpu.VMEM((width, 2 * piece, w), jnp.bfloat16),
            pltpu.VMEM((2, s, w), jnp.float32),
            pltpu.VMEM((2 * length, s), jnp.bfloat16),
            pltpu.VMEM((groups, chunk_rows, s), jnp.bfloat16),
            pltpu.VMEM((groups, chunk_rows, s), jnp.bfloat16),
            pltpu.SemaphoreType.DMA((width,)),
            pltpu.SemaphoreType.DMA((width,)),
            pltpu.SemaphoreType.DMA((2, 4)),
            pltpu.SemaphoreType.DMA((2, 4)),
            pltpu.SemaphoreType.DMA((width,)),
            pltpu.SemaphoreType.DMA((width,)),
            pltpu.SemaphoreType.DMA((3,)),
            pltpu.SemaphoreType.DMA((width,)),
            pltpu.SemaphoreType.DMA((width,)),
            pltpu.SemaphoreType.DMA((groups,)),
            pltpu.SemaphoreType.DMA((groups,)),
            pltpu.SemaphoreType.DMA((groups,)),
            pltpu.SemaphoreType.DMA((groups,)),
            pltpu.VMEM((length, length), jnp.float32),
            pltpu.VMEM((8, w), jnp.float32),
        ],
        compiler_params=pltpu.CompilerParams(collective_id=1, has_side_effects=True),
    )(pack, decay_cols, x, dy, cumulative, columns, b_inputs, c_inputs)
    sums = sums.reshape(2 * length, s)
    return grad_values, sums[:length], sums[length:]


def shards(count, groups, token_values, b_inputs, c_inputs, log_decay, grad_out):
    length = token_values.shape[0]
    heads_here = log_decay.shape[0]
    head_dim = token_values.shape[1] // heads_here
    state_size = b_inputs.shape[1]
    positions = lax.iota(jnp.int32, length)
    upto = (positions[:, None] <= positions[None, :]).astype(jnp.float32)
    cumulative = jnp.dot(log_decay, upto, precision=PRECISE)
    block_log = cumulative[:, -1]
    into_end = jnp.exp(block_log[:, None] - cumulative)
    from_start = jnp.exp(cumulative)
    block_decay = jnp.exp(block_log)
    b_float = b_inputs.astype(jnp.float32)
    c_float = c_inputs.astype(jnp.float32)
    decayed_b = (into_end[:, :, None] * b_float[None]).astype(jnp.bfloat16)
    decayed_c = (from_start[:, :, None] * c_float[None]).astype(jnp.bfloat16)
    x_heads = token_values.reshape(length, heads_here, head_dim)
    dy_heads = grad_out.reshape(length, heads_here, head_dim)
    state_local = jnp.einsum(
        "htn,thp->nhp", decayed_b, x_heads, preferred_element_type=jnp.float32
    ).reshape(state_size, heads_here * head_dim)
    adjoint_local = jnp.einsum(
        "hsn,shp->nhp", decayed_c, dy_heads, preferred_element_type=jnp.float32
    ).reshape(state_size, heads_here * head_dim)
    decay_cols = jnp.repeat(block_decay, head_dim)[None, :]
    grad_values, grad_b, grad_c = exclusive_scans(
        count, groups, decay_cols, state_local, adjoint_local, token_values, grad_out,
        cumulative, into_end, from_start, b_inputs, c_inputs,
    )
    return grad_values, grad_b, grad_c


def solution(mesh):
    in_specs = (
        P("seq", "head"),
        P("seq", None),
        P("seq", None),
        P("head", "seq"),
        P("seq", "head"),
    )
    out_specs = (P("seq", "head"), P("seq", None), P("seq", None))
    body = functools.partial(shards, mesh.shape["seq"], mesh.shape["head"])
    return jax.shard_map(body, mesh=mesh, in_specs=in_specs, out_specs=out_specs, check_vma=False)
```

```python
import functools

import jax
import jax.numpy as jnp
from jax import lax
from jax.experimental import pallas as pl
from jax.experimental.pallas import tpu as pltpu
from jax.sharding import PartitionSpec as P

PRECISE = lax.Precision.HIGHEST
MESH = pl.DeviceIdType.MESH


def nt_dot(p, q):
    return lax.dot_general(p, q, (((1,), (1,)), ((), ())), preferred_element_type=jnp.float32)


def nt_dot_f32(p, q):
    ph = p.astype(jnp.bfloat16)
    pl_ = (p - ph.astype(jnp.float32)).astype(jnp.bfloat16)
    qh = q.astype(jnp.bfloat16)
    ql = (q - qh.astype(jnp.float32)).astype(jnp.bfloat16)
    return nt_dot(ph, qh) + (nt_dot(ph, ql) + nt_dot(pl_, qh))


def scan_kernel(rows_n, width, groups, pack_ref, dcol_ref, x_ref, dy_ref, cr_ref, cc_ref,
                b_ref, c_ref, gv_ref, sum_ref, run_ref, dx_ref, xs_ref, ds_ref, recv1, rdec,
                win, out3, recv3, full, parts, gather1, gather2, send1, rsem1, send2, rsem2, send3, rsem3,
                local, dsend, drecv, hsend1, hrecv1, hsend2, hrecv2, sc_ref, pdec_ref,
                early):
    me = lax.axis_index("seq")
    col = lax.axis_index("head")
    c = me % width
    y = me // width
    piece = recv1.shape[1] // 2
    spans = [1, 2, 3, 4]

    length = x_ref.shape[0]
    pdec_ref[...] = jnp.broadcast_to(dcol_ref[...], pdec_ref.shape)
    later = lax.broadcasted_iota(jnp.int32, (length, length), 1) >= lax.broadcasted_iota(
        jnp.int32, (length, length), 0)
    run_ref[...] = jnp.zeros(run_ref.shape, run_ref.dtype)

    def head(h):
        gaps = cr_ref[h:h + 1, :] - cc_ref[:, h:h + 1]

        dec = jnp.where(later, jnp.exp(jnp.where(later, gaps, 0.0)), 0.0)
        mix = (sc_ref[...] * dec).astype(jnp.bfloat16)
        lanes = slice(h * hd, (h + 1) * hd)
        dy_h = dy_ref[:, lanes]
        x_h = x_ref[:, lanes]
        xs_ref[:, lanes] = x_h.astype(jnp.float32) * cc_ref[:, nh + h:nh + h + 1]
        ds_ref[:, lanes] = dy_h.astype(jnp.float32) * cc_ref[:, 2 * nh + h:2 * nh + h + 1]
        dx_ref[:, lanes] = jnp.dot(mix, dy_h, preferred_element_type=jnp.float32)
        pairs = lax.dot_general(
            x_h, dy_h, (((1,), (1,)), ((), ())), preferred_element_type=jnp.float32)
        run_ref[...] += dec * pairs

    nh = cr_ref.shape[0]
    heads_left = list(range(nh))
    hd = x_ref.shape[1] // cr_ref.shape[0]

    def heads(k):
        for _ in range(k):
            if heads_left:
                head(heads_left.pop(0))

    barrier = pltpu.get_barrier_semaphore()
    for off in range(1, width):
        peer = y * width + (c + off) % width
        pl.semaphore_signal(barrier, inc=1, device_id=(peer, col), device_id_type=MESH)
    for d in spans:
        @pl.when(y + d < rows_n)
        def _():
            pl.semaphore_signal(barrier, inc=1, device_id=(me + d * width, col), device_id_type=MESH)

        @pl.when(y - d >= 0)
        def _():
            pl.semaphore_signal(barrier, inc=1, device_id=(me - d * width, col), device_id_type=MESH)
    z = lax.axis_index("head")
    for off in range(1, groups):
        pl.semaphore_signal(
            barrier, inc=1, device_id=(me, (z + off) % groups), device_id_type=MESH)
    peers = width - 1 + groups - 1
    for d in spans:
        peers = peers + ((rows_n - 1 - y) // d + rows_n - 1) // rows_n + (y // d + rows_n - 1) // rows_n
    sc_ref[...] = nt_dot(b_ref[...], c_ref[...])
    heads(2)
    pl.semaphore_wait(barrier, peers)

    own = pltpu.make_async_copy(pack_ref.at[c], recv1.at[c], local.at[0])
    own.start()
    own_dec = pltpu.make_async_copy(pdec_ref, rdec.at[c], local.at[2])
    own_dec.start()
    sends = []
    for off in range(1, width):
        k = (c + off) % width
        cp = pltpu.make_async_remote_copy(
            src_ref=pack_ref.at[k], dst_ref=recv1.at[c], send_sem=send1.at[off],
            recv_sem=rsem1.at[off], device_id=(y * width + k, col), device_id_type=MESH)
        cp.start()
        sends.append(cp)
        cp = pltpu.make_async_remote_copy(
            src_ref=pdec_ref, dst_ref=rdec.at[c], send_sem=dsend.at[off],
            recv_sem=drecv.at[off], device_id=(y * width + k, col), device_id_type=MESH)
        cp.start()
        sends.append(cp)
    heads(3)
    for off in range(1, width):
        k = (c + width - off) % width
        pltpu.make_async_remote_copy(
            src_ref=pack_ref.at[k], dst_ref=recv1.at[k], send_sem=send1.at[off],
            recv_sem=rsem1.at[off], device_id=(y * width + k, col), device_id_type=MESH).wait_recv()
        pltpu.make_async_remote_copy(
            src_ref=pdec_ref, dst_ref=rdec.at[k], send_sem=dsend.at[off],
            recv_sem=drecv.at[off], device_id=(y * width + k, col), device_id_type=MESH).wait_recv()
    own.wait()
    own_dec.wait()
    for cp in sends:
        cp.wait_send()

    def decay(i):
        return rdec[i, 0:1, :]

    fwd_e, fwd_g = [None] * width, [None] * width
    e = jnp.zeros((piece, recv1.shape[2]), jnp.float32)
    g = jnp.ones((1, recv1.shape[2]), jnp.float32)
    for i in range(width):
        fwd_e[i], fwd_g[i] = e, g
        a = decay(i)
        e = a * e + recv1[i, :piece, :].astype(jnp.float32)
        g = g * a
    bwd_e, bwd_g = [None] * width, [None] * width
    f = jnp.zeros((piece, recv1.shape[2]), jnp.float32)
    h = jnp.ones((1, recv1.shape[2]), jnp.float32)
    for i in reversed(range(width)):
        bwd_e[i], bwd_g[i] = f, h
        a = decay(i)
        f = a * f + recv1[i, piece:2 * piece, :].astype(jnp.float32)
        h = h * a
    win[0, 0, :piece, :] = e
    win[0, 0, piece:, :] = jnp.broadcast_to(g, (win.shape[2] - piece, g.shape[1]))
    win[1, 0, :piece, :] = f
    win[1, 0, piece:, :] = jnp.broadcast_to(h, (win.shape[2] - piece, h.shape[1]))

    def combine(w_near, w_far):
        a = w_near[piece:, :]
        return w_near[:piece, :] + jnp.broadcast_to(a[:1], (piece, a.shape[1])) * w_far[:piece, :], a * w_far[piece:, :]

    def copy2(way, slot, src_slot, target, sem):
        return pltpu.make_async_remote_copy(
            src_ref=win.at[way, src_slot], dst_ref=win.at[way, slot], send_sem=send2.at[way, sem],
            recv_sem=rsem2.at[way, sem], device_id=(target, col), device_id_type=MESH)

    def exists(row):
        return jnp.logical_and(row >= 0, row < rows_n)

    near = [1, 2, 3]
    for way, sign in ((0, 1), (1, -1)):
        for k in near:
            @pl.when(exists(y + sign * k))
            def _():
                copy2(way, k, 0, me + sign * k * width, k - 1).start()
    heads(2)
    for way, sign in ((0, 1), (1, -1)):
        win[way, 4] = jnp.zeros(win.shape[2:], win.dtype)
        for k in near:
            @pl.when(exists(y - sign * k))
            def _():
                copy2(way, k, 0, me - sign * k * width, k - 1).wait_recv()
                s_new, a_new = combine(win[way, 4], win[way, k])
                if k == 1:
                    win[way, 4] = win[way, 1]
                else:
                    win[way, 4, :piece, :] = s_new
                    win[way, 4, piece:, :] = a_new
        s_inc, a_inc = combine(win[way, 0], win[way, 4])
        win[way, 5, :piece, :] = s_inc
        win[way, 5, piece:, :] = a_inc

        @pl.when(exists(y + sign * 4))
        def _():
            copy2(way, 6, 5, me + sign * 4 * width, 3).start()
    heads(len(heads_left))
    for way, sign in ((0, 1), (1, -1)):
        @pl.when(exists(y - sign * 4))
        def _():
            copy2(way, 6, 5, me - sign * 4 * width, 3).wait_recv()
            s_new, a_new = combine(win[way, 4], win[way, 6])
            win[way, 7, :piece, :] = s_new
            win[way, 7, piece:, :] = a_new

        @pl.when(jnp.logical_not(exists(y - sign * 4)))
        def _():
            win[way, 7] = win[way, 4]
    for way, sign in ((0, 1), (1, -1)):
        for k in near:
            @pl.when(exists(y + sign * k))
            def _():
                copy2(way, k, 0, me + sign * k * width, k - 1).wait_send()

        @pl.when(exists(y + sign * 4))
        def _():
            copy2(way, 6, 5, me + sign * 4 * width, 3).wait_send()
    entering = win[0, 7, :piece, :]
    leaving = win[1, 7, :piece, :]

    for i in range(width):
        out3[i, :piece, :] = (fwd_e[i] + fwd_g[i] * entering).astype(out3.dtype)
        out3[i, piece:, :] = (bwd_e[i] + bwd_g[i] * leaving).astype(out3.dtype)
    own = pltpu.make_async_copy(out3.at[c], recv3.at[c], local.at[1])
    own.start()
    sends = []
    for off in range(1, width):
        k = (c + off) % width
        cp = pltpu.make_async_remote_copy(
            src_ref=out3.at[k], dst_ref=recv3.at[c], send_sem=send3.at[off],
            recv_sem=rsem3.at[off], device_id=(y * width + k, col), device_id_type=MESH)
        cp.start()
        sends.append(cp)
    weighted = run_ref[...].astype(jnp.bfloat16)
    early[0] = jnp.dot(weighted, c_ref[...], preferred_element_type=jnp.float32)
    early[1] = lax.dot_general(
        weighted, b_ref[...], (((0,), (0,)), ((), ())), preferred_element_type=jnp.float32)
    for off in range(1, width):
        k = (c + width - off) % width
        pltpu.make_async_remote_copy(
            src_ref=out3.at[k], dst_ref=recv3.at[k], send_sem=send3.at[off],
            recv_sem=rsem3.at[off], device_id=(y * width + k, col), device_id_type=MESH).wait_recv()
    own.wait()
    for cp in sends:
        cp.wait_send()

    s = width * piece
    for k in range(width):
        full[0, k * piece:(k + 1) * piece, :] = recv3[k, :piece, :].astype(jnp.float32)
        full[1, k * piece:(k + 1) * piece, :] = recv3[k, piece:, :].astype(jnp.float32)
    part_b = early[0] + nt_dot_f32(xs_ref[...], full[1])
    part_c = early[1] + nt_dot_f32(ds_ref[...], full[0])
    n_rows = part_b.shape[0]
    parts[:n_rows, :] = part_b.astype(parts.dtype)
    parts[n_rows:, :] = part_c.astype(parts.dtype)
    rows = gather1.shape[1]

    def chunk(i):
        return parts.at[pl.ds(pl.multiple_of(i * rows, rows), rows)]

    sends = []
    for k in range(1, groups):
        peer = (z + k) % groups
        cp = pltpu.make_async_remote_copy(
            src_ref=chunk(peer), dst_ref=gather1.at[z], send_sem=hsend1.at[k],
            recv_sem=hrecv1.at[k], device_id=(me, peer), device_id_type=MESH)
        cp.start()
        sends.append(cp)
    adj = full[1]
    adj_hi = adj.astype(jnp.bfloat16)
    adj_lo = (adj - adj_hi.astype(jnp.float32)).astype(jnp.bfloat16)
    b_adj = jnp.dot(b_ref[...], adj_hi, preferred_element_type=jnp.float32) + jnp.dot(
        b_ref[...], adj_lo, preferred_element_type=jnp.float32)
    for h in range(cr_ref.shape[0]):
        lanes = slice(h * hd, (h + 1) * hd)
        gv_ref[:, lanes] = (dx_ref[:, lanes] + cc_ref[:, nh + h:nh + h + 1] * b_adj[:, lanes]).astype(
            gv_ref.dtype)
    total = parts[pl.ds(pl.multiple_of(z * rows, rows), rows), :].astype(jnp.float32)
    for k in range(1, groups):
        source = (z + groups - k) % groups
        pltpu.make_async_remote_copy(
            src_ref=chunk(source), dst_ref=gather1.at[source], send_sem=hsend1.at[k],
            recv_sem=hrecv1.at[k], device_id=(me, source), device_id_type=MESH).wait_recv()
        total = total + gather1[source].astype(jnp.float32)
    for cp in sends:
        cp.wait_send()
    gather2[z] = total.astype(gather2.dtype)
    sends = []
    for k in range(1, groups):
        peer = (z + k) % groups
        cp = pltpu.make_async_remote_copy(
            src_ref=gather2.at[z], dst_ref=gather2.at[z], send_sem=hsend2.at[k],
            recv_sem=hrecv2.at[k], device_id=(me, peer), device_id_type=MESH)
        cp.start()
        sends.append(cp)
    for k in range(1, groups):
        source = (z + groups - k) % groups
        pltpu.make_async_remote_copy(
            src_ref=gather2.at[source], dst_ref=gather2.at[source], send_sem=hsend2.at[k],
            recv_sem=hrecv2.at[k], device_id=(me, source), device_id_type=MESH).wait_recv()
    for cp in sends:
        cp.wait_send()
    sum_ref[...] = gather2[...]


def exclusive_scans(count, groups, decay_cols, forward, backward, x, dy, cumulative,
                    into_end, from_start, b_inputs, c_inputs):
    s, w = forward.shape
    width = 8 if count % 8 == 0 else 1
    rows_n = count // width
    piece = s // width
    assert rows_n <= 8
    pack = jnp.concatenate(
        [forward.reshape(width, piece, w), backward.reshape(width, piece, w)], axis=1
    ).astype(jnp.bfloat16)
    length = x.shape[0]
    chunk_rows = 2 * length // groups
    columns = jnp.concatenate([cumulative, into_end, from_start], axis=0).T
    grad_values, sums = pl.pallas_call(
        functools.partial(scan_kernel, rows_n, width, groups),
        out_shape=(
            jax.ShapeDtypeStruct(x.shape, jnp.bfloat16),
            jax.ShapeDtypeStruct((groups, chunk_rows, s), jnp.bfloat16),
        ),
        in_specs=[pl.BlockSpec(memory_space=pltpu.VMEM)] * 8,
        out_specs=(pl.BlockSpec(memory_space=pltpu.VMEM),) * 2,
        scratch_shapes=[
            pltpu.VMEM((length, length), jnp.float32),
            pltpu.VMEM(x.shape, jnp.float32),
            pltpu.VMEM(x.shape, jnp.float32),
            pltpu.VMEM(x.shape, jnp.float32),
            pltpu.VMEM((width, 2 * piece, w), jnp.bfloat16),
            pltpu.VMEM((width, 8, w), jnp.float32),
            pltpu.VMEM((2, 8, piece + 8, w), jnp.float32),
            pltpu.VMEM((width, 2 * piece, w), jnp.bfloat16),
            pltpu.VMEM((width, 2 * piece, w), jnp.bfloat16),
            pltpu.VMEM((2, s, w), jnp.float32),
            pltpu.VMEM((2 * length, s), jnp.bfloat16),
            pltpu.VMEM((groups, chunk_rows, s), jnp.bfloat16),
            pltpu.VMEM((groups, chunk_rows, s), jnp.bfloat16),
            pltpu.SemaphoreType.DMA((width,)),
            pltpu.SemaphoreType.DMA((width,)),
            pltpu.SemaphoreType.DMA((2, 4)),
            pltpu.SemaphoreType.DMA((2, 4)),
            pltpu.SemaphoreType.DMA((width,)),
            pltpu.SemaphoreType.DMA((width,)),
            pltpu.SemaphoreType.DMA((3,)),
            pltpu.SemaphoreType.DMA((width,)),
            pltpu.SemaphoreType.DMA((width,)),
            pltpu.SemaphoreType.DMA((groups,)),
            pltpu.SemaphoreType.DMA((groups,)),
            pltpu.SemaphoreType.DMA((groups,)),
            pltpu.SemaphoreType.DMA((groups,)),
            pltpu.VMEM((length, length), jnp.float32),
            pltpu.VMEM((8, w), jnp.float32),
            pltpu.VMEM((2, length, s), jnp.float32),
        ],
        compiler_params=pltpu.CompilerParams(collective_id=1, has_side_effects=True),
    )(pack, decay_cols, x, dy, cumulative, columns, b_inputs, c_inputs)
    sums = sums.reshape(2 * length, s)
    return grad_values, sums[:length], sums[length:]


def shards(count, groups, token_values, b_inputs, c_inputs, log_decay, grad_out):
    length = token_values.shape[0]
    heads_here = log_decay.shape[0]
    head_dim = token_values.shape[1] // heads_here
    state_size = b_inputs.shape[1]
    positions = lax.iota(jnp.int32, length)
    upto = (positions[:, None] <= positions[None, :]).astype(jnp.float32)
    cumulative = jnp.dot(log_decay, upto, precision=PRECISE)
    block_log = cumulative[:, -1]
    into_end = jnp.exp(block_log[:, None] - cumulative)
    from_start = jnp.exp(cumulative)
    block_decay = jnp.exp(block_log)
    b_float = b_inputs.astype(jnp.float32)
    c_float = c_inputs.astype(jnp.float32)
    decayed_b = (into_end[:, :, None] * b_float[None]).astype(jnp.bfloat16)
    decayed_c = (from_start[:, :, None] * c_float[None]).astype(jnp.bfloat16)
    x_heads = token_values.reshape(length, heads_here, head_dim)
    dy_heads = grad_out.reshape(length, heads_here, head_dim)
    state_local = jnp.einsum(
        "htn,thp->nhp", decayed_b, x_heads, preferred_element_type=jnp.float32
    ).reshape(state_size, heads_here * head_dim)
    adjoint_local = jnp.einsum(
        "hsn,shp->nhp", decayed_c, dy_heads, preferred_element_type=jnp.float32
    ).reshape(state_size, heads_here * head_dim)
    decay_cols = jnp.repeat(block_decay, head_dim)[None, :]
    grad_values, grad_b, grad_c = exclusive_scans(
        count, groups, decay_cols, state_local, adjoint_local, token_values, grad_out,
        cumulative, into_end, from_start, b_inputs, c_inputs,
    )
    return grad_values, grad_b, grad_c


def solution(mesh):
    in_specs = (
        P("seq", "head"),
        P("seq", None),
        P("seq", None),
        P("head", "seq"),
        P("seq", "head"),
    )
    out_specs = (P("seq", "head"), P("seq", None), P("seq", None))
    body = functools.partial(shards, mesh.shape["seq"], mesh.shape["head"])
    return jax.shard_map(body, mesh=mesh, in_specs=in_specs, out_specs=out_specs, check_vma=False)
```

```python
import functools

import jax
import jax.numpy as jnp
from jax import lax
from jax.experimental import pallas as pl
from jax.experimental.pallas import tpu as pltpu
from jax.sharding import PartitionSpec as P

PRECISE = lax.Precision.HIGHEST
MESH = pl.DeviceIdType.MESH


def nt_dot(p, q):
    return lax.dot_general(p, q, (((1,), (1,)), ((), ())), preferred_element_type=jnp.float32)


def nt_dot_f32(p, q):
    ph = p.astype(jnp.bfloat16)
    pl_ = (p - ph.astype(jnp.float32)).astype(jnp.bfloat16)
    qh = q.astype(jnp.bfloat16)
    ql = (q - qh.astype(jnp.float32)).astype(jnp.bfloat16)
    return nt_dot(ph, qh) + (nt_dot(ph, ql) + nt_dot(pl_, qh))


def scan_kernel(rows_n, width, groups, fwd_ref, bwd_ref, x_ref, dy_ref, cr_ref, cc_ref,
                b_ref, c_ref, gv_ref, sum_ref, run_ref, dx_ref, xs_ref, ds_ref, recv1, rdec,
                win, out3, recv3, full, parts, gather1, gather2, send1, rsem1, send2, rsem2, send3, rsem3,
                local, dsend, drecv, hsend1, hrecv1, hsend2, hrecv2, sc_ref, pdec_ref,
                early, pack_ref):
    me = lax.axis_index("seq")
    col = lax.axis_index("head")
    c = me % width
    y = me // width
    piece = recv1.shape[1] // 2
    spans = [1, 2, 3, 4]

    length = x_ref.shape[0]
    later = lax.broadcasted_iota(jnp.int32, (length, length), 1) >= lax.broadcasted_iota(
        jnp.int32, (length, length), 0)
    run_ref[...] = jnp.zeros(run_ref.shape, run_ref.dtype)

    def head(h):
        gaps = cr_ref[h:h + 1, :] - cc_ref[:, h:h + 1]

        dec = jnp.where(later, jnp.exp(jnp.where(later, gaps, 0.0)), 0.0)
        mix = (sc_ref[...] * dec).astype(jnp.bfloat16)
        lanes = slice(h * hd, (h + 1) * hd)
        dy_h = dy_ref[:, lanes]
        x_h = x_ref[:, lanes]
        xs_ref[:, lanes] = x_h.astype(jnp.float32) * cc_ref[:, nh + h:nh + h + 1]
        ds_ref[:, lanes] = dy_h.astype(jnp.float32) * cc_ref[:, 2 * nh + h:2 * nh + h + 1]
        dx_ref[:, lanes] = jnp.dot(mix, dy_h, preferred_element_type=jnp.float32)
        pairs = lax.dot_general(
            x_h, dy_h, (((1,), (1,)), ((), ())), preferred_element_type=jnp.float32)
        run_ref[...] += dec * pairs

    nh = cr_ref.shape[0]
    heads_left = list(range(nh))
    hd = x_ref.shape[1] // cr_ref.shape[0]
    for h in range(nh):
        pdec_ref[:, h * hd:(h + 1) * hd] = jnp.broadcast_to(
            jnp.exp(cc_ref[length - 1:length, h:h + 1]), (pdec_ref.shape[0], hd))
    span = pack_ref.shape[1] // 2
    for k in range(pack_ref.shape[0]):
        pack_ref[k, :span, :] = fwd_ref[k * span:(k + 1) * span, :].astype(pack_ref.dtype)
        pack_ref[k, span:, :] = bwd_ref[k * span:(k + 1) * span, :].astype(pack_ref.dtype)

    def heads(k):
        for _ in range(k):
            if heads_left:
                head(heads_left.pop(0))

    barrier = pltpu.get_barrier_semaphore()
    for off in range(1, width):
        peer = y * width + (c + off) % width
        pl.semaphore_signal(barrier, inc=1, device_id=(peer, col), device_id_type=MESH)
    for d in spans:
        @pl.when(y + d < rows_n)
        def _():
            pl.semaphore_signal(barrier, inc=1, device_id=(me + d * width, col), device_id_type=MESH)

        @pl.when(y - d >= 0)
        def _():
            pl.semaphore_signal(barrier, inc=1, device_id=(me - d * width, col), device_id_type=MESH)
    z = lax.axis_index("head")
    for off in range(1, groups):
        pl.semaphore_signal(
            barrier, inc=1, device_id=(me, (z + off) % groups), device_id_type=MESH)
    peers = width - 1 + groups - 1
    for d in spans:
        peers = peers + ((rows_n - 1 - y) // d + rows_n - 1) // rows_n + (y // d + rows_n - 1) // rows_n
    sc_ref[...] = nt_dot(b_ref[...], c_ref[...])
    heads(2)
    pl.semaphore_wait(barrier, peers)

    own = pltpu.make_async_copy(pack_ref.at[c], recv1.at[c], local.at[0])
    own.start()
    own_dec = pltpu.make_async_copy(pdec_ref, rdec.at[c], local.at[2])
    own_dec.start()
    sends = []
    for off in range(1, width):
        k = (c + off) % width
        cp = pltpu.make_async_remote_copy(
            src_ref=pack_ref.at[k], dst_ref=recv1.at[c], send_sem=send1.at[off],
            recv_sem=rsem1.at[off], device_id=(y * width + k, col), device_id_type=MESH)
        cp.start()
        sends.append(cp)
        cp = pltpu.make_async_remote_copy(
            src_ref=pdec_ref, dst_ref=rdec.at[c], send_sem=dsend.at[off],
            recv_sem=drecv.at[off], device_id=(y * width + k, col), device_id_type=MESH)
        cp.start()
        sends.append(cp)
    heads(3)
    for off in range(1, width):
        k = (c + width - off) % width
        pltpu.make_async_remote_copy(
            src_ref=pack_ref.at[k], dst_ref=recv1.at[k], send_sem=send1.at[off],
            recv_sem=rsem1.at[off], device_id=(y * width + k, col), device_id_type=MESH).wait_recv()
        pltpu.make_async_remote_copy(
            src_ref=pdec_ref, dst_ref=rdec.at[k], send_sem=dsend.at[off],
            recv_sem=drecv.at[off], device_id=(y * width + k, col), device_id_type=MESH).wait_recv()
    own.wait()
    own_dec.wait()
    for cp in sends:
        cp.wait_send()

    def decay(i):
        return rdec[i, 0:1, :]

    fwd_e, fwd_g = [None] * width, [None] * width
    e = jnp.zeros((piece, recv1.shape[2]), jnp.float32)
    g = jnp.ones((1, recv1.shape[2]), jnp.float32)
    for i in range(width):
        fwd_e[i], fwd_g[i] = e, g
        a = decay(i)
        e = a * e + recv1[i, :piece, :].astype(jnp.float32)
        g = g * a
    bwd_e, bwd_g = [None] * width, [None] * width
    f = jnp.zeros((piece, recv1.shape[2]), jnp.float32)
    h = jnp.ones((1, recv1.shape[2]), jnp.float32)
    for i in reversed(range(width)):
        bwd_e[i], bwd_g[i] = f, h
        a = decay(i)
        f = a * f + recv1[i, piece:2 * piece, :].astype(jnp.float32)
        h = h * a
    win[0, 0, :piece, :] = e
    win[0, 0, piece:, :] = jnp.broadcast_to(g, (win.shape[2] - piece, g.shape[1]))
    win[1, 0, :piece, :] = f
    win[1, 0, piece:, :] = jnp.broadcast_to(h, (win.shape[2] - piece, h.shape[1]))

    def combine(w_near, w_far):
        a = w_near[piece:, :]
        return w_near[:piece, :] + jnp.broadcast_to(a[:1], (piece, a.shape[1])) * w_far[:piece, :], a * w_far[piece:, :]

    def copy2(way, slot, src_slot, target, sem):
        return pltpu.make_async_remote_copy(
            src_ref=win.at[way, src_slot], dst_ref=win.at[way, slot], send_sem=send2.at[way, sem],
            recv_sem=rsem2.at[way, sem], device_id=(target, col), device_id_type=MESH)

    def exists(row):
        return jnp.logical_and(row >= 0, row < rows_n)

    near = [1, 2, 3]
    for way, sign in ((0, 1), (1, -1)):
        for k in near:
            @pl.when(exists(y + sign * k))
            def _():
                copy2(way, k, 0, me + sign * k * width, k - 1).start()
    heads(2)
    for way, sign in ((0, 1), (1, -1)):
        win[way, 4] = jnp.zeros(win.shape[2:], win.dtype)
        for k in near:
            @pl.when(exists(y - sign * k))
            def _():
                copy2(way, k, 0, me - sign * k * width, k - 1).wait_recv()
                s_new, a_new = combine(win[way, 4], win[way, k])
                if k == 1:
                    win[way, 4] = win[way, 1]
                else:
                    win[way, 4, :piece, :] = s_new
                    win[way, 4, piece:, :] = a_new
        s_inc, a_inc = combine(win[way, 0], win[way, 4])
        win[way, 5, :piece, :] = s_inc
        win[way, 5, piece:, :] = a_inc

        @pl.when(exists(y + sign * 4))
        def _():
            copy2(way, 6, 5, me + sign * 4 * width, 3).start()
    heads(len(heads_left))
    for way, sign in ((0, 1), (1, -1)):
        @pl.when(exists(y - sign * 4))
        def _():
            copy2(way, 6, 5, me - sign * 4 * width, 3).wait_recv()
            s_new, a_new = combine(win[way, 4], win[way, 6])
            win[way, 7, :piece, :] = s_new
            win[way, 7, piece:, :] = a_new

        @pl.when(jnp.logical_not(exists(y - sign * 4)))
        def _():
            win[way, 7] = win[way, 4]
    for way, sign in ((0, 1), (1, -1)):
        for k in near:
            @pl.when(exists(y + sign * k))
            def _():
                copy2(way, k, 0, me + sign * k * width, k - 1).wait_send()

        @pl.when(exists(y + sign * 4))
        def _():
            copy2(way, 6, 5, me + sign * 4 * width, 3).wait_send()
    entering = win[0, 7, :piece, :]
    leaving = win[1, 7, :piece, :]

    for i in range(width):
        out3[i, :piece, :] = (fwd_e[i] + fwd_g[i] * entering).astype(out3.dtype)
        out3[i, piece:, :] = (bwd_e[i] + bwd_g[i] * leaving).astype(out3.dtype)
    own = pltpu.make_async_copy(out3.at[c], recv3.at[c], local.at[1])
    own.start()
    sends = []
    for off in range(1, width):
        k = (c + off) % width
        cp = pltpu.make_async_remote_copy(
            src_ref=out3.at[k], dst_ref=recv3.at[c], send_sem=send3.at[off],
            recv_sem=rsem3.at[off], device_id=(y * width + k, col), device_id_type=MESH)
        cp.start()
        sends.append(cp)
    weighted = run_ref[...].astype(jnp.bfloat16)
    early[0] = jnp.dot(weighted, c_ref[...], preferred_element_type=jnp.float32)
    early[1] = lax.dot_general(
        weighted, b_ref[...], (((0,), (0,)), ((), ())), preferred_element_type=jnp.float32)
    for off in range(1, width):
        k = (c + width - off) % width
        pltpu.make_async_remote_copy(
            src_ref=out3.at[k], dst_ref=recv3.at[k], send_sem=send3.at[off],
            recv_sem=rsem3.at[off], device_id=(y * width + k, col), device_id_type=MESH).wait_recv()
    own.wait()
    for cp in sends:
        cp.wait_send()

    s = width * piece
    for k in range(width):
        full[0, k * piece:(k + 1) * piece, :] = recv3[k, :piece, :].astype(jnp.float32)
        full[1, k * piece:(k + 1) * piece, :] = recv3[k, piece:, :].astype(jnp.float32)
    part_b = early[0] + nt_dot_f32(xs_ref[...], full[1])
    part_c = early[1] + nt_dot_f32(ds_ref[...], full[0])
    n_rows = part_b.shape[0]
    parts[:n_rows, :] = part_b.astype(parts.dtype)
    parts[n_rows:, :] = part_c.astype(parts.dtype)
    rows = gather1.shape[1]

    def chunk(i):
        return parts.at[pl.ds(pl.multiple_of(i * rows, rows), rows)]

    sends = []
    for k in range(1, groups):
        peer = (z + k) % groups
        cp = pltpu.make_async_remote_copy(
            src_ref=chunk(peer), dst_ref=gather1.at[z], send_sem=hsend1.at[k],
            recv_sem=hrecv1.at[k], device_id=(me, peer), device_id_type=MESH)
        cp.start()
        sends.append(cp)
    adj = full[1]
    adj_hi = adj.astype(jnp.bfloat16)
    adj_lo = (adj - adj_hi.astype(jnp.float32)).astype(jnp.bfloat16)
    b_adj = jnp.dot(b_ref[...], adj_hi, preferred_element_type=jnp.float32) + jnp.dot(
        b_ref[...], adj_lo, preferred_element_type=jnp.float32)
    for h in range(cr_ref.shape[0]):
        lanes = slice(h * hd, (h + 1) * hd)
        gv_ref[:, lanes] = (dx_ref[:, lanes] + cc_ref[:, nh + h:nh + h + 1] * b_adj[:, lanes]).astype(
            gv_ref.dtype)
    total = parts[pl.ds(pl.multiple_of(z * rows, rows), rows), :].astype(jnp.float32)
    for k in range(1, groups):
        source = (z + groups - k) % groups
        pltpu.make_async_remote_copy(
            src_ref=chunk(source), dst_ref=gather1.at[source], send_sem=hsend1.at[k],
            recv_sem=hrecv1.at[k], device_id=(me, source), device_id_type=MESH).wait_recv()
        total = total + gather1[source].astype(jnp.float32)
    for cp in sends:
        cp.wait_send()
    gather2[z] = total.astype(gather2.dtype)
    sends = []
    for k in range(1, groups):
        peer = (z + k) % groups
        cp = pltpu.make_async_remote_copy(
            src_ref=gather2.at[z], dst_ref=gather2.at[z], send_sem=hsend2.at[k],
            recv_sem=hrecv2.at[k], device_id=(me, peer), device_id_type=MESH)
        cp.start()
        sends.append(cp)
    for k in range(1, groups):
        source = (z + groups - k) % groups
        pltpu.make_async_remote_copy(
            src_ref=gather2.at[source], dst_ref=gather2.at[source], send_sem=hsend2.at[k],
            recv_sem=hrecv2.at[k], device_id=(me, source), device_id_type=MESH).wait_recv()
    for cp in sends:
        cp.wait_send()
    sum_ref[...] = gather2[...]


def exclusive_scans(count, groups, decay_cols, forward, backward, x, dy, cumulative,
                    into_end, from_start, b_inputs, c_inputs):
    s, w = forward.shape
    width = 8 if count % 8 == 0 else 1
    rows_n = count // width
    piece = s // width
    assert rows_n <= 8
    length = x.shape[0]
    chunk_rows = 2 * length // groups
    columns = jnp.concatenate([cumulative, into_end, from_start], axis=0).T
    grad_values, sums = pl.pallas_call(
        functools.partial(scan_kernel, rows_n, width, groups),
        out_shape=(
            jax.ShapeDtypeStruct(x.shape, jnp.bfloat16),
            jax.ShapeDtypeStruct((groups, chunk_rows, s), jnp.bfloat16),
        ),
        in_specs=[pl.BlockSpec(memory_space=pltpu.VMEM)] * 8,
        out_specs=(pl.BlockSpec(memory_space=pltpu.VMEM),) * 2,
        scratch_shapes=[
            pltpu.VMEM((length, length), jnp.float32),
            pltpu.VMEM(x.shape, jnp.float32),
            pltpu.VMEM(x.shape, jnp.float32),
            pltpu.VMEM(x.shape, jnp.float32),
            pltpu.VMEM((width, 2 * piece, w), jnp.bfloat16),
            pltpu.VMEM((width, 8, w), jnp.float32),
            pltpu.VMEM((2, 8, piece + 8, w), jnp.float32),
            pltpu.VMEM((width, 2 * piece, w), jnp.bfloat16),
            pltpu.VMEM((width, 2 * piece, w), jnp.bfloat16),
            pltpu.VMEM((2, s, w), jnp.float32),
            pltpu.VMEM((2 * length, s), jnp.bfloat16),
            pltpu.VMEM((groups, chunk_rows, s), jnp.bfloat16),
            pltpu.VMEM((groups, chunk_rows, s), jnp.bfloat16),
            pltpu.SemaphoreType.DMA((width,)),
            pltpu.SemaphoreType.DMA((width,)),
            pltpu.SemaphoreType.DMA((2, 4)),
            pltpu.SemaphoreType.DMA((2, 4)),
            pltpu.SemaphoreType.DMA((width,)),
            pltpu.SemaphoreType.DMA((width,)),
            pltpu.SemaphoreType.DMA((3,)),
            pltpu.SemaphoreType.DMA((width,)),
            pltpu.SemaphoreType.DMA((width,)),
            pltpu.SemaphoreType.DMA((groups,)),
            pltpu.SemaphoreType.DMA((groups,)),
            pltpu.SemaphoreType.DMA((groups,)),
            pltpu.SemaphoreType.DMA((groups,)),
            pltpu.VMEM((length, length), jnp.float32),
            pltpu.VMEM((8, w), jnp.float32),
            pltpu.VMEM((2, length, s), jnp.float32),
            pltpu.VMEM((width, 2 * piece, w), jnp.bfloat16),
        ],
        compiler_params=pltpu.CompilerParams(collective_id=1, has_side_effects=True),
    )(forward, backward, x, dy, cumulative, columns, b_inputs, c_inputs)
    sums = sums.reshape(2 * length, s)
    return grad_values, sums[:length], sums[length:]


def shards(count, groups, token_values, b_inputs, c_inputs, log_decay, grad_out):
    length = token_values.shape[0]
    heads_here = log_decay.shape[0]
    head_dim = token_values.shape[1] // heads_here
    state_size = b_inputs.shape[1]
    positions = lax.iota(jnp.int32, length)
    upto = (positions[:, None] <= positions[None, :]).astype(jnp.float32)
    cumulative = jnp.dot(log_decay, upto, precision=PRECISE)
    block_log = cumulative[:, -1]
    into_end = jnp.exp(block_log[:, None] - cumulative)
    from_start = jnp.exp(cumulative)
    block_decay = jnp.exp(block_log)
    b_float = b_inputs.astype(jnp.float32)
    c_float = c_inputs.astype(jnp.float32)
    decayed_b = (into_end[:, :, None] * b_float[None]).astype(jnp.bfloat16)
    decayed_c = (from_start[:, :, None] * c_float[None]).astype(jnp.bfloat16)
    x_heads = token_values.reshape(length, heads_here, head_dim)
    dy_heads = grad_out.reshape(length, heads_here, head_dim)
    state_local = jnp.einsum(
        "htn,thp->nhp", decayed_b, x_heads, preferred_element_type=jnp.float32
    ).reshape(state_size, heads_here * head_dim)
    adjoint_local = jnp.einsum(
        "hsn,shp->nhp", decayed_c, dy_heads, preferred_element_type=jnp.float32
    ).reshape(state_size, heads_here * head_dim)
    decay_cols = jnp.repeat(block_decay, head_dim)[None, :]
    grad_values, grad_b, grad_c = exclusive_scans(
        count, groups, decay_cols, state_local, adjoint_local, token_values, grad_out,
        cumulative, into_end, from_start, b_inputs, c_inputs,
    )
    return grad_values, grad_b, grad_c


def solution(mesh):
    in_specs = (
        P("seq", "head"),
        P("seq", None),
        P("seq", None),
        P("head", "seq"),
        P("seq", "head"),
    )
    out_specs = (P("seq", "head"), P("seq", None), P("seq", None))
    body = functools.partial(shards, mesh.shape["seq"], mesh.shape["head"])
    return jax.shard_map(body, mesh=mesh, in_specs=in_specs, out_specs=out_specs, check_vma=False)
```

```python
import functools

import jax
import jax.numpy as jnp
from jax import lax
from jax.experimental import pallas as pl
from jax.experimental.pallas import tpu as pltpu
from jax.sharding import PartitionSpec as P

PRECISE = lax.Precision.HIGHEST
MESH = pl.DeviceIdType.MESH


def nt_dot(p, q):
    return lax.dot_general(p, q, (((1,), (1,)), ((), ())), preferred_element_type=jnp.float32)


def nt_dot_f32(p, q):
    ph = p.astype(jnp.bfloat16)
    pl_ = (p - ph.astype(jnp.float32)).astype(jnp.bfloat16)
    qh = q.astype(jnp.bfloat16)
    ql = (q - qh.astype(jnp.float32)).astype(jnp.bfloat16)
    return nt_dot(ph, qh) + (nt_dot(ph, ql) + nt_dot(pl_, qh))


def scan_kernel(rows_n, width, groups, x_ref, dy_ref, cr_ref, cc_ref,
                b_ref, c_ref, gv_ref, sum_ref, run_ref, dx_ref, xs_ref, ds_ref, recv1, rdec,
                win, out3, recv3, full, parts, gather1, gather2, send1, rsem1, send2, rsem2, send3, rsem3,
                local, dsend, drecv, hsend1, hrecv1, hsend2, hrecv2, sc_ref, pdec_ref,
                early, pack_ref, local_ref):
    me = lax.axis_index("seq")
    col = lax.axis_index("head")
    c = me % width
    y = me // width
    piece = recv1.shape[1] // 2
    spans = [1, 2, 3, 4]

    length = x_ref.shape[0]
    later = lax.broadcasted_iota(jnp.int32, (length, length), 1) >= lax.broadcasted_iota(
        jnp.int32, (length, length), 0)
    run_ref[...] = jnp.zeros(run_ref.shape, run_ref.dtype)

    def head(h):
        gaps = cr_ref[h:h + 1, :] - cc_ref[:, h:h + 1]

        dec = jnp.where(later, jnp.exp(jnp.where(later, gaps, 0.0)), 0.0)
        mix = (sc_ref[...] * dec).astype(jnp.bfloat16)
        lanes = slice(h * hd, (h + 1) * hd)
        dy_h = dy_ref[:, lanes]
        x_h = x_ref[:, lanes]
        xs_ref[:, lanes] = x_h.astype(jnp.float32) * cc_ref[:, nh + h:nh + h + 1]
        ds_ref[:, lanes] = dy_h.astype(jnp.float32) * cc_ref[:, 2 * nh + h:2 * nh + h + 1]
        dx_ref[:, lanes] = jnp.dot(mix, dy_h, preferred_element_type=jnp.float32)
        pairs = lax.dot_general(
            x_h, dy_h, (((1,), (1,)), ((), ())), preferred_element_type=jnp.float32)
        run_ref[...] += dec * pairs

    nh = cr_ref.shape[0]
    heads_left = list(range(nh))
    hd = x_ref.shape[1] // cr_ref.shape[0]
    for h in range(nh):
        pdec_ref[:, h * hd:(h + 1) * hd] = jnp.broadcast_to(
            jnp.exp(cc_ref[length - 1:length, h:h + 1]), (pdec_ref.shape[0], hd))
    b_all = b_ref[...].astype(jnp.float32)
    c_all = c_ref[...].astype(jnp.float32)
    for h in range(nh):
        lanes = slice(h * hd, (h + 1) * hd)
        decayed_b = (cc_ref[:, nh + h:nh + h + 1] * b_all).astype(jnp.bfloat16)
        decayed_c = (cc_ref[:, 2 * nh + h:2 * nh + h + 1] * c_all).astype(jnp.bfloat16)
        local_ref[0, :, lanes] = lax.dot_general(
            decayed_b, x_ref[:, lanes], (((0,), (0,)), ((), ())), preferred_element_type=jnp.float32)
        local_ref[1, :, lanes] = lax.dot_general(
            decayed_c, dy_ref[:, lanes], (((0,), (0,)), ((), ())), preferred_element_type=jnp.float32)
    span = pack_ref.shape[1] // 2
    for k in range(pack_ref.shape[0]):
        pack_ref[k, :span, :] = local_ref[0, k * span:(k + 1) * span, :].astype(pack_ref.dtype)
        pack_ref[k, span:, :] = local_ref[1, k * span:(k + 1) * span, :].astype(pack_ref.dtype)

    def heads(k):
        for _ in range(k):
            if heads_left:
                head(heads_left.pop(0))

    barrier = pltpu.get_barrier_semaphore()
    for off in range(1, width):
        peer = y * width + (c + off) % width
        pl.semaphore_signal(barrier, inc=1, device_id=(peer, col), device_id_type=MESH)
    for d in spans:
        @pl.when(y + d < rows_n)
        def _():
            pl.semaphore_signal(barrier, inc=1, device_id=(me + d * width, col), device_id_type=MESH)

        @pl.when(y - d >= 0)
        def _():
            pl.semaphore_signal(barrier, inc=1, device_id=(me - d * width, col), device_id_type=MESH)
    z = lax.axis_index("head")
    for off in range(1, groups):
        pl.semaphore_signal(
            barrier, inc=1, device_id=(me, (z + off) % groups), device_id_type=MESH)
    peers = width - 1 + groups - 1
    for d in spans:
        peers = peers + ((rows_n - 1 - y) // d + rows_n - 1) // rows_n + (y // d + rows_n - 1) // rows_n
    sc_ref[...] = nt_dot(b_ref[...], c_ref[...])
    heads(2)
    pl.semaphore_wait(barrier, peers)

    own = pltpu.make_async_copy(pack_ref.at[c], recv1.at[c], local.at[0])
    own.start()
    own_dec = pltpu.make_async_copy(pdec_ref, rdec.at[c], local.at[2])
    own_dec.start()
    sends = []
    for off in range(1, width):
        k = (c + off) % width
        cp = pltpu.make_async_remote_copy(
            src_ref=pack_ref.at[k], dst_ref=recv1.at[c], send_sem=send1.at[off],
            recv_sem=rsem1.at[off], device_id=(y * width + k, col), device_id_type=MESH)
        cp.start()
        sends.append(cp)
        cp = pltpu.make_async_remote_copy(
            src_ref=pdec_ref, dst_ref=rdec.at[c], send_sem=dsend.at[off],
            recv_sem=drecv.at[off], device_id=(y * width + k, col), device_id_type=MESH)
        cp.start()
        sends.append(cp)
    heads(3)
    for off in range(1, width):
        k = (c + width - off) % width
        pltpu.make_async_remote_copy(
            src_ref=pack_ref.at[k], dst_ref=recv1.at[k], send_sem=send1.at[off],
            recv_sem=rsem1.at[off], device_id=(y * width + k, col), device_id_type=MESH).wait_recv()
        pltpu.make_async_remote_copy(
            src_ref=pdec_ref, dst_ref=rdec.at[k], send_sem=dsend.at[off],
            recv_sem=drecv.at[off], device_id=(y * width + k, col), device_id_type=MESH).wait_recv()
    own.wait()
    own_dec.wait()
    for cp in sends:
        cp.wait_send()

    def decay(i):
        return rdec[i, 0:1, :]

    fwd_e, fwd_g = [None] * width, [None] * width
    e = jnp.zeros((piece, recv1.shape[2]), jnp.float32)
    g = jnp.ones((1, recv1.shape[2]), jnp.float32)
    for i in range(width):
        fwd_e[i], fwd_g[i] = e, g
        a = decay(i)
        e = a * e + recv1[i, :piece, :].astype(jnp.float32)
        g = g * a
    bwd_e, bwd_g = [None] * width, [None] * width
    f = jnp.zeros((piece, recv1.shape[2]), jnp.float32)
    h = jnp.ones((1, recv1.shape[2]), jnp.float32)
    for i in reversed(range(width)):
        bwd_e[i], bwd_g[i] = f, h
        a = decay(i)
        f = a * f + recv1[i, piece:2 * piece, :].astype(jnp.float32)
        h = h * a
    win[0, 0, :piece, :] = e
    win[0, 0, piece:, :] = jnp.broadcast_to(g, (win.shape[2] - piece, g.shape[1]))
    win[1, 0, :piece, :] = f
    win[1, 0, piece:, :] = jnp.broadcast_to(h, (win.shape[2] - piece, h.shape[1]))

    def combine(w_near, w_far):
        a = w_near[piece:, :]
        return w_near[:piece, :] + jnp.broadcast_to(a[:1], (piece, a.shape[1])) * w_far[:piece, :], a * w_far[piece:, :]

    def copy2(way, slot, src_slot, target, sem):
        return pltpu.make_async_remote_copy(
            src_ref=win.at[way, src_slot], dst_ref=win.at[way, slot], send_sem=send2.at[way, sem],
            recv_sem=rsem2.at[way, sem], device_id=(target, col), device_id_type=MESH)

    def exists(row):
        return jnp.logical_and(row >= 0, row < rows_n)

    near = [1, 2, 3]
    for way, sign in ((0, 1), (1, -1)):
        for k in near:
            @pl.when(exists(y + sign * k))
            def _():
                copy2(way, k, 0, me + sign * k * width, k - 1).start()
    heads(2)
    for way, sign in ((0, 1), (1, -1)):
        win[way, 4] = jnp.zeros(win.shape[2:], win.dtype)
        for k in near:
            @pl.when(exists(y - sign * k))
            def _():
                copy2(way, k, 0, me - sign * k * width, k - 1).wait_recv()
                s_new, a_new = combine(win[way, 4], win[way, k])
                if k == 1:
                    win[way, 4] = win[way, 1]
                else:
                    win[way, 4, :piece, :] = s_new
                    win[way, 4, piece:, :] = a_new
        s_inc, a_inc = combine(win[way, 0], win[way, 4])
        win[way, 5, :piece, :] = s_inc
        win[way, 5, piece:, :] = a_inc

        @pl.when(exists(y + sign * 4))
        def _():
            copy2(way, 6, 5, me + sign * 4 * width, 3).start()
    heads(len(heads_left))
    for way, sign in ((0, 1), (1, -1)):
        @pl.when(exists(y - sign * 4))
        def _():
            copy2(way, 6, 5, me - sign * 4 * width, 3).wait_recv()
            s_new, a_new = combine(win[way, 4], win[way, 6])
            win[way, 7, :piece, :] = s_new
            win[way, 7, piece:, :] = a_new

        @pl.when(jnp.logical_not(exists(y - sign * 4)))
        def _():
            win[way, 7] = win[way, 4]
    for way, sign in ((0, 1), (1, -1)):
        for k in near:
            @pl.when(exists(y + sign * k))
            def _():
                copy2(way, k, 0, me + sign * k * width, k - 1).wait_send()

        @pl.when(exists(y + sign * 4))
        def _():
            copy2(way, 6, 5, me + sign * 4 * width, 3).wait_send()
    entering = win[0, 7, :piece, :]
    leaving = win[1, 7, :piece, :]

    for i in range(width):
        out3[i, :piece, :] = (fwd_e[i] + fwd_g[i] * entering).astype(out3.dtype)
        out3[i, piece:, :] = (bwd_e[i] + bwd_g[i] * leaving).astype(out3.dtype)
    own = pltpu.make_async_copy(out3.at[c], recv3.at[c], local.at[1])
    own.start()
    sends = []
    for off in range(1, width):
        k = (c + off) % width
        cp = pltpu.make_async_remote_copy(
            src_ref=out3.at[k], dst_ref=recv3.at[c], send_sem=send3.at[off],
            recv_sem=rsem3.at[off], device_id=(y * width + k, col), device_id_type=MESH)
        cp.start()
        sends.append(cp)
    weighted = run_ref[...].astype(jnp.bfloat16)
    early[0] = jnp.dot(weighted, c_ref[...], preferred_element_type=jnp.float32)
    early[1] = lax.dot_general(
        weighted, b_ref[...], (((0,), (0,)), ((), ())), preferred_element_type=jnp.float32)
    for off in range(1, width):
        k = (c + width - off) % width
        pltpu.make_async_remote_copy(
            src_ref=out3.at[k], dst_ref=recv3.at[k], send_sem=send3.at[off],
            recv_sem=rsem3.at[off], device_id=(y * width + k, col), device_id_type=MESH).wait_recv()
    own.wait()
    for cp in sends:
        cp.wait_send()

    s = width * piece
    for k in range(width):
        full[0, k * piece:(k + 1) * piece, :] = recv3[k, :piece, :].astype(jnp.float32)
        full[1, k * piece:(k + 1) * piece, :] = recv3[k, piece:, :].astype(jnp.float32)
    part_b = early[0] + nt_dot_f32(xs_ref[...], full[1])
    part_c = early[1] + nt_dot_f32(ds_ref[...], full[0])
    n_rows = part_b.shape[0]
    parts[:n_rows, :] = part_b.astype(parts.dtype)
    parts[n_rows:, :] = part_c.astype(parts.dtype)
    rows = gather1.shape[1]

    def chunk(i):
        return parts.at[pl.ds(pl.multiple_of(i * rows, rows), rows)]

    sends = []
    for k in range(1, groups):
        peer = (z + k) % groups
        cp = pltpu.make_async_remote_copy(
            src_ref=chunk(peer), dst_ref=gather1.at[z], send_sem=hsend1.at[k],
            recv_sem=hrecv1.at[k], device_id=(me, peer), device_id_type=MESH)
        cp.start()
        sends.append(cp)
    adj = full[1]
    adj_hi = adj.astype(jnp.bfloat16)
    adj_lo = (adj - adj_hi.astype(jnp.float32)).astype(jnp.bfloat16)
    b_adj = jnp.dot(b_ref[...], adj_hi, preferred_element_type=jnp.float32) + jnp.dot(
        b_ref[...], adj_lo, preferred_element_type=jnp.float32)
    for h in range(cr_ref.shape[0]):
        lanes = slice(h * hd, (h + 1) * hd)
        gv_ref[:, lanes] = (dx_ref[:, lanes] + cc_ref[:, nh + h:nh + h + 1] * b_adj[:, lanes]).astype(
            gv_ref.dtype)
    total = parts[pl.ds(pl.multiple_of(z * rows, rows), rows), :].astype(jnp.float32)
    for k in range(1, groups):
        source = (z + groups - k) % groups
        pltpu.make_async_remote_copy(
            src_ref=chunk(source), dst_ref=gather1.at[source], send_sem=hsend1.at[k],
            recv_sem=hrecv1.at[k], device_id=(me, source), device_id_type=MESH).wait_recv()
        total = total + gather1[source].astype(jnp.float32)
    for cp in sends:
        cp.wait_send()
    gather2[z] = total.astype(gather2.dtype)
    sends = []
    for k in range(1, groups):
        peer = (z + k) % groups
        cp = pltpu.make_async_remote_copy(
            src_ref=gather2.at[z], dst_ref=gather2.at[z], send_sem=hsend2.at[k],
            recv_sem=hrecv2.at[k], device_id=(me, peer), device_id_type=MESH)
        cp.start()
        sends.append(cp)
    for k in range(1, groups):
        source = (z + groups - k) % groups
        pltpu.make_async_remote_copy(
            src_ref=gather2.at[source], dst_ref=gather2.at[source], send_sem=hsend2.at[k],
            recv_sem=hrecv2.at[k], device_id=(me, source), device_id_type=MESH).wait_recv()
    for cp in sends:
        cp.wait_send()
    sum_ref[...] = gather2[...]


def exclusive_scans(count, groups, decay_cols, forward, backward, x, dy, cumulative,
                    into_end, from_start, b_inputs, c_inputs):
    s, w = forward.shape
    width = 8 if count % 8 == 0 else 1
    rows_n = count // width
    piece = s // width
    assert rows_n <= 8
    length = x.shape[0]
    chunk_rows = 2 * length // groups
    columns = jnp.concatenate([cumulative, into_end, from_start], axis=0).T
    grad_values, sums = pl.pallas_call(
        functools.partial(scan_kernel, rows_n, width, groups),
        out_shape=(
            jax.ShapeDtypeStruct(x.shape, jnp.bfloat16),
            jax.ShapeDtypeStruct((groups, chunk_rows, s), jnp.bfloat16),
        ),
        in_specs=[pl.BlockSpec(memory_space=pltpu.VMEM)] * 6,
        out_specs=(pl.BlockSpec(memory_space=pltpu.VMEM),) * 2,
        scratch_shapes=[
            pltpu.VMEM((length, length), jnp.float32),
            pltpu.VMEM(x.shape, jnp.float32),
            pltpu.VMEM(x.shape, jnp.float32),
            pltpu.VMEM(x.shape, jnp.float32),
            pltpu.VMEM((width, 2 * piece, w), jnp.bfloat16),
            pltpu.VMEM((width, 8, w), jnp.float32),
            pltpu.VMEM((2, 8, piece + 8, w), jnp.float32),
            pltpu.VMEM((width, 2 * piece, w), jnp.bfloat16),
            pltpu.VMEM((width, 2 * piece, w), jnp.bfloat16),
            pltpu.VMEM((2, s, w), jnp.float32),
            pltpu.VMEM((2 * length, s), jnp.bfloat16),
            pltpu.VMEM((groups, chunk_rows, s), jnp.bfloat16),
            pltpu.VMEM((groups, chunk_rows, s), jnp.bfloat16),
            pltpu.SemaphoreType.DMA((width,)),
            pltpu.SemaphoreType.DMA((width,)),
            pltpu.SemaphoreType.DMA((2, 4)),
            pltpu.SemaphoreType.DMA((2, 4)),
            pltpu.SemaphoreType.DMA((width,)),
            pltpu.SemaphoreType.DMA((width,)),
            pltpu.SemaphoreType.DMA((3,)),
            pltpu.SemaphoreType.DMA((width,)),
            pltpu.SemaphoreType.DMA((width,)),
            pltpu.SemaphoreType.DMA((groups,)),
            pltpu.SemaphoreType.DMA((groups,)),
            pltpu.SemaphoreType.DMA((groups,)),
            pltpu.SemaphoreType.DMA((groups,)),
            pltpu.VMEM((length, length), jnp.float32),
            pltpu.VMEM((8, w), jnp.float32),
            pltpu.VMEM((2, length, s), jnp.float32),
            pltpu.VMEM((width, 2 * piece, w), jnp.bfloat16),
            pltpu.VMEM((2, s, w), jnp.float32),
        ],
        compiler_params=pltpu.CompilerParams(collective_id=1, has_side_effects=True),
    )(x, dy, cumulative, columns, b_inputs, c_inputs)
    sums = sums.reshape(2 * length, s)
    return grad_values, sums[:length], sums[length:]


def shards(count, groups, token_values, b_inputs, c_inputs, log_decay, grad_out):
    length = token_values.shape[0]
    heads_here = log_decay.shape[0]
    head_dim = token_values.shape[1] // heads_here
    state_size = b_inputs.shape[1]
    positions = lax.iota(jnp.int32, length)
    upto = (positions[:, None] <= positions[None, :]).astype(jnp.float32)
    cumulative = jnp.dot(log_decay, upto, precision=PRECISE)
    block_log = cumulative[:, -1]
    into_end = jnp.exp(block_log[:, None] - cumulative)
    from_start = jnp.exp(cumulative)
    block_decay = jnp.exp(block_log)
    b_float = b_inputs.astype(jnp.float32)
    c_float = c_inputs.astype(jnp.float32)
    decayed_b = (into_end[:, :, None] * b_float[None]).astype(jnp.bfloat16)
    decayed_c = (from_start[:, :, None] * c_float[None]).astype(jnp.bfloat16)
    x_heads = token_values.reshape(length, heads_here, head_dim)
    dy_heads = grad_out.reshape(length, heads_here, head_dim)
    state_local = jnp.einsum(
        "htn,thp->nhp", decayed_b, x_heads, preferred_element_type=jnp.float32
    ).reshape(state_size, heads_here * head_dim)
    adjoint_local = jnp.einsum(
        "hsn,shp->nhp", decayed_c, dy_heads, preferred_element_type=jnp.float32
    ).reshape(state_size, heads_here * head_dim)
    decay_cols = jnp.repeat(block_decay, head_dim)[None, :]
    grad_values, grad_b, grad_c = exclusive_scans(
        count, groups, decay_cols, state_local, adjoint_local, token_values, grad_out,
        cumulative, into_end, from_start, b_inputs, c_inputs,
    )
    return grad_values, grad_b, grad_c


def solution(mesh):
    in_specs = (
        P("seq", "head"),
        P("seq", None),
        P("seq", None),
        P("head", "seq"),
        P("seq", "head"),
    )
    out_specs = (P("seq", "head"), P("seq", None), P("seq", None))
    body = functools.partial(shards, mesh.shape["seq"], mesh.shape["head"])
    return jax.shard_map(body, mesh=mesh, in_specs=in_specs, out_specs=out_specs, check_vma=False)
```

```python
import functools

import jax
import jax.numpy as jnp
from jax import lax
from jax.experimental import pallas as pl
from jax.experimental.pallas import tpu as pltpu
from jax.sharding import PartitionSpec as P

PRECISE = lax.Precision.HIGHEST
MESH = pl.DeviceIdType.MESH


def nt_dot(p, q):
    return lax.dot_general(p, q, (((1,), (1,)), ((), ())), preferred_element_type=jnp.float32)


def nt_dot_f32(p, q):
    ph = p.astype(jnp.bfloat16)
    pl_ = (p - ph.astype(jnp.float32)).astype(jnp.bfloat16)
    qh = q.astype(jnp.bfloat16)
    ql = (q - qh.astype(jnp.float32)).astype(jnp.bfloat16)
    return nt_dot(ph, qh) + (nt_dot(ph, ql) + nt_dot(pl_, qh))


def scan_kernel(rows_n, width, groups, x_ref, dy_ref, cr_ref,
                b_ref, c_ref, gv_ref, sum_ref, run_ref, dx_ref, xs_ref, ds_ref, recv1, rdec,
                win, out3, recv3, full, parts, gather1, gather2, send1, rsem1, send2, rsem2, send3, rsem3,
                local, dsend, drecv, hsend1, hrecv1, hsend2, hrecv2, sc_ref, pdec_ref,
                early, pack_ref, local_ref, cc_ref):
    me = lax.axis_index("seq")
    col = lax.axis_index("head")
    c = me % width
    y = me // width
    piece = recv1.shape[1] // 2
    spans = [1, 2, 3, 4]

    length = x_ref.shape[0]
    cc_ref[...] = cr_ref[...].T
    later = lax.broadcasted_iota(jnp.int32, (length, length), 1) >= lax.broadcasted_iota(
        jnp.int32, (length, length), 0)
    run_ref[...] = jnp.zeros(run_ref.shape, run_ref.dtype)

    def head(h):
        gaps = cr_ref[h:h + 1, :] - cc_ref[:, h:h + 1]

        dec = jnp.where(later, jnp.exp(jnp.where(later, gaps, 0.0)), 0.0)
        mix = (sc_ref[...] * dec).astype(jnp.bfloat16)
        lanes = slice(h * hd, (h + 1) * hd)
        dy_h = dy_ref[:, lanes]
        x_h = x_ref[:, lanes]
        xs_ref[:, lanes] = x_h.astype(jnp.float32) * cc_ref[:, nh + h:nh + h + 1]
        ds_ref[:, lanes] = dy_h.astype(jnp.float32) * cc_ref[:, 2 * nh + h:2 * nh + h + 1]
        dx_ref[:, lanes] = jnp.dot(mix, dy_h, preferred_element_type=jnp.float32)
        pairs = lax.dot_general(
            x_h, dy_h, (((1,), (1,)), ((), ())), preferred_element_type=jnp.float32)
        run_ref[...] += dec * pairs

    nh = cr_ref.shape[0] // 3
    heads_left = list(range(nh))
    hd = x_ref.shape[1] // nh
    for h in range(nh):
        pdec_ref[:, h * hd:(h + 1) * hd] = jnp.broadcast_to(
            jnp.exp(cc_ref[length - 1:length, h:h + 1]), (pdec_ref.shape[0], hd))
    b_all = b_ref[...].astype(jnp.float32)
    c_all = c_ref[...].astype(jnp.float32)
    for h in range(nh):
        lanes = slice(h * hd, (h + 1) * hd)
        decayed_b = (cc_ref[:, nh + h:nh + h + 1] * b_all).astype(jnp.bfloat16)
        decayed_c = (cc_ref[:, 2 * nh + h:2 * nh + h + 1] * c_all).astype(jnp.bfloat16)
        local_ref[0, :, lanes] = lax.dot_general(
            decayed_b, x_ref[:, lanes], (((0,), (0,)), ((), ())), preferred_element_type=jnp.float32)
        local_ref[1, :, lanes] = lax.dot_general(
            decayed_c, dy_ref[:, lanes], (((0,), (0,)), ((), ())), preferred_element_type=jnp.float32)
    span = pack_ref.shape[1] // 2
    for k in range(pack_ref.shape[0]):
        pack_ref[k, :span, :] = local_ref[0, k * span:(k + 1) * span, :].astype(pack_ref.dtype)
        pack_ref[k, span:, :] = local_ref[1, k * span:(k + 1) * span, :].astype(pack_ref.dtype)

    def heads(k):
        for _ in range(k):
            if heads_left:
                head(heads_left.pop(0))

    barrier = pltpu.get_barrier_semaphore()
    for off in range(1, width):
        peer = y * width + (c + off) % width
        pl.semaphore_signal(barrier, inc=1, device_id=(peer, col), device_id_type=MESH)
    for d in spans:
        @pl.when(y + d < rows_n)
        def _():
            pl.semaphore_signal(barrier, inc=1, device_id=(me + d * width, col), device_id_type=MESH)

        @pl.when(y - d >= 0)
        def _():
            pl.semaphore_signal(barrier, inc=1, device_id=(me - d * width, col), device_id_type=MESH)
    z = lax.axis_index("head")
    for off in range(1, groups):
        pl.semaphore_signal(
            barrier, inc=1, device_id=(me, (z + off) % groups), device_id_type=MESH)
    peers = width - 1 + groups - 1
    for d in spans:
        peers = peers + ((rows_n - 1 - y) // d + rows_n - 1) // rows_n + (y // d + rows_n - 1) // rows_n
    sc_ref[...] = nt_dot(b_ref[...], c_ref[...])
    heads(2)
    pl.semaphore_wait(barrier, peers)

    own = pltpu.make_async_copy(pack_ref.at[c], recv1.at[c], local.at[0])
    own.start()
    own_dec = pltpu.make_async_copy(pdec_ref, rdec.at[c], local.at[2])
    own_dec.start()
    sends = []
    for off in range(1, width):
        k = (c + off) % width
        cp = pltpu.make_async_remote_copy(
            src_ref=pack_ref.at[k], dst_ref=recv1.at[c], send_sem=send1.at[off],
            recv_sem=rsem1.at[off], device_id=(y * width + k, col), device_id_type=MESH)
        cp.start()
        sends.append(cp)
        cp = pltpu.make_async_remote_copy(
            src_ref=pdec_ref, dst_ref=rdec.at[c], send_sem=dsend.at[off],
            recv_sem=drecv.at[off], device_id=(y * width + k, col), device_id_type=MESH)
        cp.start()
        sends.append(cp)
    heads(3)
    for off in range(1, width):
        k = (c + width - off) % width
        pltpu.make_async_remote_copy(
            src_ref=pack_ref.at[k], dst_ref=recv1.at[k], send_sem=send1.at[off],
            recv_sem=rsem1.at[off], device_id=(y * width + k, col), device_id_type=MESH).wait_recv()
        pltpu.make_async_remote_copy(
            src_ref=pdec_ref, dst_ref=rdec.at[k], send_sem=dsend.at[off],
            recv_sem=drecv.at[off], device_id=(y * width + k, col), device_id_type=MESH).wait_recv()
    own.wait()
    own_dec.wait()
    for cp in sends:
        cp.wait_send()

    def decay(i):
        return rdec[i, 0:1, :]

    fwd_e, fwd_g = [None] * width, [None] * width
    e = jnp.zeros((piece, recv1.shape[2]), jnp.float32)
    g = jnp.ones((1, recv1.shape[2]), jnp.float32)
    for i in range(width):
        fwd_e[i], fwd_g[i] = e, g
        a = decay(i)
        e = a * e + recv1[i, :piece, :].astype(jnp.float32)
        g = g * a
    bwd_e, bwd_g = [None] * width, [None] * width
    f = jnp.zeros((piece, recv1.shape[2]), jnp.float32)
    h = jnp.ones((1, recv1.shape[2]), jnp.float32)
    for i in reversed(range(width)):
        bwd_e[i], bwd_g[i] = f, h
        a = decay(i)
        f = a * f + recv1[i, piece:2 * piece, :].astype(jnp.float32)
        h = h * a
    win[0, 0, :piece, :] = e
    win[0, 0, piece:, :] = jnp.broadcast_to(g, (win.shape[2] - piece, g.shape[1]))
    win[1, 0, :piece, :] = f
    win[1, 0, piece:, :] = jnp.broadcast_to(h, (win.shape[2] - piece, h.shape[1]))

    def combine(w_near, w_far):
        a = w_near[piece:, :]
        return w_near[:piece, :] + jnp.broadcast_to(a[:1], (piece, a.shape[1])) * w_far[:piece, :], a * w_far[piece:, :]

    def copy2(way, slot, src_slot, target, sem):
        return pltpu.make_async_remote_copy(
            src_ref=win.at[way, src_slot], dst_ref=win.at[way, slot], send_sem=send2.at[way, sem],
            recv_sem=rsem2.at[way, sem], device_id=(target, col), device_id_type=MESH)

    def exists(row):
        return jnp.logical_and(row >= 0, row < rows_n)

    near = [1, 2, 3]
    for way, sign in ((0, 1), (1, -1)):
        for k in near:
            @pl.when(exists(y + sign * k))
            def _():
                copy2(way, k, 0, me + sign * k * width, k - 1).start()
    heads(2)
    for way, sign in ((0, 1), (1, -1)):
        win[way, 4] = jnp.zeros(win.shape[2:], win.dtype)
        for k in near:
            @pl.when(exists(y - sign * k))
            def _():
                copy2(way, k, 0, me - sign * k * width, k - 1).wait_recv()
                s_new, a_new = combine(win[way, 4], win[way, k])
                if k == 1:
                    win[way, 4] = win[way, 1]
                else:
                    win[way, 4, :piece, :] = s_new
                    win[way, 4, piece:, :] = a_new
        s_inc, a_inc = combine(win[way, 0], win[way, 4])
        win[way, 5, :piece, :] = s_inc
        win[way, 5, piece:, :] = a_inc

        @pl.when(exists(y + sign * 4))
        def _():
            copy2(way, 6, 5, me + sign * 4 * width, 3).start()
    heads(len(heads_left))
    for way, sign in ((0, 1), (1, -1)):
        @pl.when(exists(y - sign * 4))
        def _():
            copy2(way, 6, 5, me - sign * 4 * width, 3).wait_recv()
            s_new, a_new = combine(win[way, 4], win[way, 6])
            win[way, 7, :piece, :] = s_new
            win[way, 7, piece:, :] = a_new

        @pl.when(jnp.logical_not(exists(y - sign * 4)))
        def _():
            win[way, 7] = win[way, 4]
    for way, sign in ((0, 1), (1, -1)):
        for k in near:
            @pl.when(exists(y + sign * k))
            def _():
                copy2(way, k, 0, me + sign * k * width, k - 1).wait_send()

        @pl.when(exists(y + sign * 4))
        def _():
            copy2(way, 6, 5, me + sign * 4 * width, 3).wait_send()
    entering = win[0, 7, :piece, :]
    leaving = win[1, 7, :piece, :]

    for i in range(width):
        out3[i, :piece, :] = (fwd_e[i] + fwd_g[i] * entering).astype(out3.dtype)
        out3[i, piece:, :] = (bwd_e[i] + bwd_g[i] * leaving).astype(out3.dtype)
    own = pltpu.make_async_copy(out3.at[c], recv3.at[c], local.at[1])
    own.start()
    sends = []
    for off in range(1, width):
        k = (c + off) % width
        cp = pltpu.make_async_remote_copy(
            src_ref=out3.at[k], dst_ref=recv3.at[c], send_sem=send3.at[off],
            recv_sem=rsem3.at[off], device_id=(y * width + k, col), device_id_type=MESH)
        cp.start()
        sends.append(cp)
    weighted = run_ref[...].astype(jnp.bfloat16)
    early[0] = jnp.dot(weighted, c_ref[...], preferred_element_type=jnp.float32)
    early[1] = lax.dot_general(
        weighted, b_ref[...], (((0,), (0,)), ((), ())), preferred_element_type=jnp.float32)
    for off in range(1, width):
        k = (c + width - off) % width
        pltpu.make_async_remote_copy(
            src_ref=out3.at[k], dst_ref=recv3.at[k], send_sem=send3.at[off],
            recv_sem=rsem3.at[off], device_id=(y * width + k, col), device_id_type=MESH).wait_recv()
    own.wait()
    for cp in sends:
        cp.wait_send()

    s = width * piece
    for k in range(width):
        full[0, k * piece:(k + 1) * piece, :] = recv3[k, :piece, :].astype(jnp.float32)
        full[1, k * piece:(k + 1) * piece, :] = recv3[k, piece:, :].astype(jnp.float32)
    part_b = early[0] + nt_dot_f32(xs_ref[...], full[1])
    part_c = early[1] + nt_dot_f32(ds_ref[...], full[0])
    n_rows = part_b.shape[0]
    parts[:n_rows, :] = part_b.astype(parts.dtype)
    parts[n_rows:, :] = part_c.astype(parts.dtype)
    rows = gather1.shape[1]

    def chunk(i):
        return parts.at[pl.ds(pl.multiple_of(i * rows, rows), rows)]

    sends = []
    for k in range(1, groups):
        peer = (z + k) % groups
        cp = pltpu.make_async_remote_copy(
            src_ref=chunk(peer), dst_ref=gather1.at[z], send_sem=hsend1.at[k],
            recv_sem=hrecv1.at[k], device_id=(me, peer), device_id_type=MESH)
        cp.start()
        sends.append(cp)
    adj = full[1]
    adj_hi = adj.astype(jnp.bfloat16)
    adj_lo = (adj - adj_hi.astype(jnp.float32)).astype(jnp.bfloat16)
    b_adj = jnp.dot(b_ref[...], adj_hi, preferred_element_type=jnp.float32) + jnp.dot(
        b_ref[...], adj_lo, preferred_element_type=jnp.float32)
    for h in range(nh):
        lanes = slice(h * hd, (h + 1) * hd)
        gv_ref[:, lanes] = (dx_ref[:, lanes] + cc_ref[:, nh + h:nh + h + 1] * b_adj[:, lanes]).astype(
            gv_ref.dtype)
    total = parts[pl.ds(pl.multiple_of(z * rows, rows), rows), :].astype(jnp.float32)
    for k in range(1, groups):
        source = (z + groups - k) % groups
        pltpu.make_async_remote_copy(
            src_ref=chunk(source), dst_ref=gather1.at[source], send_sem=hsend1.at[k],
            recv_sem=hrecv1.at[k], device_id=(me, source), device_id_type=MESH).wait_recv()
        total = total + gather1[source].astype(jnp.float32)
    for cp in sends:
        cp.wait_send()
    gather2[z] = total.astype(gather2.dtype)
    sends = []
    for k in range(1, groups):
        peer = (z + k) % groups
        cp = pltpu.make_async_remote_copy(
            src_ref=gather2.at[z], dst_ref=gather2.at[z], send_sem=hsend2.at[k],
            recv_sem=hrecv2.at[k], device_id=(me, peer), device_id_type=MESH)
        cp.start()
        sends.append(cp)
    for k in range(1, groups):
        source = (z + groups - k) % groups
        pltpu.make_async_remote_copy(
            src_ref=gather2.at[source], dst_ref=gather2.at[source], send_sem=hsend2.at[k],
            recv_sem=hrecv2.at[k], device_id=(me, source), device_id_type=MESH).wait_recv()
    for cp in sends:
        cp.wait_send()
    sum_ref[...] = gather2[...]


def exclusive_scans(count, groups, decay_cols, forward, backward, x, dy, cumulative,
                    into_end, from_start, b_inputs, c_inputs):
    s, w = forward.shape
    width = 8 if count % 8 == 0 else 1
    rows_n = count // width
    piece = s // width
    assert rows_n <= 8
    length = x.shape[0]
    chunk_rows = 2 * length // groups
    stacked = jnp.concatenate([cumulative, into_end, from_start], axis=0)
    grad_values, sums = pl.pallas_call(
        functools.partial(scan_kernel, rows_n, width, groups),
        out_shape=(
            jax.ShapeDtypeStruct(x.shape, jnp.bfloat16),
            jax.ShapeDtypeStruct((groups, chunk_rows, s), jnp.bfloat16),
        ),
        in_specs=[pl.BlockSpec(memory_space=pltpu.VMEM)] * 5,
        out_specs=(pl.BlockSpec(memory_space=pltpu.VMEM),) * 2,
        scratch_shapes=[
            pltpu.VMEM((length, length), jnp.float32),
            pltpu.VMEM(x.shape, jnp.float32),
            pltpu.VMEM(x.shape, jnp.float32),
            pltpu.VMEM(x.shape, jnp.float32),
            pltpu.VMEM((width, 2 * piece, w), jnp.bfloat16),
            pltpu.VMEM((width, 8, w), jnp.float32),
            pltpu.VMEM((2, 8, piece + 8, w), jnp.float32),
            pltpu.VMEM((width, 2 * piece, w), jnp.bfloat16),
            pltpu.VMEM((width, 2 * piece, w), jnp.bfloat16),
            pltpu.VMEM((2, s, w), jnp.float32),
            pltpu.VMEM((2 * length, s), jnp.bfloat16),
            pltpu.VMEM((groups, chunk_rows, s), jnp.bfloat16),
            pltpu.VMEM((groups, chunk_rows, s), jnp.bfloat16),
            pltpu.SemaphoreType.DMA((width,)),
            pltpu.SemaphoreType.DMA((width,)),
            pltpu.SemaphoreType.DMA((2, 4)),
            pltpu.SemaphoreType.DMA((2, 4)),
            pltpu.SemaphoreType.DMA((width,)),
            pltpu.SemaphoreType.DMA((width,)),
            pltpu.SemaphoreType.DMA((3,)),
            pltpu.SemaphoreType.DMA((width,)),
            pltpu.SemaphoreType.DMA((width,)),
            pltpu.SemaphoreType.DMA((groups,)),
            pltpu.SemaphoreType.DMA((groups,)),
            pltpu.SemaphoreType.DMA((groups,)),
            pltpu.SemaphoreType.DMA((groups,)),
            pltpu.VMEM((length, length), jnp.float32),
            pltpu.VMEM((8, w), jnp.float32),
            pltpu.VMEM((2, length, s), jnp.float32),
            pltpu.VMEM((width, 2 * piece, w), jnp.bfloat16),
            pltpu.VMEM((2, s, w), jnp.float32),
            pltpu.VMEM((length, 3 * cumulative.shape[0]), jnp.float32),
        ],
        compiler_params=pltpu.CompilerParams(collective_id=1, has_side_effects=True),
    )(x, dy, stacked, b_inputs, c_inputs)
    sums = sums.reshape(2 * length, s)
    return grad_values, sums[:length], sums[length:]


def shards(count, groups, token_values, b_inputs, c_inputs, log_decay, grad_out):
    length = token_values.shape[0]
    heads_here = log_decay.shape[0]
    head_dim = token_values.shape[1] // heads_here
    state_size = b_inputs.shape[1]
    positions = lax.iota(jnp.int32, length)
    upto = (positions[:, None] <= positions[None, :]).astype(jnp.float32)
    cumulative = jnp.dot(log_decay, upto, precision=PRECISE)
    block_log = cumulative[:, -1]
    into_end = jnp.exp(block_log[:, None] - cumulative)
    from_start = jnp.exp(cumulative)
    block_decay = jnp.exp(block_log)
    b_float = b_inputs.astype(jnp.float32)
    c_float = c_inputs.astype(jnp.float32)
    decayed_b = (into_end[:, :, None] * b_float[None]).astype(jnp.bfloat16)
    decayed_c = (from_start[:, :, None] * c_float[None]).astype(jnp.bfloat16)
    x_heads = token_values.reshape(length, heads_here, head_dim)
    dy_heads = grad_out.reshape(length, heads_here, head_dim)
    state_local = jnp.einsum(
        "htn,thp->nhp", decayed_b, x_heads, preferred_element_type=jnp.float32
    ).reshape(state_size, heads_here * head_dim)
    adjoint_local = jnp.einsum(
        "hsn,shp->nhp", decayed_c, dy_heads, preferred_element_type=jnp.float32
    ).reshape(state_size, heads_here * head_dim)
    decay_cols = jnp.repeat(block_decay, head_dim)[None, :]
    grad_values, grad_b, grad_c = exclusive_scans(
        count, groups, decay_cols, state_local, adjoint_local, token_values, grad_out,
        cumulative, into_end, from_start, b_inputs, c_inputs,
    )
    return grad_values, grad_b, grad_c


def solution(mesh):
    in_specs = (
        P("seq", "head"),
        P("seq", None),
        P("seq", None),
        P("head", "seq"),
        P("seq", "head"),
    )
    out_specs = (P("seq", "head"), P("seq", None), P("seq", None))
    body = functools.partial(shards, mesh.shape["seq"], mesh.shape["head"])
    return jax.shard_map(body, mesh=mesh, in_specs=in_specs, out_specs=out_specs, check_vma=False)
```

```python
import functools

import jax
import jax.numpy as jnp
from jax import lax
from jax.experimental import pallas as pl
from jax.experimental.pallas import tpu as pltpu
from jax.sharding import PartitionSpec as P

PRECISE = lax.Precision.HIGHEST
MESH = pl.DeviceIdType.MESH


def nt_dot(p, q):
    return lax.dot_general(p, q, (((1,), (1,)), ((), ())), preferred_element_type=jnp.float32)


def nt_dot_f32(p, q):
    ph = p.astype(jnp.bfloat16)
    pl_ = (p - ph.astype(jnp.float32)).astype(jnp.bfloat16)
    qh = q.astype(jnp.bfloat16)
    ql = (q - qh.astype(jnp.float32)).astype(jnp.bfloat16)
    return nt_dot(ph, qh) + (nt_dot(ph, ql) + nt_dot(pl_, qh))


def scan_kernel(rows_n, width, groups, x_ref, dy_ref, cr_ref,
                b_ref, c_ref, gv_ref, sum_ref, run_ref, dx_ref, xs_ref, ds_ref, recv1, rdec,
                win, out3, recv3, full, parts, gather1, gather2, send1, rsem1, send2, rsem2, send3, rsem3,
                local, dsend, drecv, hsend1, hrecv1, hsend2, hrecv2, sc_ref, pdec_ref,
                early, pack_ref, local_ref, cc_ref):
    me = lax.axis_index("seq")
    col = lax.axis_index("head")
    c = me % width
    y = me // width
    piece = recv1.shape[1] // 2
    spans = [1, 2, 3, 4]

    length = x_ref.shape[0]
    cc_ref[...] = cr_ref[...].T
    later = lax.broadcasted_iota(jnp.int32, (length, length), 1) >= lax.broadcasted_iota(
        jnp.int32, (length, length), 0)
    run_ref[...] = jnp.zeros(run_ref.shape, run_ref.dtype)

    def head(h):
        gaps = cr_ref[h:h + 1, :] - cc_ref[:, h:h + 1]

        dec = jnp.where(later, jnp.exp(jnp.where(later, gaps, 0.0)), 0.0)
        mix = (sc_ref[...] * dec).astype(jnp.bfloat16)
        lanes = slice(h * hd, (h + 1) * hd)
        dy_h = dy_ref[:, lanes]
        x_h = x_ref[:, lanes]
        xs_ref[:, lanes] = x_h.astype(jnp.float32) * cc_ref[:, nh + h:nh + h + 1]
        ds_ref[:, lanes] = dy_h.astype(jnp.float32) * cc_ref[:, 2 * nh + h:2 * nh + h + 1]
        dx_ref[:, lanes] = jnp.dot(mix, dy_h, preferred_element_type=jnp.float32)
        pairs = lax.dot_general(
            x_h, dy_h, (((1,), (1,)), ((), ())), preferred_element_type=jnp.float32)
        run_ref[...] += dec * pairs

    nh = cr_ref.shape[0] // 3
    heads_left = list(range(nh))
    hd = x_ref.shape[1] // nh
    for h in range(nh):
        pdec_ref[:, h * hd:(h + 1) * hd] = jnp.broadcast_to(
            jnp.exp(cc_ref[length - 1:length, h:h + 1]), (pdec_ref.shape[0], hd))
    b_all = b_ref[...].astype(jnp.float32)
    c_all = c_ref[...].astype(jnp.float32)
    for h in range(nh):
        lanes = slice(h * hd, (h + 1) * hd)
        decayed_b = (cc_ref[:, nh + h:nh + h + 1] * b_all).astype(jnp.bfloat16)
        decayed_c = (cc_ref[:, 2 * nh + h:2 * nh + h + 1] * c_all).astype(jnp.bfloat16)
        local_ref[0, :, lanes] = lax.dot_general(
            decayed_b, x_ref[:, lanes], (((0,), (0,)), ((), ())), preferred_element_type=jnp.float32)
        local_ref[1, :, lanes] = lax.dot_general(
            decayed_c, dy_ref[:, lanes], (((0,), (0,)), ((), ())), preferred_element_type=jnp.float32)
    span = pack_ref.shape[1] // 2
    for k in range(pack_ref.shape[0]):
        pack_ref[k, :span, :] = local_ref[0, k * span:(k + 1) * span, :].astype(pack_ref.dtype)
        pack_ref[k, span:, :] = local_ref[1, k * span:(k + 1) * span, :].astype(pack_ref.dtype)

    def heads(k):
        for _ in range(k):
            if heads_left:
                head(heads_left.pop(0))

    barrier = pltpu.get_barrier_semaphore()
    for off in range(1, width):
        peer = y * width + (c + off) % width
        pl.semaphore_signal(barrier, inc=1, device_id=(peer, col), device_id_type=MESH)
    for d in spans:
        @pl.when(y + d < rows_n)
        def _():
            pl.semaphore_signal(barrier, inc=1, device_id=(me + d * width, col), device_id_type=MESH)

        @pl.when(y - d >= 0)
        def _():
            pl.semaphore_signal(barrier, inc=1, device_id=(me - d * width, col), device_id_type=MESH)
    z = lax.axis_index("head")
    for off in range(1, groups):
        pl.semaphore_signal(
            barrier, inc=1, device_id=(me, (z + off) % groups), device_id_type=MESH)
    peers = width - 1 + groups - 1
    for d in spans:
        peers = peers + ((rows_n - 1 - y) // d + rows_n - 1) // rows_n + (y // d + rows_n - 1) // rows_n
    sc_ref[...] = nt_dot(b_ref[...], c_ref[...])
    heads(1)
    pl.semaphore_wait(barrier, peers)

    own = pltpu.make_async_copy(pack_ref.at[c], recv1.at[c], local.at[0])
    own.start()
    own_dec = pltpu.make_async_copy(pdec_ref, rdec.at[c], local.at[2])
    own_dec.start()
    sends = []
    for off in range(1, width):
        k = (c + off) % width
        cp = pltpu.make_async_remote_copy(
            src_ref=pack_ref.at[k], dst_ref=recv1.at[c], send_sem=send1.at[off],
            recv_sem=rsem1.at[off], device_id=(y * width + k, col), device_id_type=MESH)
        cp.start()
        sends.append(cp)
        cp = pltpu.make_async_remote_copy(
            src_ref=pdec_ref, dst_ref=rdec.at[c], send_sem=dsend.at[off],
            recv_sem=drecv.at[off], device_id=(y * width + k, col), device_id_type=MESH)
        cp.start()
        sends.append(cp)
    heads(3)
    for off in range(1, width):
        k = (c + width - off) % width
        pltpu.make_async_remote_copy(
            src_ref=pack_ref.at[k], dst_ref=recv1.at[k], send_sem=send1.at[off],
            recv_sem=rsem1.at[off], device_id=(y * width + k, col), device_id_type=MESH).wait_recv()
        pltpu.make_async_remote_copy(
            src_ref=pdec_ref, dst_ref=rdec.at[k], send_sem=dsend.at[off],
            recv_sem=drecv.at[off], device_id=(y * width + k, col), device_id_type=MESH).wait_recv()
    own.wait()
    own_dec.wait()
    for cp in sends:
        cp.wait_send()

    def decay(i):
        return rdec[i, 0:1, :]

    fwd_e, fwd_g = [None] * width, [None] * width
    e = jnp.zeros((piece, recv1.shape[2]), jnp.float32)
    g = jnp.ones((1, recv1.shape[2]), jnp.float32)
    for i in range(width):
        fwd_e[i], fwd_g[i] = e, g
        a = decay(i)
        e = a * e + recv1[i, :piece, :].astype(jnp.float32)
        g = g * a
    bwd_e, bwd_g = [None] * width, [None] * width
    f = jnp.zeros((piece, recv1.shape[2]), jnp.float32)
    h = jnp.ones((1, recv1.shape[2]), jnp.float32)
    for i in reversed(range(width)):
        bwd_e[i], bwd_g[i] = f, h
        a = decay(i)
        f = a * f + recv1[i, piece:2 * piece, :].astype(jnp.float32)
        h = h * a
    win[0, 0, :piece, :] = e
    win[0, 0, piece:, :] = jnp.broadcast_to(g, (win.shape[2] - piece, g.shape[1]))
    win[1, 0, :piece, :] = f
    win[1, 0, piece:, :] = jnp.broadcast_to(h, (win.shape[2] - piece, h.shape[1]))

    def combine(w_near, w_far):
        a = w_near[piece:, :]
        return w_near[:piece, :] + jnp.broadcast_to(a[:1], (piece, a.shape[1])) * w_far[:piece, :], a * w_far[piece:, :]

    def copy2(way, slot, src_slot, target, sem):
        return pltpu.make_async_remote_copy(
            src_ref=win.at[way, src_slot], dst_ref=win.at[way, slot], send_sem=send2.at[way, sem],
            recv_sem=rsem2.at[way, sem], device_id=(target, col), device_id_type=MESH)

    def exists(row):
        return jnp.logical_and(row >= 0, row < rows_n)

    near = [1, 2, 3]
    for way, sign in ((0, 1), (1, -1)):
        for k in near:
            @pl.when(exists(y + sign * k))
            def _():
                copy2(way, k, 0, me + sign * k * width, k - 1).start()
    heads(2)
    for way, sign in ((0, 1), (1, -1)):
        win[way, 4] = jnp.zeros(win.shape[2:], win.dtype)
        for k in near:
            @pl.when(exists(y - sign * k))
            def _():
                copy2(way, k, 0, me - sign * k * width, k - 1).wait_recv()
                s_new, a_new = combine(win[way, 4], win[way, k])
                if k == 1:
                    win[way, 4] = win[way, 1]
                else:
                    win[way, 4, :piece, :] = s_new
                    win[way, 4, piece:, :] = a_new
        s_inc, a_inc = combine(win[way, 0], win[way, 4])
        win[way, 5, :piece, :] = s_inc
        win[way, 5, piece:, :] = a_inc

        @pl.when(exists(y + sign * 4))
        def _():
            copy2(way, 6, 5, me + sign * 4 * width, 3).start()
    heads(len(heads_left))
    for way, sign in ((0, 1), (1, -1)):
        @pl.when(exists(y - sign * 4))
        def _():
            copy2(way, 6, 5, me - sign * 4 * width, 3).wait_recv()
            s_new, a_new = combine(win[way, 4], win[way, 6])
            win[way, 7, :piece, :] = s_new
            win[way, 7, piece:, :] = a_new

        @pl.when(jnp.logical_not(exists(y - sign * 4)))
        def _():
            win[way, 7] = win[way, 4]
    for way, sign in ((0, 1), (1, -1)):
        for k in near:
            @pl.when(exists(y + sign * k))
            def _():
                copy2(way, k, 0, me + sign * k * width, k - 1).wait_send()

        @pl.when(exists(y + sign * 4))
        def _():
            copy2(way, 6, 5, me + sign * 4 * width, 3).wait_send()
    entering = win[0, 7, :piece, :]
    leaving = win[1, 7, :piece, :]

    for i in range(width):
        out3[i, :piece, :] = (fwd_e[i] + fwd_g[i] * entering).astype(out3.dtype)
        out3[i, piece:, :] = (bwd_e[i] + bwd_g[i] * leaving).astype(out3.dtype)
    own = pltpu.make_async_copy(out3.at[c], recv3.at[c], local.at[1])
    own.start()
    sends = []
    for off in range(1, width):
        k = (c + off) % width
        cp = pltpu.make_async_remote_copy(
            src_ref=out3.at[k], dst_ref=recv3.at[c], send_sem=send3.at[off],
            recv_sem=rsem3.at[off], device_id=(y * width + k, col), device_id_type=MESH)
        cp.start()
        sends.append(cp)
    weighted = run_ref[...].astype(jnp.bfloat16)
    early[0] = jnp.dot(weighted, c_ref[...], preferred_element_type=jnp.float32)
    early[1] = lax.dot_general(
        weighted, b_ref[...], (((0,), (0,)), ((), ())), preferred_element_type=jnp.float32)
    for off in range(1, width):
        k = (c + width - off) % width
        pltpu.make_async_remote_copy(
            src_ref=out3.at[k], dst_ref=recv3.at[k], send_sem=send3.at[off],
            recv_sem=rsem3.at[off], device_id=(y * width + k, col), device_id_type=MESH).wait_recv()
    own.wait()
    for cp in sends:
        cp.wait_send()

    s = width * piece
    for k in range(width):
        full[0, k * piece:(k + 1) * piece, :] = recv3[k, :piece, :].astype(jnp.float32)
        full[1, k * piece:(k + 1) * piece, :] = recv3[k, piece:, :].astype(jnp.float32)
    part_b = early[0] + nt_dot_f32(xs_ref[...], full[1])
    part_c = early[1] + nt_dot_f32(ds_ref[...], full[0])
    n_rows = part_b.shape[0]
    parts[:n_rows, :] = part_b.astype(parts.dtype)
    parts[n_rows:, :] = part_c.astype(parts.dtype)
    rows = gather1.shape[1]

    def chunk(i):
        return parts.at[pl.ds(pl.multiple_of(i * rows, rows), rows)]

    sends = []
    for k in range(1, groups):
        peer = (z + k) % groups
        cp = pltpu.make_async_remote_copy(
            src_ref=chunk(peer), dst_ref=gather1.at[z], send_sem=hsend1.at[k],
            recv_sem=hrecv1.at[k], device_id=(me, peer), device_id_type=MESH)
        cp.start()
        sends.append(cp)
    adj = full[1]
    adj_hi = adj.astype(jnp.bfloat16)
    adj_lo = (adj - adj_hi.astype(jnp.float32)).astype(jnp.bfloat16)
    b_adj = jnp.dot(b_ref[...], adj_hi, preferred_element_type=jnp.float32) + jnp.dot(
        b_ref[...], adj_lo, preferred_element_type=jnp.float32)
    for h in range(nh):
        lanes = slice(h * hd, (h + 1) * hd)
        gv_ref[:, lanes] = (dx_ref[:, lanes] + cc_ref[:, nh + h:nh + h + 1] * b_adj[:, lanes]).astype(
            gv_ref.dtype)
    total = parts[pl.ds(pl.multiple_of(z * rows, rows), rows), :].astype(jnp.float32)
    for k in range(1, groups):
        source = (z + groups - k) % groups
        pltpu.make_async_remote_copy(
            src_ref=chunk(source), dst_ref=gather1.at[source], send_sem=hsend1.at[k],
            recv_sem=hrecv1.at[k], device_id=(me, source), device_id_type=MESH).wait_recv()
        total = total + gather1[source].astype(jnp.float32)
    for cp in sends:
        cp.wait_send()
    gather2[z] = total.astype(gather2.dtype)
    sends = []
    for k in range(1, groups):
        peer = (z + k) % groups
        cp = pltpu.make_async_remote_copy(
            src_ref=gather2.at[z], dst_ref=gather2.at[z], send_sem=hsend2.at[k],
            recv_sem=hrecv2.at[k], device_id=(me, peer), device_id_type=MESH)
        cp.start()
        sends.append(cp)
    for k in range(1, groups):
        source = (z + groups - k) % groups
        pltpu.make_async_remote_copy(
            src_ref=gather2.at[source], dst_ref=gather2.at[source], send_sem=hsend2.at[k],
            recv_sem=hrecv2.at[k], device_id=(me, source), device_id_type=MESH).wait_recv()
    for cp in sends:
        cp.wait_send()
    sum_ref[...] = gather2[...]


def exclusive_scans(count, groups, decay_cols, forward, backward, x, dy, cumulative,
                    into_end, from_start, b_inputs, c_inputs):
    s, w = forward.shape
    width = 8 if count % 8 == 0 else 1
    rows_n = count // width
    piece = s // width
    assert rows_n <= 8
    length = x.shape[0]
    chunk_rows = 2 * length // groups
    stacked = jnp.concatenate([cumulative, into_end, from_start], axis=0)
    grad_values, sums = pl.pallas_call(
        functools.partial(scan_kernel, rows_n, width, groups),
        out_shape=(
            jax.ShapeDtypeStruct(x.shape, jnp.bfloat16),
            jax.ShapeDtypeStruct((groups, chunk_rows, s), jnp.bfloat16),
        ),
        in_specs=[pl.BlockSpec(memory_space=pltpu.VMEM)] * 5,
        out_specs=(pl.BlockSpec(memory_space=pltpu.VMEM),) * 2,
        scratch_shapes=[
            pltpu.VMEM((length, length), jnp.float32),
            pltpu.VMEM(x.shape, jnp.float32),
            pltpu.VMEM(x.shape, jnp.float32),
            pltpu.VMEM(x.shape, jnp.float32),
            pltpu.VMEM((width, 2 * piece, w), jnp.bfloat16),
            pltpu.VMEM((width, 8, w), jnp.float32),
            pltpu.VMEM((2, 8, piece + 8, w), jnp.float32),
            pltpu.VMEM((width, 2 * piece, w), jnp.bfloat16),
            pltpu.VMEM((width, 2 * piece, w), jnp.bfloat16),
            pltpu.VMEM((2, s, w), jnp.float32),
            pltpu.VMEM((2 * length, s), jnp.bfloat16),
            pltpu.VMEM((groups, chunk_rows, s), jnp.bfloat16),
            pltpu.VMEM((groups, chunk_rows, s), jnp.bfloat16),
            pltpu.SemaphoreType.DMA((width,)),
            pltpu.SemaphoreType.DMA((width,)),
            pltpu.SemaphoreType.DMA((2, 4)),
            pltpu.SemaphoreType.DMA((2, 4)),
            pltpu.SemaphoreType.DMA((width,)),
            pltpu.SemaphoreType.DMA((width,)),
            pltpu.SemaphoreType.DMA((3,)),
            pltpu.SemaphoreType.DMA((width,)),
            pltpu.SemaphoreType.DMA((width,)),
            pltpu.SemaphoreType.DMA((groups,)),
            pltpu.SemaphoreType.DMA((groups,)),
            pltpu.SemaphoreType.DMA((groups,)),
            pltpu.SemaphoreType.DMA((groups,)),
            pltpu.VMEM((length, length), jnp.float32),
            pltpu.VMEM((8, w), jnp.float32),
            pltpu.VMEM((2, length, s), jnp.float32),
            pltpu.VMEM((width, 2 * piece, w), jnp.bfloat16),
            pltpu.VMEM((2, s, w), jnp.float32),
            pltpu.VMEM((length, 3 * cumulative.shape[0]), jnp.float32),
        ],
        compiler_params=pltpu.CompilerParams(collective_id=1, has_side_effects=True),
    )(x, dy, stacked, b_inputs, c_inputs)
    sums = sums.reshape(2 * length, s)
    return grad_values, sums[:length], sums[length:]


def shards(count, groups, token_values, b_inputs, c_inputs, log_decay, grad_out):
    length = token_values.shape[0]
    heads_here = log_decay.shape[0]
    head_dim = token_values.shape[1] // heads_here
    state_size = b_inputs.shape[1]
    positions = lax.iota(jnp.int32, length)
    upto = (positions[:, None] <= positions[None, :]).astype(jnp.float32)
    cumulative = jnp.dot(log_decay, upto, precision=PRECISE)
    block_log = cumulative[:, -1]
    into_end = jnp.exp(block_log[:, None] - cumulative)
    from_start = jnp.exp(cumulative)
    block_decay = jnp.exp(block_log)
    b_float = b_inputs.astype(jnp.float32)
    c_float = c_inputs.astype(jnp.float32)
    decayed_b = (into_end[:, :, None] * b_float[None]).astype(jnp.bfloat16)
    decayed_c = (from_start[:, :, None] * c_float[None]).astype(jnp.bfloat16)
    x_heads = token_values.reshape(length, heads_here, head_dim)
    dy_heads = grad_out.reshape(length, heads_here, head_dim)
    state_local = jnp.einsum(
        "htn,thp->nhp", decayed_b, x_heads, preferred_element_type=jnp.float32
    ).reshape(state_size, heads_here * head_dim)
    adjoint_local = jnp.einsum(
        "hsn,shp->nhp", decayed_c, dy_heads, preferred_element_type=jnp.float32
    ).reshape(state_size, heads_here * head_dim)
    decay_cols = jnp.repeat(block_decay, head_dim)[None, :]
    grad_values, grad_b, grad_c = exclusive_scans(
        count, groups, decay_cols, state_local, adjoint_local, token_values, grad_out,
        cumulative, into_end, from_start, b_inputs, c_inputs,
    )
    return grad_values, grad_b, grad_c


def solution(mesh):
    in_specs = (
        P("seq", "head"),
        P("seq", None),
        P("seq", None),
        P("head", "seq"),
        P("seq", "head"),
    )
    out_specs = (P("seq", "head"), P("seq", None), P("seq", None))
    body = functools.partial(shards, mesh.shape["seq"], mesh.shape["head"])
    return jax.shard_map(body, mesh=mesh, in_specs=in_specs, out_specs=out_specs, check_vma=False)
```

```python
import functools

import jax
import jax.numpy as jnp
from jax import lax
from jax.experimental import pallas as pl
from jax.experimental.pallas import tpu as pltpu
from jax.sharding import PartitionSpec as P

PRECISE = lax.Precision.HIGHEST
MESH = pl.DeviceIdType.MESH


def nt_dot(p, q):
    return lax.dot_general(p, q, (((1,), (1,)), ((), ())), preferred_element_type=jnp.float32)


def nt_dot_f32(p, q):
    ph = p.astype(jnp.bfloat16)
    pl_ = (p - ph.astype(jnp.float32)).astype(jnp.bfloat16)
    qh = q.astype(jnp.bfloat16)
    ql = (q - qh.astype(jnp.float32)).astype(jnp.bfloat16)
    return nt_dot(ph, qh) + (nt_dot(ph, ql) + nt_dot(pl_, qh))


def scan_kernel(rows_n, width, groups, x_ref, dy_ref, cr_ref,
                b_ref, c_ref, gv_ref, sum_ref, run_ref, dx_ref, xs_ref, ds_ref, recv1, rdec,
                win, out3, recv3, full, parts, gather1, gather2, send1, rsem1, send2, rsem2, send3, rsem3,
                local, dsend, drecv, hsend1, hrecv1, hsend2, hrecv2, sc_ref, pdec_ref,
                early, pack_ref, local_ref, cc_ref):
    me = lax.axis_index("seq")
    col = lax.axis_index("head")
    c = me % width
    y = me // width
    piece = recv1.shape[1] // 2
    spans = [1, 2, 3, 4]

    length = x_ref.shape[0]
    cc_ref[...] = cr_ref[...].T
    later = lax.broadcasted_iota(jnp.int32, (length, length), 1) >= lax.broadcasted_iota(
        jnp.int32, (length, length), 0)
    run_ref[...] = jnp.zeros(run_ref.shape, run_ref.dtype)

    def head(h):
        gaps = cr_ref[h:h + 1, :] - cc_ref[:, h:h + 1]

        dec = jnp.where(later, jnp.exp(jnp.where(later, gaps, 0.0)), 0.0)
        mix = (sc_ref[...] * dec).astype(jnp.bfloat16)
        lanes = slice(h * hd, (h + 1) * hd)
        dy_h = dy_ref[:, lanes]
        x_h = x_ref[:, lanes]
        xs_ref[:, lanes] = x_h.astype(jnp.float32) * cc_ref[:, nh + h:nh + h + 1]
        ds_ref[:, lanes] = dy_h.astype(jnp.float32) * cc_ref[:, 2 * nh + h:2 * nh + h + 1]
        dx_ref[:, lanes] = jnp.dot(mix, dy_h, preferred_element_type=jnp.float32)
        pairs = lax.dot_general(
            x_h, dy_h, (((1,), (1,)), ((), ())), preferred_element_type=jnp.float32)
        run_ref[...] += dec * pairs

    nh = cr_ref.shape[0] // 3
    heads_left = list(range(nh))
    hd = x_ref.shape[1] // nh
    for h in range(nh):
        pdec_ref[:, h * hd:(h + 1) * hd] = jnp.broadcast_to(
            jnp.exp(cc_ref[length - 1:length, h:h + 1]), (pdec_ref.shape[0], hd))
    b_all = b_ref[...].astype(jnp.float32)
    c_all = c_ref[...].astype(jnp.float32)
    for h in range(nh):
        lanes = slice(h * hd, (h + 1) * hd)
        decayed_b = (cc_ref[:, nh + h:nh + h + 1] * b_all).astype(jnp.bfloat16)
        decayed_c = (cc_ref[:, 2 * nh + h:2 * nh + h + 1] * c_all).astype(jnp.bfloat16)
        local_ref[0, :, lanes] = lax.dot_general(
            decayed_b, x_ref[:, lanes], (((0,), (0,)), ((), ())), preferred_element_type=jnp.float32)
        local_ref[1, :, lanes] = lax.dot_general(
            decayed_c, dy_ref[:, lanes], (((0,), (0,)), ((), ())), preferred_element_type=jnp.float32)
    span = pack_ref.shape[1] // 2
    for k in range(pack_ref.shape[0]):
        pack_ref[k, :span, :] = local_ref[0, k * span:(k + 1) * span, :].astype(pack_ref.dtype)
        pack_ref[k, span:, :] = local_ref[1, k * span:(k + 1) * span, :].astype(pack_ref.dtype)

    def heads(k):
        for _ in range(k):
            if heads_left:
                head(heads_left.pop(0))

    barrier = pltpu.get_barrier_semaphore()
    for off in range(1, width):
        peer = y * width + (c + off) % width
        pl.semaphore_signal(barrier, inc=1, device_id=(peer, col), device_id_type=MESH)
    for d in spans:
        @pl.when(y + d < rows_n)
        def _():
            pl.semaphore_signal(barrier, inc=1, device_id=(me + d * width, col), device_id_type=MESH)

        @pl.when(y - d >= 0)
        def _():
            pl.semaphore_signal(barrier, inc=1, device_id=(me - d * width, col), device_id_type=MESH)
    z = lax.axis_index("head")
    for off in range(1, groups):
        pl.semaphore_signal(
            barrier, inc=1, device_id=(me, (z + off) % groups), device_id_type=MESH)
    peers = width - 1 + groups - 1
    for d in spans:
        peers = peers + ((rows_n - 1 - y) // d + rows_n - 1) // rows_n + (y // d + rows_n - 1) // rows_n
    sc_ref[...] = nt_dot(b_ref[...], c_ref[...])
    heads(0)
    pl.semaphore_wait(barrier, peers)

    own = pltpu.make_async_copy(pack_ref.at[c], recv1.at[c], local.at[0])
    own.start()
    own_dec = pltpu.make_async_copy(pdec_ref, rdec.at[c], local.at[2])
    own_dec.start()
    sends = []
    for off in range(1, width):
        k = (c + off) % width
        cp = pltpu.make_async_remote_copy(
            src_ref=pack_ref.at[k], dst_ref=recv1.at[c], send_sem=send1.at[off],
            recv_sem=rsem1.at[off], device_id=(y * width + k, col), device_id_type=MESH)
        cp.start()
        sends.append(cp)
        cp = pltpu.make_async_remote_copy(
            src_ref=pdec_ref, dst_ref=rdec.at[c], send_sem=dsend.at[off],
            recv_sem=drecv.at[off], device_id=(y * width + k, col), device_id_type=MESH)
        cp.start()
        sends.append(cp)
    heads(3)
    for off in range(1, width):
        k = (c + width - off) % width
        pltpu.make_async_remote_copy(
            src_ref=pack_ref.at[k], dst_ref=recv1.at[k], send_sem=send1.at[off],
            recv_sem=rsem1.at[off], device_id=(y * width + k, col), device_id_type=MESH).wait_recv()
        pltpu.make_async_remote_copy(
            src_ref=pdec_ref, dst_ref=rdec.at[k], send_sem=dsend.at[off],
            recv_sem=drecv.at[off], device_id=(y * width + k, col), device_id_type=MESH).wait_recv()
    own.wait()
    own_dec.wait()
    for cp in sends:
        cp.wait_send()

    def decay(i):
        return rdec[i, 0:1, :]

    fwd_e, fwd_g = [None] * width, [None] * width
    e = jnp.zeros((piece, recv1.shape[2]), jnp.float32)
    g = jnp.ones((1, recv1.shape[2]), jnp.float32)
    for i in range(width):
        fwd_e[i], fwd_g[i] = e, g
        a = decay(i)
        e = a * e + recv1[i, :piece, :].astype(jnp.float32)
        g = g * a
    bwd_e, bwd_g = [None] * width, [None] * width
    f = jnp.zeros((piece, recv1.shape[2]), jnp.float32)
    h = jnp.ones((1, recv1.shape[2]), jnp.float32)
    for i in reversed(range(width)):
        bwd_e[i], bwd_g[i] = f, h
        a = decay(i)
        f = a * f + recv1[i, piece:2 * piece, :].astype(jnp.float32)
        h = h * a
    win[0, 0, :piece, :] = e
    win[0, 0, piece:, :] = jnp.broadcast_to(g, (win.shape[2] - piece, g.shape[1]))
    win[1, 0, :piece, :] = f
    win[1, 0, piece:, :] = jnp.broadcast_to(h, (win.shape[2] - piece, h.shape[1]))

    def combine(w_near, w_far):
        a = w_near[piece:, :]
        return w_near[:piece, :] + jnp.broadcast_to(a[:1], (piece, a.shape[1])) * w_far[:piece, :], a * w_far[piece:, :]

    def copy2(way, slot, src_slot, target, sem):
        return pltpu.make_async_remote_copy(
            src_ref=win.at[way, src_slot], dst_ref=win.at[way, slot], send_sem=send2.at[way, sem],
            recv_sem=rsem2.at[way, sem], device_id=(target, col), device_id_type=MESH)

    def exists(row):
        return jnp.logical_and(row >= 0, row < rows_n)

    near = [1, 2, 3]
    for way, sign in ((0, 1), (1, -1)):
        for k in near:
            @pl.when(exists(y + sign * k))
            def _():
                copy2(way, k, 0, me + sign * k * width, k - 1).start()
    heads(2)
    for way, sign in ((0, 1), (1, -1)):
        win[way, 4] = jnp.zeros(win.shape[2:], win.dtype)
        for k in near:
            @pl.when(exists(y - sign * k))
            def _():
                copy2(way, k, 0, me - sign * k * width, k - 1).wait_recv()
                s_new, a_new = combine(win[way, 4], win[way, k])
                if k == 1:
                    win[way, 4] = win[way, 1]
                else:
                    win[way, 4, :piece, :] = s_new
                    win[way, 4, piece:, :] = a_new
        s_inc, a_inc = combine(win[way, 0], win[way, 4])
        win[way, 5, :piece, :] = s_inc
        win[way, 5, piece:, :] = a_inc

        @pl.when(exists(y + sign * 4))
        def _():
            copy2(way, 6, 5, me + sign * 4 * width, 3).start()
    heads(len(heads_left))
    for way, sign in ((0, 1), (1, -1)):
        @pl.when(exists(y - sign * 4))
        def _():
            copy2(way, 6, 5, me - sign * 4 * width, 3).wait_recv()
            s_new, a_new = combine(win[way, 4], win[way, 6])
            win[way, 7, :piece, :] = s_new
            win[way, 7, piece:, :] = a_new

        @pl.when(jnp.logical_not(exists(y - sign * 4)))
        def _():
            win[way, 7] = win[way, 4]
    for way, sign in ((0, 1), (1, -1)):
        for k in near:
            @pl.when(exists(y + sign * k))
            def _():
                copy2(way, k, 0, me + sign * k * width, k - 1).wait_send()

        @pl.when(exists(y + sign * 4))
        def _():
            copy2(way, 6, 5, me + sign * 4 * width, 3).wait_send()
    entering = win[0, 7, :piece, :]
    leaving = win[1, 7, :piece, :]

    for i in range(width):
        out3[i, :piece, :] = (fwd_e[i] + fwd_g[i] * entering).astype(out3.dtype)
        out3[i, piece:, :] = (bwd_e[i] + bwd_g[i] * leaving).astype(out3.dtype)
    own = pltpu.make_async_copy(out3.at[c], recv3.at[c], local.at[1])
    own.start()
    sends = []
    for off in range(1, width):
        k = (c + off) % width
        cp = pltpu.make_async_remote_copy(
            src_ref=out3.at[k], dst_ref=recv3.at[c], send_sem=send3.at[off],
            recv_sem=rsem3.at[off], device_id=(y * width + k, col), device_id_type=MESH)
        cp.start()
        sends.append(cp)
    weighted = run_ref[...].astype(jnp.bfloat16)
    early[0] = jnp.dot(weighted, c_ref[...], preferred_element_type=jnp.float32)
    early[1] = lax.dot_general(
        weighted, b_ref[...], (((0,), (0,)), ((), ())), preferred_element_type=jnp.float32)
    for off in range(1, width):
        k = (c + width - off) % width
        pltpu.make_async_remote_copy(
            src_ref=out3.at[k], dst_ref=recv3.at[k], send_sem=send3.at[off],
            recv_sem=rsem3.at[off], device_id=(y * width + k, col), device_id_type=MESH).wait_recv()
    own.wait()
    for cp in sends:
        cp.wait_send()

    s = width * piece
    for k in range(width):
        full[0, k * piece:(k + 1) * piece, :] = recv3[k, :piece, :].astype(jnp.float32)
        full[1, k * piece:(k + 1) * piece, :] = recv3[k, piece:, :].astype(jnp.float32)
    part_b = early[0] + nt_dot_f32(xs_ref[...], full[1])
    part_c = early[1] + nt_dot_f32(ds_ref[...], full[0])
    n_rows = part_b.shape[0]
    parts[:n_rows, :] = part_b.astype(parts.dtype)
    parts[n_rows:, :] = part_c.astype(parts.dtype)
    rows = gather1.shape[1]

    def chunk(i):
        return parts.at[pl.ds(pl.multiple_of(i * rows, rows), rows)]

    sends = []
    for k in range(1, groups):
        peer = (z + k) % groups
        cp = pltpu.make_async_remote_copy(
            src_ref=chunk(peer), dst_ref=gather1.at[z], send_sem=hsend1.at[k],
            recv_sem=hrecv1.at[k], device_id=(me, peer), device_id_type=MESH)
        cp.start()
        sends.append(cp)
    adj = full[1]
    adj_hi = adj.astype(jnp.bfloat16)
    adj_lo = (adj - adj_hi.astype(jnp.float32)).astype(jnp.bfloat16)
    b_adj = jnp.dot(b_ref[...], adj_hi, preferred_element_type=jnp.float32) + jnp.dot(
        b_ref[...], adj_lo, preferred_element_type=jnp.float32)
    for h in range(nh):
        lanes = slice(h * hd, (h + 1) * hd)
        gv_ref[:, lanes] = (dx_ref[:, lanes] + cc_ref[:, nh + h:nh + h + 1] * b_adj[:, lanes]).astype(
            gv_ref.dtype)
    total = parts[pl.ds(pl.multiple_of(z * rows, rows), rows), :].astype(jnp.float32)
    for k in range(1, groups):
        source = (z + groups - k) % groups
        pltpu.make_async_remote_copy(
            src_ref=chunk(source), dst_ref=gather1.at[source], send_sem=hsend1.at[k],
            recv_sem=hrecv1.at[k], device_id=(me, source), device_id_type=MESH).wait_recv()
        total = total + gather1[source].astype(jnp.float32)
    for cp in sends:
        cp.wait_send()
    gather2[z] = total.astype(gather2.dtype)
    sends = []
    for k in range(1, groups):
        peer = (z + k) % groups
        cp = pltpu.make_async_remote_copy(
            src_ref=gather2.at[z], dst_ref=gather2.at[z], send_sem=hsend2.at[k],
            recv_sem=hrecv2.at[k], device_id=(me, peer), device_id_type=MESH)
        cp.start()
        sends.append(cp)
    for k in range(1, groups):
        source = (z + groups - k) % groups
        pltpu.make_async_remote_copy(
            src_ref=gather2.at[source], dst_ref=gather2.at[source], send_sem=hsend2.at[k],
            recv_sem=hrecv2.at[k], device_id=(me, source), device_id_type=MESH).wait_recv()
    for cp in sends:
        cp.wait_send()
    sum_ref[...] = gather2[...]


def exclusive_scans(count, groups, decay_cols, forward, backward, x, dy, cumulative,
                    into_end, from_start, b_inputs, c_inputs):
    s, w = forward.shape
    width = 8 if count % 8 == 0 else 1
    rows_n = count // width
    piece = s // width
    assert rows_n <= 8
    length = x.shape[0]
    chunk_rows = 2 * length // groups
    stacked = jnp.concatenate([cumulative, into_end, from_start], axis=0)
    grad_values, sums = pl.pallas_call(
        functools.partial(scan_kernel, rows_n, width, groups),
        out_shape=(
            jax.ShapeDtypeStruct(x.shape, jnp.bfloat16),
            jax.ShapeDtypeStruct((groups, chunk_rows, s), jnp.bfloat16),
        ),
        in_specs=[pl.BlockSpec(memory_space=pltpu.VMEM)] * 5,
        out_specs=(pl.BlockSpec(memory_space=pltpu.VMEM),) * 2,
        scratch_shapes=[
            pltpu.VMEM((length, length), jnp.float32),
            pltpu.VMEM(x.shape, jnp.float32),
            pltpu.VMEM(x.shape, jnp.float32),
            pltpu.VMEM(x.shape, jnp.float32),
            pltpu.VMEM((width, 2 * piece, w), jnp.bfloat16),
            pltpu.VMEM((width, 8, w), jnp.float32),
            pltpu.VMEM((2, 8, piece + 8, w), jnp.float32),
            pltpu.VMEM((width, 2 * piece, w), jnp.bfloat16),
            pltpu.VMEM((width, 2 * piece, w), jnp.bfloat16),
            pltpu.VMEM((2, s, w), jnp.float32),
            pltpu.VMEM((2 * length, s), jnp.bfloat16),
            pltpu.VMEM((groups, chunk_rows, s), jnp.bfloat16),
            pltpu.VMEM((groups, chunk_rows, s), jnp.bfloat16),
            pltpu.SemaphoreType.DMA((width,)),
            pltpu.SemaphoreType.DMA((width,)),
            pltpu.SemaphoreType.DMA((2, 4)),
            pltpu.SemaphoreType.DMA((2, 4)),
            pltpu.SemaphoreType.DMA((width,)),
            pltpu.SemaphoreType.DMA((width,)),
            pltpu.SemaphoreType.DMA((3,)),
            pltpu.SemaphoreType.DMA((width,)),
            pltpu.SemaphoreType.DMA((width,)),
            pltpu.SemaphoreType.DMA((groups,)),
            pltpu.SemaphoreType.DMA((groups,)),
            pltpu.SemaphoreType.DMA((groups,)),
            pltpu.SemaphoreType.DMA((groups,)),
            pltpu.VMEM((length, length), jnp.float32),
            pltpu.VMEM((8, w), jnp.float32),
            pltpu.VMEM((2, length, s), jnp.float32),
            pltpu.VMEM((width, 2 * piece, w), jnp.bfloat16),
            pltpu.VMEM((2, s, w), jnp.float32),
            pltpu.VMEM((length, 3 * cumulative.shape[0]), jnp.float32),
        ],
        compiler_params=pltpu.CompilerParams(collective_id=1, has_side_effects=True),
    )(x, dy, stacked, b_inputs, c_inputs)
    sums = sums.reshape(2 * length, s)
    return grad_values, sums[:length], sums[length:]


def shards(count, groups, token_values, b_inputs, c_inputs, log_decay, grad_out):
    length = token_values.shape[0]
    heads_here = log_decay.shape[0]
    head_dim = token_values.shape[1] // heads_here
    state_size = b_inputs.shape[1]
    positions = lax.iota(jnp.int32, length)
    upto = (positions[:, None] <= positions[None, :]).astype(jnp.float32)
    cumulative = jnp.dot(log_decay, upto, precision=PRECISE)
    block_log = cumulative[:, -1]
    into_end = jnp.exp(block_log[:, None] - cumulative)
    from_start = jnp.exp(cumulative)
    block_decay = jnp.exp(block_log)
    b_float = b_inputs.astype(jnp.float32)
    c_float = c_inputs.astype(jnp.float32)
    decayed_b = (into_end[:, :, None] * b_float[None]).astype(jnp.bfloat16)
    decayed_c = (from_start[:, :, None] * c_float[None]).astype(jnp.bfloat16)
    x_heads = token_values.reshape(length, heads_here, head_dim)
    dy_heads = grad_out.reshape(length, heads_here, head_dim)
    state_local = jnp.einsum(
        "htn,thp->nhp", decayed_b, x_heads, preferred_element_type=jnp.float32
    ).reshape(state_size, heads_here * head_dim)
    adjoint_local = jnp.einsum(
        "hsn,shp->nhp", decayed_c, dy_heads, preferred_element_type=jnp.float32
    ).reshape(state_size, heads_here * head_dim)
    decay_cols = jnp.repeat(block_decay, head_dim)[None, :]
    grad_values, grad_b, grad_c = exclusive_scans(
        count, groups, decay_cols, state_local, adjoint_local, token_values, grad_out,
        cumulative, into_end, from_start, b_inputs, c_inputs,
    )
    return grad_values, grad_b, grad_c


def solution(mesh):
    in_specs = (
        P("seq", "head"),
        P("seq", None),
        P("seq", None),
        P("head", "seq"),
        P("seq", "head"),
    )
    out_specs = (P("seq", "head"), P("seq", None), P("seq", None))
    body = functools.partial(shards, mesh.shape["seq"], mesh.shape["head"])
    return jax.shard_map(body, mesh=mesh, in_specs=in_specs, out_specs=out_specs, check_vma=False)
```

```python
import functools

import jax
import jax.numpy as jnp
from jax import lax
from jax.experimental import pallas as pl
from jax.experimental.pallas import tpu as pltpu
from jax.sharding import PartitionSpec as P

PRECISE = lax.Precision.HIGHEST
MESH = pl.DeviceIdType.MESH


def nt_dot(p, q):
    return lax.dot_general(p, q, (((1,), (1,)), ((), ())), preferred_element_type=jnp.float32)


def nt_dot_f32(p, q):
    ph = p.astype(jnp.bfloat16)
    pl_ = (p - ph.astype(jnp.float32)).astype(jnp.bfloat16)
    qh = q.astype(jnp.bfloat16)
    ql = (q - qh.astype(jnp.float32)).astype(jnp.bfloat16)
    return nt_dot(ph, qh) + (nt_dot(ph, ql) + nt_dot(pl_, qh))


def scan_kernel(rows_n, width, groups, x_ref, dy_ref, cr_ref,
                b_ref, c_ref, gv_ref, sum_ref, run_ref, dx_ref, xs_ref, ds_ref, recv1, rdec,
                win, out3, recv3, full, parts, gather1, gather2, send1, rsem1, send2, rsem2, send3, rsem3,
                local, dsend, drecv, hsend1, hrecv1, hsend2, hrecv2, sc_ref, pdec_ref,
                early, pack_ref, local_ref, cc_ref):
    me = lax.axis_index("seq")
    col = lax.axis_index("head")
    c = me % width
    y = me // width
    piece = recv1.shape[1] // 2
    spans = [1, 2, 3, 4]

    length = x_ref.shape[0]
    cc_ref[...] = cr_ref[...].T
    later = lax.broadcasted_iota(jnp.int32, (length, length), 1) >= lax.broadcasted_iota(
        jnp.int32, (length, length), 0)
    run_ref[...] = jnp.zeros(run_ref.shape, run_ref.dtype)

    def head(h):
        gaps = cr_ref[h:h + 1, :] - cc_ref[:, h:h + 1]

        dec = jnp.where(later, jnp.exp(jnp.where(later, gaps, 0.0)), 0.0)
        mix = (sc_ref[...] * dec).astype(jnp.bfloat16)
        lanes = slice(h * hd, (h + 1) * hd)
        dy_h = dy_ref[:, lanes]
        x_h = x_ref[:, lanes]
        xs_ref[:, lanes] = x_h.astype(jnp.float32) * cc_ref[:, nh + h:nh + h + 1]
        ds_ref[:, lanes] = dy_h.astype(jnp.float32) * cc_ref[:, 2 * nh + h:2 * nh + h + 1]
        dx_ref[:, lanes] = jnp.dot(mix, dy_h, preferred_element_type=jnp.float32)
        pairs = lax.dot_general(
            x_h, dy_h, (((1,), (1,)), ((), ())), preferred_element_type=jnp.float32)
        run_ref[...] += dec * pairs

    nh = cr_ref.shape[0] // 3
    heads_left = list(range(nh))
    hd = x_ref.shape[1] // nh
    for h in range(nh):
        pdec_ref[:, h * hd:(h + 1) * hd] = jnp.broadcast_to(
            jnp.exp(cc_ref[length - 1:length, h:h + 1]), (pdec_ref.shape[0], hd))
    b_all = b_ref[...].astype(jnp.float32)
    c_all = c_ref[...].astype(jnp.float32)
    for h in range(nh):
        lanes = slice(h * hd, (h + 1) * hd)
        decayed_b = (cc_ref[:, nh + h:nh + h + 1] * b_all).astype(jnp.bfloat16)
        decayed_c = (cc_ref[:, 2 * nh + h:2 * nh + h + 1] * c_all).astype(jnp.bfloat16)
        local_ref[0, :, lanes] = lax.dot_general(
            decayed_b, x_ref[:, lanes], (((0,), (0,)), ((), ())), preferred_element_type=jnp.float32)
        local_ref[1, :, lanes] = lax.dot_general(
            decayed_c, dy_ref[:, lanes], (((0,), (0,)), ((), ())), preferred_element_type=jnp.float32)
    span = pack_ref.shape[1] // 2
    for k in range(pack_ref.shape[0]):
        pack_ref[k, :span, :] = local_ref[0, k * span:(k + 1) * span, :].astype(pack_ref.dtype)
        pack_ref[k, span:, :] = local_ref[1, k * span:(k + 1) * span, :].astype(pack_ref.dtype)

    def heads(k):
        for _ in range(k):
            if heads_left:
                head(heads_left.pop(0))

    barrier = pltpu.get_barrier_semaphore()
    for off in range(1, width):
        peer = y * width + (c + off) % width
        pl.semaphore_signal(barrier, inc=1, device_id=(peer, col), device_id_type=MESH)
    for d in spans:
        @pl.when(y + d < rows_n)
        def _():
            pl.semaphore_signal(barrier, inc=1, device_id=(me + d * width, col), device_id_type=MESH)

        @pl.when(y - d >= 0)
        def _():
            pl.semaphore_signal(barrier, inc=1, device_id=(me - d * width, col), device_id_type=MESH)
    z = lax.axis_index("head")
    for off in range(1, groups):
        pl.semaphore_signal(
            barrier, inc=1, device_id=(me, (z + off) % groups), device_id_type=MESH)
    peers = width - 1 + groups - 1
    for d in spans:
        peers = peers + ((rows_n - 1 - y) // d + rows_n - 1) // rows_n + (y // d + rows_n - 1) // rows_n
    sc_ref[...] = nt_dot(b_ref[...], c_ref[...])
    heads(1)
    pl.semaphore_wait(barrier, peers)

    own = pltpu.make_async_copy(pack_ref.at[c], recv1.at[c], local.at[0])
    own.start()
    own_dec = pltpu.make_async_copy(pdec_ref, rdec.at[c], local.at[2])
    own_dec.start()
    sends = []
    for off in range(1, width):
        k = (c + off) % width
        cp = pltpu.make_async_remote_copy(
            src_ref=pack_ref.at[k], dst_ref=recv1.at[c], send_sem=send1.at[off],
            recv_sem=rsem1.at[off], device_id=(y * width + k, col), device_id_type=MESH)
        cp.start()
        sends.append(cp)
        cp = pltpu.make_async_remote_copy(
            src_ref=pdec_ref, dst_ref=rdec.at[c], send_sem=dsend.at[off],
            recv_sem=drecv.at[off], device_id=(y * width + k, col), device_id_type=MESH)
        cp.start()
        sends.append(cp)
    heads(4)
    for off in range(1, width):
        k = (c + width - off) % width
        pltpu.make_async_remote_copy(
            src_ref=pack_ref.at[k], dst_ref=recv1.at[k], send_sem=send1.at[off],
            recv_sem=rsem1.at[off], device_id=(y * width + k, col), device_id_type=MESH).wait_recv()
        pltpu.make_async_remote_copy(
            src_ref=pdec_ref, dst_ref=rdec.at[k], send_sem=dsend.at[off],
            recv_sem=drecv.at[off], device_id=(y * width + k, col), device_id_type=MESH).wait_recv()
    own.wait()
    own_dec.wait()
    for cp in sends:
        cp.wait_send()

    def decay(i):
        return rdec[i, 0:1, :]

    fwd_e, fwd_g = [None] * width, [None] * width
    e = jnp.zeros((piece, recv1.shape[2]), jnp.float32)
    g = jnp.ones((1, recv1.shape[2]), jnp.float32)
    for i in range(width):
        fwd_e[i], fwd_g[i] = e, g
        a = decay(i)
        e = a * e + recv1[i, :piece, :].astype(jnp.float32)
        g = g * a
    bwd_e, bwd_g = [None] * width, [None] * width
    f = jnp.zeros((piece, recv1.shape[2]), jnp.float32)
    h = jnp.ones((1, recv1.shape[2]), jnp.float32)
    for i in reversed(range(width)):
        bwd_e[i], bwd_g[i] = f, h
        a = decay(i)
        f = a * f + recv1[i, piece:2 * piece, :].astype(jnp.float32)
        h = h * a
    win[0, 0, :piece, :] = e
    win[0, 0, piece:, :] = jnp.broadcast_to(g, (win.shape[2] - piece, g.shape[1]))
    win[1, 0, :piece, :] = f
    win[1, 0, piece:, :] = jnp.broadcast_to(h, (win.shape[2] - piece, h.shape[1]))

    def combine(w_near, w_far):
        a = w_near[piece:, :]
        return w_near[:piece, :] + jnp.broadcast_to(a[:1], (piece, a.shape[1])) * w_far[:piece, :], a * w_far[piece:, :]

    def copy2(way, slot, src_slot, target, sem):
        return pltpu.make_async_remote_copy(
            src_ref=win.at[way, src_slot], dst_ref=win.at[way, slot], send_sem=send2.at[way, sem],
            recv_sem=rsem2.at[way, sem], device_id=(target, col), device_id_type=MESH)

    def exists(row):
        return jnp.logical_and(row >= 0, row < rows_n)

    near = [1, 2, 3]
    for way, sign in ((0, 1), (1, -1)):
        for k in near:
            @pl.when(exists(y + sign * k))
            def _():
                copy2(way, k, 0, me + sign * k * width, k - 1).start()
    heads(2)
    for way, sign in ((0, 1), (1, -1)):
        win[way, 4] = jnp.zeros(win.shape[2:], win.dtype)
        for k in near:
            @pl.when(exists(y - sign * k))
            def _():
                copy2(way, k, 0, me - sign * k * width, k - 1).wait_recv()
                s_new, a_new = combine(win[way, 4], win[way, k])
                if k == 1:
                    win[way, 4] = win[way, 1]
                else:
                    win[way, 4, :piece, :] = s_new
                    win[way, 4, piece:, :] = a_new
        s_inc, a_inc = combine(win[way, 0], win[way, 4])
        win[way, 5, :piece, :] = s_inc
        win[way, 5, piece:, :] = a_inc

        @pl.when(exists(y + sign * 4))
        def _():
            copy2(way, 6, 5, me + sign * 4 * width, 3).start()
    heads(len(heads_left))
    for way, sign in ((0, 1), (1, -1)):
        @pl.when(exists(y - sign * 4))
        def _():
            copy2(way, 6, 5, me - sign * 4 * width, 3).wait_recv()
            s_new, a_new = combine(win[way, 4], win[way, 6])
            win[way, 7, :piece, :] = s_new
            win[way, 7, piece:, :] = a_new

        @pl.when(jnp.logical_not(exists(y - sign * 4)))
        def _():
            win[way, 7] = win[way, 4]
    for way, sign in ((0, 1), (1, -1)):
        for k in near:
            @pl.when(exists(y + sign * k))
            def _():
                copy2(way, k, 0, me + sign * k * width, k - 1).wait_send()

        @pl.when(exists(y + sign * 4))
        def _():
            copy2(way, 6, 5, me + sign * 4 * width, 3).wait_send()
    entering = win[0, 7, :piece, :]
    leaving = win[1, 7, :piece, :]

    for i in range(width):
        out3[i, :piece, :] = (fwd_e[i] + fwd_g[i] * entering).astype(out3.dtype)
        out3[i, piece:, :] = (bwd_e[i] + bwd_g[i] * leaving).astype(out3.dtype)
    own = pltpu.make_async_copy(out3.at[c], recv3.at[c], local.at[1])
    own.start()
    sends = []
    for off in range(1, width):
        k = (c + off) % width
        cp = pltpu.make_async_remote_copy(
            src_ref=out3.at[k], dst_ref=recv3.at[c], send_sem=send3.at[off],
            recv_sem=rsem3.at[off], device_id=(y * width + k, col), device_id_type=MESH)
        cp.start()
        sends.append(cp)
    weighted = run_ref[...].astype(jnp.bfloat16)
    early[0] = jnp.dot(weighted, c_ref[...], preferred_element_type=jnp.float32)
    early[1] = lax.dot_general(
        weighted, b_ref[...], (((0,), (0,)), ((), ())), preferred_element_type=jnp.float32)
    for off in range(1, width):
        k = (c + width - off) % width
        pltpu.make_async_remote_copy(
            src_ref=out3.at[k], dst_ref=recv3.at[k], send_sem=send3.at[off],
            recv_sem=rsem3.at[off], device_id=(y * width + k, col), device_id_type=MESH).wait_recv()
    own.wait()
    for cp in sends:
        cp.wait_send()

    s = width * piece
    for k in range(width):
        full[0, k * piece:(k + 1) * piece, :] = recv3[k, :piece, :].astype(jnp.float32)
        full[1, k * piece:(k + 1) * piece, :] = recv3[k, piece:, :].astype(jnp.float32)
    part_b = early[0] + nt_dot_f32(xs_ref[...], full[1])
    part_c = early[1] + nt_dot_f32(ds_ref[...], full[0])
    n_rows = part_b.shape[0]
    parts[:n_rows, :] = part_b.astype(parts.dtype)
    parts[n_rows:, :] = part_c.astype(parts.dtype)
    rows = gather1.shape[1]

    def chunk(i):
        return parts.at[pl.ds(pl.multiple_of(i * rows, rows), rows)]

    sends = []
    for k in range(1, groups):
        peer = (z + k) % groups
        cp = pltpu.make_async_remote_copy(
            src_ref=chunk(peer), dst_ref=gather1.at[z], send_sem=hsend1.at[k],
            recv_sem=hrecv1.at[k], device_id=(me, peer), device_id_type=MESH)
        cp.start()
        sends.append(cp)
    adj = full[1]
    adj_hi = adj.astype(jnp.bfloat16)
    adj_lo = (adj - adj_hi.astype(jnp.float32)).astype(jnp.bfloat16)
    b_adj = jnp.dot(b_ref[...], adj_hi, preferred_element_type=jnp.float32) + jnp.dot(
        b_ref[...], adj_lo, preferred_element_type=jnp.float32)
    for h in range(nh):
        lanes = slice(h * hd, (h + 1) * hd)
        gv_ref[:, lanes] = (dx_ref[:, lanes] + cc_ref[:, nh + h:nh + h + 1] * b_adj[:, lanes]).astype(
            gv_ref.dtype)
    total = parts[pl.ds(pl.multiple_of(z * rows, rows), rows), :].astype(jnp.float32)
    for k in range(1, groups):
        source = (z + groups - k) % groups
        pltpu.make_async_remote_copy(
            src_ref=chunk(source), dst_ref=gather1.at[source], send_sem=hsend1.at[k],
            recv_sem=hrecv1.at[k], device_id=(me, source), device_id_type=MESH).wait_recv()
        total = total + gather1[source].astype(jnp.float32)
    for cp in sends:
        cp.wait_send()
    gather2[z] = total.astype(gather2.dtype)
    sends = []
    for k in range(1, groups):
        peer = (z + k) % groups
        cp = pltpu.make_async_remote_copy(
            src_ref=gather2.at[z], dst_ref=gather2.at[z], send_sem=hsend2.at[k],
            recv_sem=hrecv2.at[k], device_id=(me, peer), device_id_type=MESH)
        cp.start()
        sends.append(cp)
    for k in range(1, groups):
        source = (z + groups - k) % groups
        pltpu.make_async_remote_copy(
            src_ref=gather2.at[source], dst_ref=gather2.at[source], send_sem=hsend2.at[k],
            recv_sem=hrecv2.at[k], device_id=(me, source), device_id_type=MESH).wait_recv()
    for cp in sends:
        cp.wait_send()
    sum_ref[...] = gather2[...]


def exclusive_scans(count, groups, decay_cols, forward, backward, x, dy, cumulative,
                    into_end, from_start, b_inputs, c_inputs):
    s, w = forward.shape
    width = 8 if count % 8 == 0 else 1
    rows_n = count // width
    piece = s // width
    assert rows_n <= 8
    length = x.shape[0]
    chunk_rows = 2 * length // groups
    stacked = jnp.concatenate([cumulative, into_end, from_start], axis=0)
    grad_values, sums = pl.pallas_call(
        functools.partial(scan_kernel, rows_n, width, groups),
        out_shape=(
            jax.ShapeDtypeStruct(x.shape, jnp.bfloat16),
            jax.ShapeDtypeStruct((groups, chunk_rows, s), jnp.bfloat16),
        ),
        in_specs=[pl.BlockSpec(memory_space=pltpu.VMEM)] * 5,
        out_specs=(pl.BlockSpec(memory_space=pltpu.VMEM),) * 2,
        scratch_shapes=[
            pltpu.VMEM((length, length), jnp.float32),
            pltpu.VMEM(x.shape, jnp.float32),
            pltpu.VMEM(x.shape, jnp.float32),
            pltpu.VMEM(x.shape, jnp.float32),
            pltpu.VMEM((width, 2 * piece, w), jnp.bfloat16),
            pltpu.VMEM((width, 8, w), jnp.float32),
            pltpu.VMEM((2, 8, piece + 8, w), jnp.float32),
            pltpu.VMEM((width, 2 * piece, w), jnp.bfloat16),
            pltpu.VMEM((width, 2 * piece, w), jnp.bfloat16),
            pltpu.VMEM((2, s, w), jnp.float32),
            pltpu.VMEM((2 * length, s), jnp.bfloat16),
            pltpu.VMEM((groups, chunk_rows, s), jnp.bfloat16),
            pltpu.VMEM((groups, chunk_rows, s), jnp.bfloat16),
            pltpu.SemaphoreType.DMA((width,)),
            pltpu.SemaphoreType.DMA((width,)),
            pltpu.SemaphoreType.DMA((2, 4)),
            pltpu.SemaphoreType.DMA((2, 4)),
            pltpu.SemaphoreType.DMA((width,)),
            pltpu.SemaphoreType.DMA((width,)),
            pltpu.SemaphoreType.DMA((3,)),
            pltpu.SemaphoreType.DMA((width,)),
            pltpu.SemaphoreType.DMA((width,)),
            pltpu.SemaphoreType.DMA((groups,)),
            pltpu.SemaphoreType.DMA((groups,)),
            pltpu.SemaphoreType.DMA((groups,)),
            pltpu.SemaphoreType.DMA((groups,)),
            pltpu.VMEM((length, length), jnp.float32),
            pltpu.VMEM((8, w), jnp.float32),
            pltpu.VMEM((2, length, s), jnp.float32),
            pltpu.VMEM((width, 2 * piece, w), jnp.bfloat16),
            pltpu.VMEM((2, s, w), jnp.float32),
            pltpu.VMEM((length, 3 * cumulative.shape[0]), jnp.float32),
        ],
        compiler_params=pltpu.CompilerParams(collective_id=1, has_side_effects=True),
    )(x, dy, stacked, b_inputs, c_inputs)
    sums = sums.reshape(2 * length, s)
    return grad_values, sums[:length], sums[length:]


def shards(count, groups, token_values, b_inputs, c_inputs, log_decay, grad_out):
    length = token_values.shape[0]
    heads_here = log_decay.shape[0]
    head_dim = token_values.shape[1] // heads_here
    state_size = b_inputs.shape[1]
    positions = lax.iota(jnp.int32, length)
    upto = (positions[:, None] <= positions[None, :]).astype(jnp.float32)
    cumulative = jnp.dot(log_decay, upto, precision=PRECISE)
    block_log = cumulative[:, -1]
    into_end = jnp.exp(block_log[:, None] - cumulative)
    from_start = jnp.exp(cumulative)
    block_decay = jnp.exp(block_log)
    b_float = b_inputs.astype(jnp.float32)
    c_float = c_inputs.astype(jnp.float32)
    decayed_b = (into_end[:, :, None] * b_float[None]).astype(jnp.bfloat16)
    decayed_c = (from_start[:, :, None] * c_float[None]).astype(jnp.bfloat16)
    x_heads = token_values.reshape(length, heads_here, head_dim)
    dy_heads = grad_out.reshape(length, heads_here, head_dim)
    state_local = jnp.einsum(
        "htn,thp->nhp", decayed_b, x_heads, preferred_element_type=jnp.float32
    ).reshape(state_size, heads_here * head_dim)
    adjoint_local = jnp.einsum(
        "hsn,shp->nhp", decayed_c, dy_heads, preferred_element_type=jnp.float32
    ).reshape(state_size, heads_here * head_dim)
    decay_cols = jnp.repeat(block_decay, head_dim)[None, :]
    grad_values, grad_b, grad_c = exclusive_scans(
        count, groups, decay_cols, state_local, adjoint_local, token_values, grad_out,
        cumulative, into_end, from_start, b_inputs, c_inputs,
    )
    return grad_values, grad_b, grad_c


def solution(mesh):
    in_specs = (
        P("seq", "head"),
        P("seq", None),
        P("seq", None),
        P("head", "seq"),
        P("seq", "head"),
    )
    out_specs = (P("seq", "head"), P("seq", None), P("seq", None))
    body = functools.partial(shards, mesh.shape["seq"], mesh.shape["head"])
    return jax.shard_map(body, mesh=mesh, in_specs=in_specs, out_specs=out_specs, check_vma=False)
```
